32 devices in a mesh: shard: 2 (over y), tensor: 4 (over z), section: 4 (over x, core).
Axes of the slice: x: 2, y: 2, z: 4, core: 2. Of those that a mesh axis runs over, the one named last changes fastest.
Arguments:
- xin: bfloat16 [4, 16384, 768], P(None, ('shard', 'tensor', 'section')), may hold values from -6 to 6
- dout: bfloat16 [4, 16384, 768], P(None, ('shard', 'tensor', 'section')), may hold values from -6 to 6
- weights: bfloat16 [4, 768, 768], P(None, ('tensor', 'section')), may hold values from -0.21875 to 0.21875
- slot_block: int32 [8], replicated, may hold values from -1 to 3, as said below
- left_stat: float32 [8, 768, 768], P('shard', ('tensor', 'section')), may hold values from -1 to 10, as said below
- right_stat: float32 [8, 768, 768], P('shard', ('tensor', 'section')), may hold values from -1 to 10, as said below
- left_root: float32 [8, 768, 768], P('shard', ('tensor', 'section')), may hold values from -1 to 10, as said below
- right_root: float32 [8, 768, 768], P('shard', ('tensor', 'section')), may hold values from -1 to 10, as said below
- first_moment: float32 [8, 768, 768], P('shard', ('tensor', 'section')), may hold values from -0.3 to 0.3
- second_moment: float32 [8, 768, 768], P('shard', ('tensor', 'section')), may hold values from 0.001 to 0.01
Outputs:
- new_weights: bfloat16 [4, 768, 768], P(None, ('tensor', 'section'))
- new_left: float32 [8, 768, 768], P('shard', ('tensor', 'section'))
- new_right: float32 [8, 768, 768], P('shard', ('tensor', 'section'))
- new_first: float32 [8, 768, 768], P('shard', ('tensor', 'section'))
- new_second: float32 [8, 768, 768], P('shard', ('tensor', 'section'))
The draws below stay inside these ranges and needn't reach their ends.
Inputs may be any that keep to these rules, and one draw needn't show every extreme that they name: `slot_block`: every block 0 to 3 stands in exactly one slot; slots 4 s to 4 s + 3 belong to shard index s; some shard index holds two blocks and none holds more; the other slots hold -1. `left_stat`: each slot is a symmetric positive definite matrix. `right_stat`: each slot is a symmetric positive definite matrix. `left_root`: each slot is a symmetric positive definite matrix. `right_root`: each slot is a symmetric positive definite matrix.
All inputs are finite; a program needn't handle non-finite values.
Results may differ from the reference program's by a relative error of at most 0.00045.
Values may be sent and summed in bfloat16 or wider, within the bound.
No kernel may reach another device: no remote copies, remote signals or barrier semaphores. Data moves between devices by JAX's collectives and lax.ppermute only.
A program may use at most 128 MiB of HBM per device.

```python
import math
import jax
import jax.numpy as jnp
from jax import lax

BLOCK = 768
NB = 4
SLOTS = 4
TOKENS = 16384
SLOT_ALL = 8
N_SHARD = 2


def definite(key, upper):
    noise_key, diag_key = jax.random.split(key)
    noise = jax.random.normal(noise_key, (SLOT_ALL, BLOCK, BLOCK), jnp.float32)
    diag = jnp.exp(jax.random.uniform(diag_key, (SLOT_ALL, 1, BLOCK), jnp.float32, 0.0, math.log(upper)))
    sym = (noise + jnp.swapaxes(noise, 1, 2)) * (0.28 / math.sqrt(BLOCK))
    rows = lax.broadcasted_iota(jnp.int32, (1, BLOCK, BLOCK), 1)
    cols = lax.broadcasted_iota(jnp.int32, (1, BLOCK, BLOCK), 2)
    return sym + jnp.where(rows == cols, diag, 0.0)


def draw_left_stat(key, part):
    return definite(jax.random.fold_in(key, 11), 3.0)


def draw_right_stat(key, part):
    return definite(jax.random.fold_in(key, 12), 3.0)


def draw_left_root(key, part):
    return definite(jax.random.fold_in(key, 13), 3.0)


def draw_right_root(key, part):
    return definite(jax.random.fold_in(key, 14), 3.0)


def distinct_order(key, count):
    scores = jax.random.randint(key, (count,), 0, 1 << 20, dtype=jnp.int32) * count + jnp.arange(count, dtype=jnp.int32)
    return jnp.argsort(scores, stable=True).astype(jnp.int32)


def draw_slot_block(key, part):
    base = jax.random.fold_in(key, 15)
    block_order = distinct_order(jax.random.fold_in(base, 1), NB)
    shard_order = distinct_order(jax.random.fold_in(base, 2), N_SHARD)
    table = jnp.full((SLOT_ALL,), -1, jnp.int32)
    for position in range(NB):
        if position < 2:
            owner = shard_order[0]
            place = distinct_order(jax.random.fold_in(base, 100), SLOTS)[position]
        elif N_SHARD >= NB - 1:
            owner = shard_order[position - 1]
            place = jax.random.randint(jax.random.fold_in(base, 200 + position), (), 0, SLOTS, dtype=jnp.int32)
        else:
            owner = shard_order[position // 2]
            place = distinct_order(jax.random.fold_in(base, 100 + position // 2), SLOTS)[position % 2]
        table = table.at[owner * SLOTS + place].set(block_order[position])
    return table


def spiked(entries, stream_key, source, target, blocks, factor):
    def block_of(dim):
        return (jnp.arange(entries.shape[dim]) // (entries.shape[dim] // blocks)).reshape((-1,) + (1,) * (entries.ndim - 1 - dim))

    near = jax.random.permutation(stream_key, blocks)[block_of(target)]
    other_side = (block_of(target) + blocks // 2) % blocks
    return jnp.where((block_of(source) == near) | (block_of(source) == other_side), factor * entries, entries)


def steps_of(stream_key, extent, cuts, smallest, high):
    loudness = 1.0
    for axis_at, shards_of in cuts:
        heights = jax.random.uniform(jax.random.fold_in(jax.random.fold_in(stream_key, 6), axis_at), (shards_of,), jnp.float32, smallest / len(cuts), high / len(cuts))
        loudness = loudness * jnp.repeat(jnp.exp(heights), extent[axis_at] // shards_of).reshape((-1,) + (1,) * (len(extent) - 1 - axis_at))
    return loudness


def gaussian(stream_key, shape, width, bound, cuts=(), kind=jnp.bfloat16):
    gain = steps_of(stream_key, shape, cuts, -0.22, 0.18) if cuts else 1.0
    result = jax.random.normal(stream_key, shape, jnp.float32) * width * gain
    return jnp.minimum(jnp.maximum(result, -bound), bound).astype(kind)


def bell_draw_with(own_key, dims, deviation, limit, cuts, heavy, kind=jnp.bfloat16):
    values = deviation * jax.random.normal(own_key, dims, jnp.float32)
    if cuts:
        values = values * steps_of(own_key, dims, cuts, -0.22, 0.18)
    return jnp.clip(spiked(values, jax.random.fold_in(own_key, 3), *heavy), -limit, limit).astype(kind)


def setup_inputs(seed: int = 0) -> dict:
    splits = jax.random.split(jax.random.key(seed), 11)
    return {
        "xin": bell_draw_with(splits[0], (NB, TOKENS, BLOCK), 1.0, 6.0, ((1, 32),), (1, 2, 32, 2.75)),
        "dout": gaussian(splits[1], (NB, TOKENS, BLOCK), 1.0, 6.0, ((1, 32),)),
        "weights": gaussian(splits[2], (NB, BLOCK, BLOCK), BLOCK ** -0.5, 0.21875, ((1, 16),)),
        "slot_block": draw_slot_block(jax.random.fold_in(splits[10], 71), 0),
        "left_stat": draw_left_stat(jax.random.fold_in(splits[10], 71), 0),
        "right_stat": draw_right_stat(jax.random.fold_in(splits[10], 71), 0),
        "left_root": draw_left_root(jax.random.fold_in(splits[10], 71), 0),
        "right_root": draw_right_root(jax.random.fold_in(splits[10], 71), 0),
        "first_moment": gaussian(splits[8], (SLOT_ALL, BLOCK, BLOCK), 0.05, 0.3, ((0, 2), (1, 16)), jnp.float32),
        "second_moment": jnp.clip(jnp.exp(math.log(0.01) - 2.30258502 * jax.random.uniform(splits[9], (SLOT_ALL, BLOCK, BLOCK), jnp.float32) ** steps_of(splits[9], (SLOT_ALL, BLOCK, BLOCK), ((0, 2), (1, 16)), -0.2, 0.2)), 0.001, 0.01),
    }


def reference(xin, dout, weights, slot_block, left_stat, right_stat, left_root, right_root, first_moment, second_moment):
    highest = lax.Precision.HIGHEST
    factor = 1.0 / math.sqrt(TOKENS * BLOCK)
    slot_ids = jnp.arange(SLOT_ALL, dtype=jnp.int32)
    new_left, new_right = (left_stat, right_stat)
    new_first, new_second = (first_moment, second_moment)
    updated = []
    for member in range(NB):
        gradient = jnp.dot(xin[member].T, dout[member], preferred_element_type=jnp.float32) * factor
        holder = jnp.sum(slot_ids * (slot_block == member).astype(jnp.int32)).astype(jnp.int32)
        left_gram = jnp.dot(gradient, gradient.T, precision=highest)
        right_gram = jnp.dot(gradient.T, gradient, precision=highest)
        new_left = new_left.at[holder].set(0.5 * left_stat[holder] + 0.5 * left_gram)
        new_right = new_right.at[holder].set(0.5 * right_stat[holder] + 0.5 * right_gram)
        direction = jnp.dot(jnp.dot(left_root[holder], gradient, precision=highest), right_root[holder], precision=highest)
        moment_one = 0.9 * first_moment[holder] + 0.1 * gradient
        moment_two = 0.999 * second_moment[holder] + 0.001 * gradient * gradient
        new_first = new_first.at[holder].set(moment_one)
        new_second = new_second.at[holder].set(moment_two)
        adam = moment_one / (jnp.sqrt(moment_two) + 1e-08)
        graft = jnp.sqrt(jnp.sum(adam * adam)) / (jnp.sqrt(jnp.sum(direction * direction)) + 1e-06)
        updated.append((weights[member].astype(jnp.float32) - 0.05 * graft * direction).astype(jnp.bfloat16))
    return (jnp.stack(updated), new_left, new_right, new_first, new_second)
```

```python
import math

import jax
import jax.numpy as jnp
from jax import lax
from jax.experimental import pallas as pl
from jax.experimental.pallas import tpu as pltpu
from jax.sharding import PartitionSpec as P

F32 = jnp.float32
BF16 = jnp.bfloat16
GROUP = ("tensor", "section")


def spread(value, axis, source):
    kept = jnp.where(lax.axis_index(axis) == source, value, 0).astype(value.dtype)
    return lax.psum(kept, axis)


def absorb_slot(mine_rows, root_rows, portion, col_first):
    highest = lax.Precision.HIGHEST
    row_count = mine_rows.shape[0]
    block_part = jnp.dot(mine_rows, portion.T, precision=highest)
    own_cols = lax.dynamic_slice_in_dim(portion, col_first, row_count, 1)
    right_gram = jnp.dot(own_cols.T, portion, precision=highest)
    left_prod = jnp.dot(root_rows, portion, precision=highest)
    return (block_part, right_gram, left_prod)


def apply_slot(prod_rows, portion):
    return jnp.dot(prod_rows, portion, precision=lax.Precision.HIGHEST)


def any_mesh(
    xin,
    dout,
    weights,
    slot_block,
    left_stat,
    right_stat,
    left_root,
    right_root,
    first_moment,
    second_moment,
):
    block_count, tok_count, block_size = xin.shape
    slot_count, row_count = (left_stat.shape[0], left_stat.shape[1])
    group_count = lax.axis_size(GROUP)
    shard_count = lax.axis_size("shard")
    factor = 1.0 / math.sqrt(tok_count * shard_count * group_count * block_size)
    pieces_out = []
    for grad_member in range(block_count):
        cols = xin[grad_member]
        pieces_out.append(
            jnp.einsum("tr,tc->rc", cols, dout[grad_member], preferred_element_type=jnp.float32)
        )
    partial_rows = lax.psum_scatter(
        jnp.concatenate(pieces_out, axis=1) * factor,
        GROUP,
        scatter_dimension=0,
        tiled=True,
    )
    grad_rows = lax.psum(partial_rows, "shard")
    shard_idx = lax.axis_index("shard")
    group_idx = lax.axis_index(GROUP)
    my_slots = lax.dynamic_slice_in_dim(slot_block, shard_idx * slot_count, slot_count)
    valid = my_slots >= 0
    picks = jnp.maximum(my_slots, 0)
    grad_three = grad_rows.reshape(row_count, block_count, block_size)
    mine = jnp.moveaxis(jnp.take(grad_three, picks, axis=1), 1, 0)
    col_first = group_idx * row_count
    zeros_rows = jnp.zeros((slot_count, row_count, block_size), jnp.float32)
    totals = (zeros_rows, zeros_rows, zeros_rows)
    portion = lax.all_gather(mine, GROUP, axis=1, tiled=True)
    lefts = []
    rights = []
    prods = []
    for slot_pos in range(slot_count):
        current = (totals[0][slot_pos], totals[1][slot_pos], totals[2][slot_pos])
        result = lax.cond(
            valid[slot_pos],
            lambda values: absorb_slot(
                mine[slot_pos], left_root[slot_pos], portion[slot_pos], col_first
            ),
            lambda values: values,
            current,
        )
        lefts.append(result[0])
        rights.append(result[1])
        prods.append(result[2])
    left_gram = jnp.stack(lefts)
    right_gram = jnp.stack(rights)
    left_prod = jnp.stack(prods)
    apply_portion = lax.all_gather(right_root, GROUP, axis=1, tiled=True)
    outputs = []
    for apply_slot_pos in range(slot_count):
        outputs.append(
            lax.cond(
                valid[apply_slot_pos],
                lambda values: apply_slot(left_prod[apply_slot_pos], apply_portion[apply_slot_pos]),
                lambda values: values,
                zeros_rows[apply_slot_pos],
            )
        )
    direction = jnp.stack(outputs)
    moment_one = 0.9 * first_moment + 0.1 * mine
    moment_two = 0.999 * second_moment + 0.001 * mine * mine
    adam = moment_one / (jnp.sqrt(moment_two) + 1e-08)
    adam_sq, dir_sq = lax.psum(
        (jnp.sum(adam * adam, axis=(1, 2)), jnp.sum(direction * direction, axis=(1, 2))),
        GROUP,
    )
    graft = jnp.sqrt(adam_sq) / (jnp.sqrt(dir_sq) + 1e-06)
    mask = valid[:, None, None]
    new_left = jnp.where(mask, 0.5 * left_stat + 0.5 * left_gram, left_stat)
    new_right = jnp.where(mask, 0.5 * right_stat + 0.5 * right_gram, right_stat)
    new_first = jnp.where(mask, moment_one, first_moment)
    new_second = jnp.where(mask, moment_two, second_moment)
    my_weights = jnp.take(weights, picks, axis=0)
    new_rows = (my_weights.astype(jnp.float32) - 0.05 * graft[:, None, None] * direction).astype(
        jnp.bfloat16
    )
    slot_ids = jnp.arange(slot_block.shape[0], dtype=jnp.int32)
    holders = [
        jnp.sum(slot_ids * (slot_block == member).astype(jnp.int32))
        for member in range(block_count)
    ]
    published = []
    for member in range(block_count):
        owner = holders[member] // slot_count
        within = holders[member] % slot_count
        chosen = lax.dynamic_index_in_dim(new_rows, within, 0, keepdims=False)
        published.append(spread(chosen, "shard", owner))
    new_weights = jnp.stack(published)
    return (new_weights, new_left, new_right, new_first, new_second)


def to_core(value):
    return lax.ppermute(value, "section", [(i, i ^ 1) for i in range(4)])


def to_x(value):
    return lax.ppermute(value, "section", [(i, i ^ 2) for i in range(4)])


def to_y(value):
    return lax.ppermute(value, "shard", [(0, 1), (1, 0)])


def to_z(value, bits):
    return lax.ppermute(value, "tensor", [(i, i ^ bits) for i in range(4)])


def to_xz(value, bits):
    pairs = [(4 * z + s, 4 * (z ^ bits) + (s ^ 2)) for z in range(4) for s in range(4)]
    return lax.ppermute(value, GROUP, pairs)


def to_cy(value):
    pairs = [(4 * y + s, 4 * (1 - y) + (s ^ 1)) for y in range(2) for s in range(4)]
    return lax.ppermute(value, ("shard", "section"), pairs)


def row_dot(rows, full):
    return lax.dot_general(rows, full, (((1,), (0,)), ((), ())), preferred_element_type=F32)


def row_dot_t(rows, full):
    return lax.dot_general(rows, full, (((1,), (1,)), ((), ())), preferred_element_type=F32)


def halves(value):
    high = value.astype(BF16)
    return high, (value - high.astype(F32)).astype(BF16)


def place_pieces(where, pieces, high_ref, low_ref):
    rows = pieces[0].shape[0]
    for step in range(4):
        for side in range(2):
            spot = 2 * (where[0] ^ step) + (where[1] ^ side)
            first = pl.multiple_of(spot * rows, 32)
            high, low = halves(pieces[2 * step + side][...])
            high_ref[pl.ds(first, rows), :] = high
            low_ref[pl.ds(first, rows), :] = low


def root_kernel(where, *refs):
    place_pieces(where, refs[:8], refs[8], refs[9])


def join_root(where, pieces):
    size = pieces[0].shape[1]
    return pl.pallas_call(
        root_kernel,
        out_shape=[jax.ShapeDtypeStruct((size, size), BF16)] * 2,
        in_specs=[pl.BlockSpec(memory_space=pltpu.SMEM)]
        + [pl.BlockSpec(memory_space=pltpu.VMEM)] * 8,
        out_specs=[pl.BlockSpec(memory_space=pltpu.VMEM)] * 2,
        compiler_params=pltpu.CompilerParams(vmem_limit_bytes=40 << 20),
    )(where, *pieces)


def block_kernel(where, *refs):
    pieces = refs[:8]
    left_ref, root_high, root_low = refs[8:11]
    left_out, right_out, dir_out, sum_out = refs[11:15]
    high_ref, low_ref = refs[15:17]
    place_pieces(where, pieces, high_ref, low_ref)
    rows, size = left_ref.shape
    first = (2 * where[0] + where[1]) * rows
    high, low = high_ref[...], low_ref[...]
    left_high, left_low = halves(left_ref[...])
    prod = row_dot(left_high, high) + (row_dot(left_low, high) + row_dot(left_high, low))
    prod_high, prod_low = halves(prod)
    root_h, root_l = root_high[...], root_low[...]
    direction = row_dot(prod_high, root_h) + (
        row_dot(prod_low, root_h) + row_dot(prod_high, root_l)
    )
    dir_out[...] = direction
    sum_out[...] = jnp.sum(direction * direction, axis=0, keepdims=True)
    own_high, own_low = halves(pieces[0][...])
    left_out[...] = row_dot_t(own_high, high) + (
        row_dot_t(own_low, high) + row_dot_t(own_high, low)
    )
    row_ids = lax.broadcasted_iota(jnp.int32, (rows, size), 0) + first
    col_ids = lax.broadcasted_iota(jnp.int32, (rows, size), 1)
    pick = jnp.where(row_ids == col_ids, 1.0, 0.0).astype(BF16)
    col_high = row_dot_t(pick, high).astype(BF16)
    col_low = row_dot_t(pick, low).astype(BF16)
    right_out[...] = row_dot(col_high, high) + (row_dot(col_low, high) + row_dot(col_high, low))


def block_products(where, pieces, left_rows, root_high, root_low):
    rows, size = left_rows.shape
    tile = jax.ShapeDtypeStruct((rows, size), F32)
    return pl.pallas_call(
        block_kernel,
        out_shape=[tile, tile, tile, jax.ShapeDtypeStruct((1, size), F32)],
        in_specs=[pl.BlockSpec(memory_space=pltpu.SMEM)]
        + [pl.BlockSpec(memory_space=pltpu.VMEM)] * 11,
        out_specs=[pl.BlockSpec(memory_space=pltpu.VMEM)] * 4,
        scratch_shapes=[pltpu.VMEM((size, size), BF16)] * 2,
        compiler_params=pltpu.CompilerParams(vmem_limit_bytes=48 << 20),
    )(where, *pieces, left_rows, root_high, root_low)


def gather_chips(value):
    column = [value] + [to_z(value, bits) for bits in (1, 2, 3)]
    pieces = []
    for piece in column:
        pieces += [piece, to_x(piece)]
    return pieces


def pick_block(stack, index):
    return lax.dynamic_index_in_dim(stack, index, 0, keepdims=False)


def pick_rows(value, first, count):
    return lax.dynamic_slice_in_dim(value, first, count, 0)


def two_planes(
    xin,
    dout,
    weights,
    slot_block,
    left_stat,
    right_stat,
    left_root,
    right_root,
    first_moment,
    second_moment,
):
    block_count, tok_count, size = xin.shape
    slot_count, rows = left_stat.shape[:2]
    factor = 1.0 / math.sqrt(tok_count * lax.axis_size(("shard",) + GROUP) * size)
    s = lax.axis_index("shard")
    z = lax.axis_index("tensor")
    section = lax.axis_index("section")
    x, c = section // 2, section % 2
    where = jnp.stack([z, x]).astype(jnp.int32)

    table = slot_block.reshape(2, slot_count)
    used = (table >= 0).astype(jnp.int32)
    order = jnp.cumsum(used, axis=1) * used
    spots = jnp.arange(slot_count, dtype=jnp.int32)
    place = jnp.stack([jnp.sum(jnp.where(order == j + 1, spots, 0), axis=1) for j in (0, 1)], 1)
    block = jnp.stack([jnp.sum(jnp.where(order == j + 1, table, 0), axis=1) for j in (0, 1)], 1)
    mine, far = block[s, c], block[1 - s, c]
    sib_mine, sib_far = block[s, 1 - c], block[1 - s, 1 - c]
    my_place, sib_place = place[s, c], place[s, 1 - c]

    def gradient(own, sibling):
        other_in = to_core(pick_block(xin, sibling))
        other_out = to_core(pick_block(dout, sibling))
        first = jnp.einsum(
            "tr,tc->rc", pick_block(xin, own), pick_block(dout, own), preferred_element_type=F32
        )
        return first + jnp.einsum("tr,tc->rc", other_in, other_out, preferred_element_type=F32)

    grad_far = gradient(far, sib_far)
    grad_mine = gradient(mine, sib_mine)

    def chip_rows(stack):
        other = to_core(pick_block(stack, sib_place))
        own = pick_block(stack, my_place)
        return jnp.concatenate(
            [jnp.where(c == 0, own, other), jnp.where(c == 0, other, own)], axis=0
        )

    chip = 2 * rows
    total = None
    for bits in (3, 2, 1, 0):
        start = (z ^ bits) * (2 * chip)
        got = to_y(pick_rows(grad_far, start, 2 * chip))
        both = got + pick_rows(grad_mine, start, 2 * chip)
        got = to_x(pick_rows(both, (1 - x) * chip, chip))
        both = got + pick_rows(both, x * chip, chip)
        if bits:
            both = to_z(both, bits)
        total = both if total is None else total + both
    grad = total * factor

    root_high, root_low = join_root(where, gather_chips(chip_rows(right_root)))
    left_rows = chip_rows(left_root)
    pieces = gather_chips(grad)

    def by_slot(own, other):
        return jnp.where(c == 0, own, other), jnp.where(c == 0, other, own)

    def swap_rows(value):
        sent = to_core(pick_rows(value, (1 - c) * rows, rows))
        return by_slot(pick_rows(value, c * rows, rows), sent)

    grad_rows = swap_rows(grad)
    places = [place[s, 0], place[s, 1]]
    held = [jnp.arange(slot_count)[:, None, None] == places[j] for j in (0, 1)]
    firsts = [
        0.9 * pick_block(first_moment, places[j]) + 0.1 * grad_rows[j] for j in (0, 1)
    ]
    seconds = [
        0.999 * pick_block(second_moment, places[j]) + 0.001 * grad_rows[j] * grad_rows[j]
        for j in (0, 1)
    ]
    new_first = jnp.where(held[0], firsts[0], jnp.where(held[1], firsts[1], first_moment))
    new_second = jnp.where(held[0], seconds[0], jnp.where(held[1], seconds[1], second_moment))

    def device_sum(mine_sums):
        near = mine_sums
        near = jnp.concatenate([near, to_core(near), to_y(near), to_cy(near)], axis=0)
        total = near
        parts = [to_x(near)]
        for bits in (1, 2, 3):
            parts += [to_z(near, bits), to_xz(near, bits)]
        for part in parts:
            total = total + part
        return total

    adams = [firsts[j] / (jnp.sqrt(seconds[j]) + 1e-08) for j in (0, 1)]
    adam_sums = [jnp.sum(value * value) for value in adams]
    lanes = lax.broadcasted_iota(jnp.int32, (1, 128), 1)
    adam_own = jnp.where(lanes == 0, adam_sums[0], jnp.where(lanes == 1, adam_sums[1], 0.0))
    adam_all = device_sum(adam_own)
    adam_near = adam_all[0] + adam_all[1]
    adam_mirror = adam_all[2] + adam_all[3]

    left_gram, right_gram, direction, dir_lanes = block_products(
        where, pieces, left_rows, root_high, root_low
    )
    dir_own = jnp.where(lanes == 0, jnp.sum(dir_lanes), 0.0)
    dir_all = device_sum(dir_own)[:, 0]

    left_rows2 = swap_rows(left_gram)
    right_rows2 = swap_rows(right_gram)
    new_left = jnp.where(
        held[0] | held[1],
        0.5 * left_stat + 0.5 * jnp.where(held[0], left_rows2[0], left_rows2[1]),
        left_stat,
    )
    new_right = jnp.where(
        held[0] | held[1],
        0.5 * right_stat + 0.5 * jnp.where(held[0], right_rows2[0], right_rows2[1]),
        right_stat,
    )

    own_dir = pick_rows(direction, c * rows, rows)
    out_dir = pick_rows(direction, (1 - c) * rows, rows)
    near_dir = jnp.stack([own_dir, to_core(out_dir)])
    dirs = jnp.concatenate([near_dir, to_y(near_dir)])
    adam_near_own = jnp.where(c == 0, adam_near[0], adam_near[1])
    adam_near_sib = jnp.where(c == 0, adam_near[1], adam_near[0])
    adam_mir_own = jnp.where(c == 0, adam_mirror[0], adam_mirror[1])
    adam_mir_sib = jnp.where(c == 0, adam_mirror[1], adam_mirror[0])
    adam_four = jnp.stack([adam_near_own, adam_near_sib, adam_mir_own, adam_mir_sib])
    graft = jnp.sqrt(adam_four) / (jnp.sqrt(dir_all) + 1e-06)
    order_four = jnp.stack([mine, sib_mine, far, sib_far])
    members = []
    for member in range(block_count):
        hit = order_four == member
        value = jnp.zeros((rows, size), F32)
        for j in range(4):
            value = jnp.where(hit[j], dirs[j], value)
        scale = jnp.sum(jnp.where(hit, graft, 0.0))
        members.append(
            (weights[member].astype(F32) - 0.05 * scale * value).astype(BF16)
        )
    return (jnp.stack(members), new_left, new_right, new_first, new_second)


def solution(mesh):
    placed = (
        P(None, ("shard", "tensor", "section"), None),
        P(None, ("shard", "tensor", "section"), None),
        P(None, ("tensor", "section"), None),
        P(),
        P("shard", ("tensor", "section"), None),
        P("shard", ("tensor", "section"), None),
        P("shard", ("tensor", "section"), None),
        P("shard", ("tensor", "section"), None),
        P("shard", ("tensor", "section"), None),
        P("shard", ("tensor", "section"), None),
    )
    shape = mesh.shape
    pair = (shape["shard"], shape["tensor"], shape["section"]) == (2, 4, 4)
    return jax.shard_map(
        two_planes if pair else any_mesh,
        mesh=mesh,
        in_specs=placed,
        out_specs=(
            P(None, ("tensor", "section"), None),
            P("shard", ("tensor", "section"), None),
            P("shard", ("tensor", "section"), None),
            P("shard", ("tensor", "section"), None),
            P("shard", ("tensor", "section"), None),
        ),
        check_vma=False,
    )
```

```python
import functools
import math

import jax
import jax.numpy as jnp
from jax import lax
from jax.experimental import pallas as pl
from jax.experimental.pallas import tpu as pltpu
from jax.sharding import PartitionSpec as P

F32 = jnp.float32
BF16 = jnp.bfloat16
GROUP = ("tensor", "section")


def spread(value, axis, source):
    kept = jnp.where(lax.axis_index(axis) == source, value, 0).astype(value.dtype)
    return lax.psum(kept, axis)


def absorb_slot(mine_rows, root_rows, portion, col_first):
    highest = lax.Precision.HIGHEST
    row_count = mine_rows.shape[0]
    block_part = jnp.dot(mine_rows, portion.T, precision=highest)
    own_cols = lax.dynamic_slice_in_dim(portion, col_first, row_count, 1)
    right_gram = jnp.dot(own_cols.T, portion, precision=highest)
    left_prod = jnp.dot(root_rows, portion, precision=highest)
    return (block_part, right_gram, left_prod)


def apply_slot(prod_rows, portion):
    return jnp.dot(prod_rows, portion, precision=lax.Precision.HIGHEST)


def any_mesh(
    xin,
    dout,
    weights,
    slot_block,
    left_stat,
    right_stat,
    left_root,
    right_root,
    first_moment,
    second_moment,
):
    block_count, tok_count, block_size = xin.shape
    slot_count, row_count = (left_stat.shape[0], left_stat.shape[1])
    group_count = lax.axis_size(GROUP)
    shard_count = lax.axis_size("shard")
    factor = 1.0 / math.sqrt(tok_count * shard_count * group_count * block_size)
    pieces_out = []
    for grad_member in range(block_count):
        cols = xin[grad_member]
        pieces_out.append(
            jnp.einsum("tr,tc->rc", cols, dout[grad_member], preferred_element_type=jnp.float32)
        )
    partial_rows = lax.psum_scatter(
        jnp.concatenate(pieces_out, axis=1) * factor,
        GROUP,
        scatter_dimension=0,
        tiled=True,
    )
    grad_rows = lax.psum(partial_rows, "shard")
    shard_idx = lax.axis_index("shard")
    group_idx = lax.axis_index(GROUP)
    my_slots = lax.dynamic_slice_in_dim(slot_block, shard_idx * slot_count, slot_count)
    valid = my_slots >= 0
    picks = jnp.maximum(my_slots, 0)
    grad_three = grad_rows.reshape(row_count, block_count, block_size)
    mine = jnp.moveaxis(jnp.take(grad_three, picks, axis=1), 1, 0)
    col_first = group_idx * row_count
    zeros_rows = jnp.zeros((slot_count, row_count, block_size), jnp.float32)
    totals = (zeros_rows, zeros_rows, zeros_rows)
    portion = lax.all_gather(mine, GROUP, axis=1, tiled=True)
    lefts = []
    rights = []
    prods = []
    for slot_pos in range(slot_count):
        current = (totals[0][slot_pos], totals[1][slot_pos], totals[2][slot_pos])
        result = lax.cond(
            valid[slot_pos],
            lambda values: absorb_slot(
                mine[slot_pos], left_root[slot_pos], portion[slot_pos], col_first
            ),
            lambda values: values,
            current,
        )
        lefts.append(result[0])
        rights.append(result[1])
        prods.append(result[2])
    left_gram = jnp.stack(lefts)
    right_gram = jnp.stack(rights)
    left_prod = jnp.stack(prods)
    apply_portion = lax.all_gather(right_root, GROUP, axis=1, tiled=True)
    outputs = []
    for apply_slot_pos in range(slot_count):
        outputs.append(
            lax.cond(
                valid[apply_slot_pos],
                lambda values: apply_slot(left_prod[apply_slot_pos], apply_portion[apply_slot_pos]),
                lambda values: values,
                zeros_rows[apply_slot_pos],
            )
        )
    direction = jnp.stack(outputs)
    moment_one = 0.9 * first_moment + 0.1 * mine
    moment_two = 0.999 * second_moment + 0.001 * mine * mine
    adam = moment_one / (jnp.sqrt(moment_two) + 1e-08)
    adam_sq, dir_sq = lax.psum(
        (jnp.sum(adam * adam, axis=(1, 2)), jnp.sum(direction * direction, axis=(1, 2))),
        GROUP,
    )
    graft = jnp.sqrt(adam_sq) / (jnp.sqrt(dir_sq) + 1e-06)
    mask = valid[:, None, None]
    new_left = jnp.where(mask, 0.5 * left_stat + 0.5 * left_gram, left_stat)
    new_right = jnp.where(mask, 0.5 * right_stat + 0.5 * right_gram, right_stat)
    new_first = jnp.where(mask, moment_one, first_moment)
    new_second = jnp.where(mask, moment_two, second_moment)
    my_weights = jnp.take(weights, picks, axis=0)
    new_rows = (my_weights.astype(jnp.float32) - 0.05 * graft[:, None, None] * direction).astype(
        jnp.bfloat16
    )
    slot_ids = jnp.arange(slot_block.shape[0], dtype=jnp.int32)
    holders = [
        jnp.sum(slot_ids * (slot_block == member).astype(jnp.int32))
        for member in range(block_count)
    ]
    published = []
    for member in range(block_count):
        owner = holders[member] // slot_count
        within = holders[member] % slot_count
        chosen = lax.dynamic_index_in_dim(new_rows, within, 0, keepdims=False)
        published.append(spread(chosen, "shard", owner))
    new_weights = jnp.stack(published)
    return (new_weights, new_left, new_right, new_first, new_second)


def to_core(value):
    return lax.ppermute(value, "section", [(i, i ^ 1) for i in range(4)])


def to_x(value):
    return lax.ppermute(value, "section", [(i, i ^ 2) for i in range(4)])


def to_y(value):
    return lax.ppermute(value, "shard", [(0, 1), (1, 0)])


def to_z(value, bits):
    return lax.ppermute(value, "tensor", [(i, i ^ bits) for i in range(4)])


def to_cy(value):
    pairs = [(4 * y + s, 4 * (1 - y) + (s ^ 1)) for y in range(2) for s in range(4)]
    return lax.ppermute(value, ("shard", "section"), pairs)


def row_dot(rows, full):
    return lax.dot_general(rows, full, (((1,), (0,)), ((), ())), preferred_element_type=F32)


def row_dot_t(rows, full):
    return lax.dot_general(rows, full, (((1,), (1,)), ((), ())), preferred_element_type=F32)


def token_dot(left, right):
    return lax.dot_general(left, right, (((0,), (0,)), ((), ())), preferred_element_type=F32)


def halves(value):
    high = value.astype(BF16)
    return high, (value - high.astype(F32)).astype(BF16)


def coded_rows(rows):
    return rows + rows // 3


def encode(value):
    rows = value.shape[0]
    part = rows // 4
    top = jnp.maximum(jnp.max(jnp.abs(value), axis=0, keepdims=True), 1e-30)
    exponent = jnp.ceil(jnp.log2(top))
    scaled = value * (jnp.exp2(-exponent) * 32760.0)
    coarse = jnp.round(scaled)
    fine = jnp.clip(jnp.floor((scaled - coarse) * 16.0), -8.0, 7.0) + 8.0
    words = fine[:part] - 32768.0
    for index in (1, 2, 3):
        words = words + fine[index * part : (index + 1) * part] * float(16**index)
    tail = jnp.broadcast_to(exponent, (rows // 3 - part, value.shape[1]))
    both = jnp.concatenate([coarse, words, tail], axis=0)
    return both.astype(jnp.int32).astype(jnp.int16)


def decode(words):
    rows = words.shape[0] // 4 * 3
    part = rows // 4
    wide = words.astype(jnp.int32)
    coarse = wide[:rows].astype(F32)
    fine = wide[rows : rows + part] + 32768
    exponent = wide[rows + part : rows + part + 8].astype(F32)[:1]
    parts = [(jnp.right_shift(fine, 4 * index) & 15).astype(F32) for index in range(4)]
    low = jnp.concatenate(parts, axis=0)
    return (coarse + (low - 7.5) * (1.0 / 16.0)) * (jnp.exp2(exponent) * (1.0 / 32760.0))


def used_slot(meta, plane, nth):
    seen = jnp.int32(0)
    place = jnp.int32(0)
    block = jnp.int32(0)
    for spot in range(4):
        entry = meta[4 * plane + spot]
        used = entry >= 0
        hit = jnp.logical_and(used, seen == nth)
        place = jnp.where(hit, spot, place)
        block = jnp.where(hit, entry, block)
        seen = seen + jnp.where(used, 1, 0)
    return place, block


SMEM_SPEC = pl.BlockSpec(memory_space=pltpu.SMEM)
VMEM_SPEC = pl.BlockSpec(memory_space=pltpu.VMEM)
ANY_SPEC = pl.BlockSpec(memory_space=pl.ANY)


def call(body, outs, ins, args, scratch=(), out_specs=None):
    return pl.pallas_call(
        body,
        out_shape=outs,
        in_specs=ins,
        out_specs=[VMEM_SPEC] * len(outs) if out_specs is None else out_specs,
        scratch_shapes=list(scratch),
        compiler_params=pltpu.CompilerParams(vmem_limit_bytes=48 << 20),
    )(*args)


def pick_kernel(meta, xin, dout, left, right, x_far, d_far, x_mine, d_mine, roots, sems):
    plane, core = meta[8], meta[11]
    place, mine = used_slot(meta, plane, 1 - core)
    _, far = used_slot(meta, 1 - plane, 1 - core)
    copies = [
        pltpu.make_async_copy(xin.at[far], x_far, sems.at[0]),
        pltpu.make_async_copy(dout.at[far], d_far, sems.at[1]),
        pltpu.make_async_copy(xin.at[mine], x_mine, sems.at[2]),
        pltpu.make_async_copy(dout.at[mine], d_mine, sems.at[3]),
        pltpu.make_async_copy(left.at[place], roots.at[0], sems.at[4]),
        pltpu.make_async_copy(right.at[place], roots.at[1], sems.at[5]),
    ]
    for copy in copies:
        copy.start()
    for copy in copies:
        copy.wait()


def own_kernel(meta, x_ref, d_ref, out_ref):
    out_ref[...] = token_dot(x_ref[...], d_ref[...])


def own_part(meta, xin, dout, across):
    _, tokens, size = xin.shape

    def block_of(step, meta_ref):
        plane = 1 - meta_ref[8] if across else meta_ref[8]
        return (used_slot(meta_ref, plane, meta_ref[11])[1], 0, 0)

    taken = pl.BlockSpec((None, tokens, size), block_of)
    return pl.pallas_call(
        own_kernel,
        out_shape=jax.ShapeDtypeStruct((size, size), F32),
        grid_spec=pltpu.PrefetchScalarGridSpec(
            num_scalar_prefetch=1,
            grid=(1,),
            in_specs=[taken, taken],
            out_specs=pl.BlockSpec((size, size), lambda step, meta_ref: (0, 0)),
        ),
        compiler_params=pltpu.CompilerParams(vmem_limit_bytes=48 << 20),
    )(meta, xin, dout)


def far_kernel(meta, x_ref, d_ref, own_ref, *refs):
    outs, total = refs[:4], refs[4]
    total[...] = own_ref[...] + token_dot(x_ref[...], d_ref[...])
    span = total.shape[0] // 4
    for out, bits in zip(outs, (3, 2, 1, 0)):
        first = pl.multiple_of((meta[9] ^ bits) * span, 64)
        out[...] = encode(total[pl.ds(first, span), :])


def mine_kernel(x_ref, d_ref, own_ref, out_ref):
    out_ref[...] = own_ref[...] + token_dot(x_ref[...], d_ref[...])


def rows_kernel(meta, left, right, got, left_out, right_out):
    core = meta[11]
    place, _ = used_slot(meta, meta[8], core)
    rows = left.shape[1]
    own_first = pl.multiple_of(core * rows, 16)
    sib_first = pl.multiple_of((1 - core) * rows, 16)
    for index, (source, out) in enumerate(((left, left_out), (right, right_out))):
        out[pl.ds(own_first, rows), :] = source[place]
        out[pl.ds(sib_first, rows), :] = got[index]


def y_kernel(meta, got, mine, coded, keep, both):
    rows = keep.shape[0]
    both[...] = decode(got[...]) + mine[...]
    side = meta[10]
    keep[...] = both[pl.ds(pl.multiple_of(side * rows, 32), rows), :]
    coded[...] = encode(both[pl.ds(pl.multiple_of((1 - side) * rows, 32), rows), :])


def after_y(meta, got, mine, bits):
    size = mine.shape[1]
    rows = size // 8
    return pl.pallas_call(
        y_kernel,
        out_shape=[
            jax.ShapeDtypeStruct((coded_rows(rows), size), jnp.int16),
            jax.ShapeDtypeStruct((rows, size), F32),
        ],
        grid_spec=pltpu.PrefetchScalarGridSpec(
            num_scalar_prefetch=1,
            grid=(1,),
            in_specs=[
                pl.BlockSpec(got.shape, lambda step, meta_ref: (0, 0)),
                pl.BlockSpec((2 * rows, size), lambda step, meta_ref: (meta_ref[9] ^ bits, 0)),
            ],
            out_specs=[
                pl.BlockSpec((coded_rows(rows), size), lambda step, meta_ref: (0, 0)),
                pl.BlockSpec((rows, size), lambda step, meta_ref: (0, 0)),
            ],
            scratch_shapes=[pltpu.VMEM((2 * rows, size), F32)],
        ),
        compiler_params=pltpu.CompilerParams(vmem_limit_bytes=48 << 20),
    )(meta, got, mine)


def x_kernel(got, keep, coded):
    coded[...] = encode(decode(got[...]) + keep[...])


def grad_kernel(factor, got, keep, one, two, three, grad, coded):
    total = decode(got[...]) + keep[...]
    for part in (one, two, three):
        total = total + decode(part[...])
    total = total * factor
    grad[...] = total
    coded[...] = encode(total)


def put_rows(spot, value, high_ref, low_ref):
    rows = value.shape[0]
    first = pl.multiple_of(spot * rows, 32)
    high, low = halves(value)
    high_ref[pl.ds(first, rows), :] = high
    low_ref[pl.ds(first, rows), :] = low


def root_kernel(meta, *refs):
    for step in range(4):
        for side in range(2):
            spot = 2 * (meta[9] ^ step) + (meta[10] ^ side)
            put_rows(spot, refs[2 * step + side][...], refs[8], refs[9])


def block_kernel(meta, *refs):
    grad_ref, pieces = refs[0], refs[1:8]
    left_ref, root_high, root_low, adam_ref = refs[8:12]
    own_left, own_right, own_dir, sib_out, sib_dir, sums = refs[12:18]
    high_ref, low_ref, whole = refs[18:21]
    for index in range(8):
        spot = 2 * (meta[9] ^ (index // 2)) + (meta[10] ^ (index % 2))
        value = grad_ref[...] if index == 0 else decode(pieces[index - 1][...])
        put_rows(spot, value, high_ref, low_ref)
    rows, size = left_ref.shape
    half = rows // 2
    own = pl.ds(pl.multiple_of(meta[11] * half, 16), half)
    sib = pl.ds(pl.multiple_of((1 - meta[11]) * half, 16), half)
    first = (2 * meta[9] + meta[10]) * rows
    high, low = high_ref[...], low_ref[...]
    left_high, left_low = halves(left_ref[...])
    prod = row_dot(left_high, high) + (row_dot(left_low, high) + row_dot(left_high, low))
    prod_high, prod_low = halves(prod)
    root_h, root_l = root_high[...], root_low[...]
    direction = row_dot(prod_high, root_h) + (
        row_dot(prod_low, root_h) + row_dot(prod_high, root_l)
    )
    whole[...] = direction
    own_dir[...] = whole[own, :]
    sib_dir[...] = whole[sib, :]
    sib_out[2] = whole[sib, :]
    lane = lax.broadcasted_iota(jnp.int32, (1, 128), 1)
    line = jnp.where(lane == 2, jnp.sum(direction * direction), adam_ref[...])
    sums[...] = jnp.broadcast_to(line.reshape(1, 1, 128), sums.shape)
    own_high, own_low = halves(grad_ref[...])
    whole[...] = row_dot_t(own_high, high) + (
        row_dot_t(own_low, high) + row_dot_t(own_high, low)
    )
    own_left[...] = whole[own, :]
    sib_out[0] = whole[sib, :]
    row_ids = lax.broadcasted_iota(jnp.int32, (rows, size), 0) + first
    col_ids = lax.broadcasted_iota(jnp.int32, (rows, size), 1)
    pick = jnp.where(row_ids == col_ids, 1.0, 0.0).astype(BF16)
    col_high = row_dot_t(pick, high).astype(BF16)
    col_low = row_dot_t(pick, low).astype(BF16)
    whole[...] = row_dot(col_high, high) + (row_dot(col_low, high) + row_dot(col_high, low))
    own_right[...] = whole[own, :]
    sib_out[1] = whole[sib, :]


def moment_kernel(meta, grad, got, first, second, first_out, second_out, adam_out):
    plane, core = meta[8], meta[11]
    rows = got.shape[0]
    first_out[...] = first[...]
    second_out[...] = second[...]
    lane = lax.broadcasted_iota(jnp.int32, (1, 128), 1)
    line = jnp.zeros((1, 128), F32)
    own = grad[pl.ds(pl.multiple_of(core * rows, 16), rows), :]
    for slot, value in ((core, own), (1 - core, got[...])):
        place, _ = used_slot(meta, plane, slot)
        one = 0.9 * first[place] + 0.1 * value
        two = 0.999 * second[place] + 0.001 * value * value
        first_out[place] = one
        second_out[place] = two
        adam = one / (jnp.sqrt(two) + 1e-08)
        line = line + jnp.where(lane == slot, jnp.sum(adam * adam), 0.0)
    adam_out[...] = line


def last_kernel(
    meta,
    sums,
    own_left,
    own_right,
    own_dir,
    got,
    y_dir,
    cy_dir,
    weights,
    left,
    right,
    weights_out,
    left_out,
    right_out,
):
    plane, core = meta[8], meta[11]
    left_out[...] = left[...]
    right_out[...] = right[...]
    for slot, left_gram, right_gram in (
        (core, own_left[...], own_right[...]),
        (1 - core, got[0], got[1]),
    ):
        place, _ = used_slot(meta, plane, slot)
        left_out[place] = 0.5 * left[place] + 0.5 * left_gram
        right_out[place] = 0.5 * right[place] + 0.5 * right_gram
    lane = lax.broadcasted_iota(jnp.int32, (1, 128), 1)

    def graft(of_plane, slot):
        line = jnp.zeros((1, 128), F32)
        for device in range(16):
            row = sums[of_plane * 16 + device]
            kept = jnp.logical_or(lane == slot, jnp.logical_and(lane == 2, slot == device % 2))
            line = line + jnp.where(kept, row, 0.0)
        dir_sq = jnp.sum(jnp.where(lane == 2, line, 0.0), axis=1, keepdims=True)
        adam_sq = jnp.sum(jnp.where(lane == 2, 0.0, line), axis=1, keepdims=True)
        return jnp.sqrt(adam_sq) / (jnp.sqrt(dir_sq) + 1e-06)

    for of_plane, slot, value in (
        (plane, core, own_dir[...]),
        (plane, 1 - core, got[2]),
        (1 - plane, core, y_dir[...]),
        (1 - plane, 1 - core, cy_dir[...]),
    ):
        _, block = used_slot(meta, of_plane, slot)
        step = 0.05 * graft(of_plane, slot)
        weights_out[block] = (weights[block].astype(F32) - step * value).astype(BF16)


def two_planes(
    xin,
    dout,
    weights,
    slot_block,
    left_stat,
    right_stat,
    left_root,
    right_root,
    first_moment,
    second_moment,
):
    block_count, tokens, size = xin.shape
    slot_count, rows = left_stat.shape[:2]
    device_count = lax.axis_size(("shard",) + GROUP)
    factor = 1.0 / math.sqrt(tokens * device_count * size)
    section = lax.axis_index("section")
    meta = jnp.concatenate(
        [
            slot_block,
            jnp.stack(
                [lax.axis_index("shard"), lax.axis_index("tensor"), section // 2, section % 2]
            ).astype(jnp.int32),
        ]
    )

    def shape(*dims, dtype=F32):
        return jax.ShapeDtypeStruct(dims, dtype)

    words = jnp.int16
    rows_in = shape(tokens, size, dtype=BF16)
    x_far, d_far, x_mine, d_mine, roots = call(
        pick_kernel,
        [rows_in] * 4 + [shape(2, rows, size)],
        [SMEM_SPEC] + [ANY_SPEC] * 4,
        (meta, xin, dout, left_root, right_root),
        [pltpu.SemaphoreType.DMA((6,))],
        [ANY_SPEC] * 5,
    )
    x_far, d_far = to_core(x_far), to_core(d_far)
    x_mine, d_mine, roots = to_core(x_mine), to_core(d_mine), to_core(roots)
    own_far = own_part(meta, xin, dout, True)
    own_mine = own_part(meta, xin, dout, False)
    chunk = coded_rows(size // 4)
    coded = call(
        far_kernel,
        [shape(chunk, size, dtype=words)] * 4,
        [SMEM_SPEC] + [VMEM_SPEC] * 3,
        (meta, x_far, d_far, own_far),
        [pltpu.VMEM((size, size), F32)],
    )
    got_y = [to_y(value) for value in coded]
    (mine,) = call(
        mine_kernel,
        [shape(size, size)],
        [VMEM_SPEC] * 3,
        (x_mine, d_mine, own_mine),
    )
    left_rows, right_rows = call(
        rows_kernel,
        [shape(2 * rows, size)] * 2,
        [SMEM_SPEC] + [VMEM_SPEC] * 3,
        (meta, left_root, right_root, roots),
    )
    root_column = [right_rows] + [to_z(right_rows, bits) for bits in (1, 2, 3)]

    piece = shape(coded_rows(2 * rows), size, dtype=words)
    order = (3, 2, 1, 0)
    got_x, keeps, got_z = [], [], []
    for index, bits in enumerate(order):
        arrived = got_y[index]
        if index == 1:
            arrived, got_x[0] = lax.optimization_barrier((arrived, got_x[0]))
        if index == 2:
            arrived, got_x[1] = lax.optimization_barrier((arrived, got_x[1]))
        if index == 3:
            arrived, got_x[2], got_z[0] = lax.optimization_barrier(
                (arrived, got_x[2], got_z[0])
            )
        sent, keep = after_y(meta, arrived, mine, bits)
        got_x.append(to_x(sent))
        keeps.append(keep)
        if index:
            (sent,) = call(
                x_kernel, [piece], [VMEM_SPEC] * 2, (got_x[index - 1], keeps[index - 1])
            )
            got_z.append(to_z(sent, order[index - 1]))
    grad, coded = call(
        functools.partial(grad_kernel, factor),
        [shape(2 * rows, size), piece],
        [VMEM_SPEC] * 5,
        (got_x[3], keeps[3], *got_z),
    )

    column = [coded] + [to_z(coded, bits) for bits in (1, 2, 3)]
    pieces = []
    for part in column:
        pieces += [part, to_x(part)]

    root_pieces = []
    for part in root_column:
        root_pieces += [part, to_x(part)]
    root_high, root_low = call(
        root_kernel,
        [shape(size, size, dtype=BF16)] * 2,
        [SMEM_SPEC] + [VMEM_SPEC] * 8,
        (meta, *root_pieces),
    )

    core = section % 2
    grad_out = lax.dynamic_slice_in_dim(grad, (1 - core) * rows, rows, 0)
    stack = shape(slot_count, rows, size)
    new_first, new_second, adam = call(
        moment_kernel,
        [stack, stack, shape(1, 128)],
        [SMEM_SPEC] + [VMEM_SPEC] * 4,
        (meta, grad, to_core(grad_out), first_moment, second_moment),
    )
    tile = shape(rows, size)
    own_left, own_right, own_dir, sib_out, sib_dir, sums = call(
        block_kernel,
        [tile, tile, tile, shape(3, rows, size), tile, shape(device_count, 1, 128)],
        [SMEM_SPEC] + [VMEM_SPEC] * 12,
        (meta, grad, *pieces[1:], left_rows, root_high, root_low, adam),
        [pltpu.VMEM((size, size), BF16)] * 2 + [pltpu.VMEM((2 * rows, size), F32)],
    )
    got = to_core(sib_out)
    y_dir = to_y(own_dir)
    cy_dir = to_cy(sib_dir)
    sums = lax.all_to_all(sums, ("shard",) + GROUP, 0, 0)
    return tuple(call(
        last_kernel,
        [shape(block_count, rows, size, dtype=BF16), stack, stack],
        [SMEM_SPEC] + [VMEM_SPEC] * 10,
        (
            meta,
            sums,
            own_left,
            own_right,
            own_dir,
            got,
            y_dir,
            cy_dir,
            weights,
            left_stat,
            right_stat,
        ),
    )) + (new_first, new_second)


def solution(mesh):
    placed = (
        P(None, ("shard", "tensor", "section"), None),
        P(None, ("shard", "tensor", "section"), None),
        P(None, ("tensor", "section"), None),
        P(),
        P("shard", ("tensor", "section"), None),
        P("shard", ("tensor", "section"), None),
        P("shard", ("tensor", "section"), None),
        P("shard", ("tensor", "section"), None),
        P("shard", ("tensor", "section"), None),
        P("shard", ("tensor", "section"), None),
    )
    shape = mesh.shape
    pair = (shape["shard"], shape["tensor"], shape["section"]) == (2, 4, 4)
    return jax.shard_map(
        two_planes if pair else any_mesh,
        mesh=mesh,
        in_specs=placed,
        out_specs=(
            P(None, ("tensor", "section"), None),
            P("shard", ("tensor", "section"), None),
            P("shard", ("tensor", "section"), None),
            P("shard", ("tensor", "section"), None),
            P("shard", ("tensor", "section"), None),
        ),
        check_vma=False,
    )
```

```python
import functools
import math

import jax
import jax.numpy as jnp
from jax import lax
from jax.experimental import pallas as pl
from jax.experimental.pallas import tpu as pltpu
from jax.sharding import PartitionSpec as P

F32 = jnp.float32
BF16 = jnp.bfloat16
GROUP = ("tensor", "section")


def spread(value, axis, source):
    kept = jnp.where(lax.axis_index(axis) == source, value, 0).astype(value.dtype)
    return lax.psum(kept, axis)


def absorb_slot(mine_rows, root_rows, portion, col_first):
    highest = lax.Precision.HIGHEST
    row_count = mine_rows.shape[0]
    block_part = jnp.dot(mine_rows, portion.T, precision=highest)
    own_cols = lax.dynamic_slice_in_dim(portion, col_first, row_count, 1)
    right_gram = jnp.dot(own_cols.T, portion, precision=highest)
    left_prod = jnp.dot(root_rows, portion, precision=highest)
    return (block_part, right_gram, left_prod)


def apply_slot(prod_rows, portion):
    return jnp.dot(prod_rows, portion, precision=lax.Precision.HIGHEST)


def any_mesh(
    xin,
    dout,
    weights,
    slot_block,
    left_stat,
    right_stat,
    left_root,
    right_root,
    first_moment,
    second_moment,
):
    block_count, tok_count, block_size = xin.shape
    slot_count, row_count = (left_stat.shape[0], left_stat.shape[1])
    group_count = lax.axis_size(GROUP)
    shard_count = lax.axis_size("shard")
    factor = 1.0 / math.sqrt(tok_count * shard_count * group_count * block_size)
    pieces_out = []
    for grad_member in range(block_count):
        cols = xin[grad_member]
        pieces_out.append(
            jnp.einsum("tr,tc->rc", cols, dout[grad_member], preferred_element_type=jnp.float32)
        )
    partial_rows = lax.psum_scatter(
        jnp.concatenate(pieces_out, axis=1) * factor,
        GROUP,
        scatter_dimension=0,
        tiled=True,
    )
    grad_rows = lax.psum(partial_rows, "shard")
    shard_idx = lax.axis_index("shard")
    group_idx = lax.axis_index(GROUP)
    my_slots = lax.dynamic_slice_in_dim(slot_block, shard_idx * slot_count, slot_count)
    valid = my_slots >= 0
    picks = jnp.maximum(my_slots, 0)
    grad_three = grad_rows.reshape(row_count, block_count, block_size)
    mine = jnp.moveaxis(jnp.take(grad_three, picks, axis=1), 1, 0)
    col_first = group_idx * row_count
    zeros_rows = jnp.zeros((slot_count, row_count, block_size), jnp.float32)
    totals = (zeros_rows, zeros_rows, zeros_rows)
    portion = lax.all_gather(mine, GROUP, axis=1, tiled=True)
    lefts = []
    rights = []
    prods = []
    for slot_pos in range(slot_count):
        current = (totals[0][slot_pos], totals[1][slot_pos], totals[2][slot_pos])
        result = lax.cond(
            valid[slot_pos],
            lambda values: absorb_slot(
                mine[slot_pos], left_root[slot_pos], portion[slot_pos], col_first
            ),
            lambda values: values,
            current,
        )
        lefts.append(result[0])
        rights.append(result[1])
        prods.append(result[2])
    left_gram = jnp.stack(lefts)
    right_gram = jnp.stack(rights)
    left_prod = jnp.stack(prods)
    apply_portion = lax.all_gather(right_root, GROUP, axis=1, tiled=True)
    outputs = []
    for apply_slot_pos in range(slot_count):
        outputs.append(
            lax.cond(
                valid[apply_slot_pos],
                lambda values: apply_slot(left_prod[apply_slot_pos], apply_portion[apply_slot_pos]),
                lambda values: values,
                zeros_rows[apply_slot_pos],
            )
        )
    direction = jnp.stack(outputs)
    moment_one = 0.9 * first_moment + 0.1 * mine
    moment_two = 0.999 * second_moment + 0.001 * mine * mine
    adam = moment_one / (jnp.sqrt(moment_two) + 1e-08)
    adam_sq, dir_sq = lax.psum(
        (jnp.sum(adam * adam, axis=(1, 2)), jnp.sum(direction * direction, axis=(1, 2))),
        GROUP,
    )
    graft = jnp.sqrt(adam_sq) / (jnp.sqrt(dir_sq) + 1e-06)
    mask = valid[:, None, None]
    new_left = jnp.where(mask, 0.5 * left_stat + 0.5 * left_gram, left_stat)
    new_right = jnp.where(mask, 0.5 * right_stat + 0.5 * right_gram, right_stat)
    new_first = jnp.where(mask, moment_one, first_moment)
    new_second = jnp.where(mask, moment_two, second_moment)
    my_weights = jnp.take(weights, picks, axis=0)
    new_rows = (my_weights.astype(jnp.float32) - 0.05 * graft[:, None, None] * direction).astype(
        jnp.bfloat16
    )
    slot_ids = jnp.arange(slot_block.shape[0], dtype=jnp.int32)
    holders = [
        jnp.sum(slot_ids * (slot_block == member).astype(jnp.int32))
        for member in range(block_count)
    ]
    published = []
    for member in range(block_count):
        owner = holders[member] // slot_count
        within = holders[member] % slot_count
        chosen = lax.dynamic_index_in_dim(new_rows, within, 0, keepdims=False)
        published.append(spread(chosen, "shard", owner))
    new_weights = jnp.stack(published)
    return (new_weights, new_left, new_right, new_first, new_second)


def to_core(value):
    return lax.ppermute(value, "section", [(i, i ^ 1) for i in range(4)])


def to_x(value):
    return lax.ppermute(value, "section", [(i, i ^ 2) for i in range(4)])


def to_y(value):
    return lax.ppermute(value, "shard", [(0, 1), (1, 0)])


def to_z(value, bits):
    return lax.ppermute(value, "tensor", [(i, i ^ bits) for i in range(4)])


def row_dot(rows, full):
    return lax.dot_general(rows, full, (((1,), (0,)), ((), ())), preferred_element_type=F32)


def row_dot_t(rows, full):
    return lax.dot_general(rows, full, (((1,), (1,)), ((), ())), preferred_element_type=F32)


def token_dot(left, right):
    return lax.dot_general(left, right, (((0,), (0,)), ((), ())), preferred_element_type=F32)


def halves(value):
    high = value.astype(BF16)
    return high, (value - high.astype(F32)).astype(BF16)


def coded_rows(rows):
    return rows + rows // 3


def encode(value):
    rows = value.shape[0]
    part = rows // 4
    top = jnp.maximum(jnp.max(jnp.abs(value), axis=0, keepdims=True), 1e-30)
    exponent = jnp.ceil(jnp.log2(top))
    scaled = value * (jnp.exp2(-exponent) * 32760.0)
    coarse = jnp.round(scaled)
    fine = jnp.clip(jnp.floor((scaled - coarse) * 16.0), -8.0, 7.0) + 8.0
    words = fine[:part] - 32768.0
    for index in (1, 2, 3):
        words = words + fine[index * part : (index + 1) * part] * float(16**index)
    tail = jnp.broadcast_to(exponent, (rows // 3 - part, value.shape[1]))
    both = jnp.concatenate([coarse, words, tail], axis=0)
    return both.astype(jnp.int32).astype(jnp.int16)


def decode(words):
    rows = words.shape[0] // 4 * 3
    part = rows // 4
    wide = words.astype(jnp.int32)
    coarse = wide[:rows].astype(F32)
    fine = wide[rows : rows + part] + 32768
    exponent = wide[rows + part : rows + part + 8].astype(F32)[:1]
    parts = [(jnp.right_shift(fine, 4 * index) & 15).astype(F32) for index in range(4)]
    low = jnp.concatenate(parts, axis=0)
    return (coarse + (low - 7.5) * (1.0 / 16.0)) * (jnp.exp2(exponent) * (1.0 / 32760.0))


def used_slot(meta, plane, nth):
    seen = jnp.int32(0)
    place = jnp.int32(0)
    block = jnp.int32(0)
    for spot in range(4):
        entry = meta[4 * plane + spot]
        used = entry >= 0
        hit = jnp.logical_and(used, seen == nth)
        place = jnp.where(hit, spot, place)
        block = jnp.where(hit, entry, block)
        seen = seen + jnp.where(used, 1, 0)
    return place, block


SMEM_SPEC = pl.BlockSpec(memory_space=pltpu.SMEM)
VMEM_SPEC = pl.BlockSpec(memory_space=pltpu.VMEM)
HBM_SPEC = pl.BlockSpec(memory_space=pltpu.HBM)


def work(micros):
    return pl.CostEstimate(
        flops=int(micros * 10**6), transcendentals=0, bytes_accessed=int(micros * 3.6 * 10**6)
    )


def call(body, outs, ins, args, scratch=(), micros=1.0):
    return pl.pallas_call(
        body,
        out_shape=outs,
        in_specs=ins,
        out_specs=[VMEM_SPEC] * len(outs),
        cost_estimate=work(micros),
        scratch_shapes=list(scratch),
        compiler_params=pltpu.CompilerParams(vmem_limit_bytes=24 << 20),
    )(*args)


def start_copies(pairs, sems):
    copies = [
        pltpu.make_async_copy(source, target, sems.at[index])
        for index, (source, target) in enumerate(pairs)
    ]
    for copy in copies:
        copy.start()
    return copies


def in_parts(source, block, target, parts=4):
    span = target.shape[0] // parts
    rows = [pl.ds(part * span, span) for part in range(parts)]
    return [(source.at[block, part], target.at[part]) for part in rows]


def pick_far_kernel(meta, xin, dout, left, right, out, roots, sems):
    _, block = used_slot(meta, 1 - meta[8], 1 - meta[11])
    place, _ = used_slot(meta, meta[8], 1 - meta[11])
    pairs = in_parts(xin, block, out.at[0]) + in_parts(dout, block, out.at[1])
    pairs += [(left.at[place], roots.at[0]), (right.at[place], roots.at[1])]
    for copy in start_copies(pairs, sems):
        copy.wait()


def pick_mine_kernel(meta, xin, dout, out, sems):
    _, block = used_slot(meta, meta[8], 1 - meta[11])
    pairs = in_parts(xin, block, out.at[0]) + in_parts(dout, block, out.at[1])
    for copy in start_copies(pairs, sems):
        copy.wait()


def own_kernel(across, meta, xin, dout, out, taken, sems):
    plane = 1 - meta[8] if across else meta[8]
    _, block = used_slot(meta, plane, meta[11])
    pairs = in_parts(xin, block, taken.at[0]) + in_parts(dout, block, taken.at[1])
    copies = start_copies(pairs, sems)
    half = taken.shape[1] // 2
    for part in (0, 1):
        for index in (0, 1):
            copies[2 * part + index].wait()
            copies[4 + 2 * part + index].wait()
        rows = pl.ds(part * half, half)
        value = token_dot(taken[0, rows, :], taken[1, rows, :])
        out[...] = value if part == 0 else out[...] + value


def far_kernel(meta, got, own_ref, *refs):
    outs, total = refs[:4], refs[4]
    total[...] = own_ref[...] + token_dot(got[0], got[1])
    span = total.shape[0] // 4
    for out, bits in zip(outs, (3, 2, 1, 0)):
        first = pl.multiple_of((meta[9] ^ bits) * span, 64)
        out[...] = encode(total[pl.ds(first, span), :])


def mine_kernel(got, own_ref, out_ref):
    out_ref[...] = own_ref[...] + token_dot(got[0], got[1])


def rows_kernel(meta, left, right, got, left_out, right_out, whole, sems):
    core = meta[11]
    rows = got.shape[1]
    place, _ = used_slot(meta, meta[8], core)
    own = pl.ds(pl.multiple_of(core * rows, 16), rows)
    sib = pl.ds(pl.multiple_of((1 - core) * rows, 16), rows)
    pairs = [(left.at[place], left_out.at[own, :]), (right.at[place], whole.at[own, :])]
    copies = start_copies(pairs, sems)
    left_out[sib, :] = got[0]
    whole[sib, :] = got[1]
    for copy in copies:
        copy.wait()
    right_out[...] = encode(whole[...])


def y_kernel(meta, got, mine, coded, keep, both):
    rows = keep.shape[0]
    both[...] = decode(got[...]) + mine[...]
    side = meta[10]
    keep[...] = both[pl.ds(pl.multiple_of(side * rows, 32), rows), :]
    coded[...] = encode(both[pl.ds(pl.multiple_of((1 - side) * rows, 32), rows), :])


def after_y(meta, got, mine, bits):
    size = mine.shape[1]
    rows = size // 8
    return pl.pallas_call(
        y_kernel,
        out_shape=[
            jax.ShapeDtypeStruct((coded_rows(rows), size), jnp.int16),
            jax.ShapeDtypeStruct((rows, size), F32),
        ],
        grid_spec=pltpu.PrefetchScalarGridSpec(
            num_scalar_prefetch=1,
            grid=(1,),
            in_specs=[
                pl.BlockSpec(got.shape, lambda step, meta_ref: (0, 0)),
                pl.BlockSpec((2 * rows, size), lambda step, meta_ref: (meta_ref[9] ^ bits, 0)),
            ],
            out_specs=[
                pl.BlockSpec((coded_rows(rows), size), lambda step, meta_ref: (0, 0)),
                pl.BlockSpec((rows, size), lambda step, meta_ref: (0, 0)),
            ],
            scratch_shapes=[pltpu.VMEM((2 * rows, size), F32)],
        ),
        compiler_params=pltpu.CompilerParams(vmem_limit_bytes=24 << 20),
        cost_estimate=work(1.1),
    )(meta, got, mine)


def x_kernel(got, keep, coded):
    coded[...] = encode(decode(got[...]) + keep[...])


def grad_kernel(factor, got, keep, one, two, three, grad, coded):
    total = decode(got[...]) + keep[...]
    for part in (one, two, three):
        total = total + decode(part[...])
    total = total * factor
    grad[...] = total
    coded[...] = encode(total)


def put_rows(spot, value, high_ref, low_ref):
    rows = value.shape[0]
    first = pl.multiple_of(spot * rows, 32)
    high, low = halves(value)
    high_ref[pl.ds(first, rows), :] = high
    low_ref[pl.ds(first, rows), :] = low


def root_kernel(meta, *refs):
    for index in range(8):
        spot = 2 * (meta[9] ^ (index // 2)) + (meta[10] ^ (index % 2))
        put_rows(spot, decode(refs[index][...]), refs[8], refs[9])


def direction_kernel(meta, *refs):
    grad_ref, pieces = refs[0], refs[1:8]
    left_ref, root_high, root_low, adam_ref = refs[8:12]
    own_dir, sib_dir, sums, high_ref, low_ref, whole = refs[12:18]
    for index in range(8):
        spot = 2 * (meta[9] ^ (index // 2)) + (meta[10] ^ (index % 2))
        value = grad_ref[...] if index == 0 else decode(pieces[index - 1][...])
        put_rows(spot, value, high_ref, low_ref)
    half = left_ref.shape[0] // 2
    high, low = high_ref[...], low_ref[...]
    left_high, left_low = halves(left_ref[...])
    prod = row_dot(left_high, high) + (row_dot(left_low, high) + row_dot(left_high, low))
    prod_high, prod_low = halves(prod)
    root_h, root_l = root_high[...], root_low[...]
    direction = row_dot(prod_high, root_h) + (
        row_dot(prod_low, root_h) + row_dot(prod_high, root_l)
    )
    whole[...] = direction
    own_dir[...] = whole[pl.ds(pl.multiple_of(meta[11] * half, 16), half), :]
    sib_dir[...] = whole[pl.ds(pl.multiple_of((1 - meta[11]) * half, 16), half), :]
    lane = lax.broadcasted_iota(jnp.int32, (1, 128), 1)
    sums[...] = jnp.where(lane == 2, jnp.sum(direction * direction), adam_ref[...])


def gram_kernel(meta, grad_ref, high_ref, low_ref, own_left, own_right, sib_out, whole):
    rows, size = grad_ref.shape
    half = rows // 2
    own = pl.ds(pl.multiple_of(meta[11] * half, 16), half)
    sib = pl.ds(pl.multiple_of((1 - meta[11]) * half, 16), half)
    first = (2 * meta[9] + meta[10]) * rows
    high, low = high_ref[...], low_ref[...]
    own_high, own_low = halves(grad_ref[...])
    whole[...] = row_dot_t(own_high, high) + (
        row_dot_t(own_low, high) + row_dot_t(own_high, low)
    )
    own_left[...] = whole[own, :]
    sib_out[0] = whole[sib, :]
    row_ids = lax.broadcasted_iota(jnp.int32, (rows, size), 0) + first
    col_ids = lax.broadcasted_iota(jnp.int32, (rows, size), 1)
    pick = jnp.where(row_ids == col_ids, 1.0, 0.0).astype(BF16)
    col_high = row_dot_t(pick, high).astype(BF16)
    col_low = row_dot_t(pick, low).astype(BF16)
    whole[...] = row_dot(col_high, high) + (row_dot(col_low, high) + row_dot(col_high, low))
    own_right[...] = whole[own, :]
    sib_out[1] = whole[sib, :]


def moment_kernel(meta, grad, got, first, second, first_out, second_out, adam_out):
    plane, core = meta[8], meta[11]
    rows = got.shape[0]
    first_out[...] = first[...]
    second_out[...] = second[...]
    lane = lax.broadcasted_iota(jnp.int32, (1, 128), 1)
    line = jnp.zeros((1, 128), F32)
    own = grad[pl.ds(pl.multiple_of(core * rows, 16), rows), :]
    for slot, value in ((core, own), (1 - core, got[...])):
        place, _ = used_slot(meta, plane, slot)
        one = 0.9 * first[place] + 0.1 * value
        two = 0.999 * second[place] + 0.001 * value * value
        first_out[place] = one
        second_out[place] = two
        adam = one / (jnp.sqrt(two) + 1e-08)
        line = line + jnp.where(lane == slot, jnp.sum(adam * adam), 0.0)
    adam_out[...] = line


def weight_kernel(meta, sums, own_dir, sib_dir, weights, out):
    plane, core = meta[8], meta[11]
    lane = lax.broadcasted_iota(jnp.int32, (1, 128), 1)
    for slot, value in ((core, own_dir[...]), (1 - core, sib_dir[...])):
        line = jnp.zeros((1, 128), F32)
        for device in range(sums.shape[0]):
            kept = jnp.logical_or(lane == slot, jnp.logical_and(lane == 2, slot == device % 2))
            line = line + jnp.where(kept, sums[device], 0.0)
        dir_sq = jnp.sum(jnp.where(lane == 2, line, 0.0), axis=1, keepdims=True)
        adam_sq = jnp.sum(jnp.where(lane == 2, 0.0, line), axis=1, keepdims=True)
        graft = jnp.sqrt(adam_sq) / (jnp.sqrt(dir_sq) + 1e-06)
        _, block = used_slot(meta, plane, slot)
        out[slot] = (weights[block].astype(F32) - 0.05 * graft * value).astype(BF16)


def stat_kernel(meta, own_left, own_right, got, left, right, left_out, right_out):
    plane, core = meta[8], meta[11]
    left_out[...] = left[...]
    right_out[...] = right[...]
    for slot, left_gram, right_gram in (
        (core, own_left[...], own_right[...]),
        (1 - core, got[0], got[1]),
    ):
        place, _ = used_slot(meta, plane, slot)
        left_out[place] = 0.5 * left[place] + 0.5 * left_gram
        right_out[place] = 0.5 * right[place] + 0.5 * right_gram


def place_kernel(meta, near, mirror, out):
    plane = meta[8]
    for slot in (0, 1):
        _, block = used_slot(meta, plane, slot)
        out[block] = near[slot]
        _, block = used_slot(meta, 1 - plane, slot)
        out[block] = mirror[slot]


def two_planes(
    xin,
    dout,
    weights,
    slot_block,
    left_stat,
    right_stat,
    left_root,
    right_root,
    first_moment,
    second_moment,
):
    block_count, tokens, size = xin.shape
    slot_count, rows = left_stat.shape[:2]
    device_count = lax.axis_size(("shard",) + GROUP)
    factor = 1.0 / math.sqrt(tokens * device_count * size)
    section = lax.axis_index("section")
    meta = jnp.concatenate(
        [
            slot_block,
            jnp.stack(
                [lax.axis_index("shard"), lax.axis_index("tensor"), section // 2, section % 2]
            ).astype(jnp.int32),
        ]
    )

    def shape(*dims, dtype=F32):
        return jax.ShapeDtypeStruct(dims, dtype)

    words = jnp.int16
    tile = shape(rows, size)
    tokens_in = shape(2, tokens, size, dtype=BF16)
    piece = shape(coded_rows(2 * rows), size, dtype=words)

    def dmas(count):
        return pltpu.SemaphoreType.DMA((count,))

    xin, dout, left_root, right_root = (
        pltpu.with_memory_space_constraint(value, pltpu.HBM)
        for value in (xin, dout, left_root, right_root)
    )
    far_in, roots = call(
        pick_far_kernel,
        [tokens_in, shape(2, rows, size)],
        [SMEM_SPEC] + [HBM_SPEC] * 4,
        (meta, xin, dout, left_root, right_root),
        [dmas(10)],
    )
    roots = to_core(roots)
    far_in = to_core(far_in)
    def own_part(across, meta):
        return call(
            functools.partial(own_kernel, across),
            [shape(size, size)],
            [SMEM_SPEC] + [HBM_SPEC] * 2,
            (meta, xin, dout),
            [pltpu.VMEM((2, tokens, size), BF16), dmas(8)],
        )[0]

    own_far = own_part(True, meta)
    chunk = coded_rows(size // 4)
    coded = list(call(
        far_kernel,
        [shape(chunk, size, dtype=words)] * 4,
        [SMEM_SPEC] + [VMEM_SPEC] * 2,
        (meta, far_in, own_far),
        [pltpu.VMEM((size, size), F32)],
    ))
    coded[0], later, roots = lax.optimization_barrier((coded[0], meta, roots))
    got_y = [to_y(value) for value in coded]
    left_rows, right_coded = call(
        rows_kernel,
        [shape(2 * rows, size), piece],
        [SMEM_SPEC] + [HBM_SPEC] * 2 + [VMEM_SPEC],
        (meta, left_root, right_root, roots),
        [pltpu.VMEM((2 * rows, size), F32), dmas(2)],
    )
    root_z = [to_z(right_coded, bits) for bits in (1, 2, 3)]
    root_x = [to_x(right_coded)]
    (mine_in,) = call(
        pick_mine_kernel,
        [tokens_in],
        [SMEM_SPEC] + [HBM_SPEC] * 2,
        (later, xin, dout),
        [dmas(8)],
        2.1,
    )
    mine_in = to_core(mine_in)
    own_mine = own_part(False, later)
    (mine,) = call(
        mine_kernel,
        [shape(size, size)],
        [VMEM_SPEC] * 2,
        (mine_in, own_mine),
    )
    order = (3, 2, 1, 0)
    got_x, keeps, got_z = [], [], []
    for index, bits in enumerate(order):
        arrived = got_y[index]
        if index == 0:
            arrived, root_x[0], root_z[0] = lax.optimization_barrier(
                (arrived, root_x[0], root_z[0])
            )
            root_x.append(to_x(root_z[0]))
        if index == 1:
            arrived, got_x[0], root_x[1], *root_z[1:] = lax.optimization_barrier(
                (arrived, got_x[0], root_x[1], *root_z[1:])
            )
            root_x += [to_x(root_z[1]), to_x(root_z[2])]
        if index == 2:
            arrived, got_x[1], root_x[2] = lax.optimization_barrier(
                (arrived, got_x[1], root_x[2])
            )
        if index == 3:
            arrived, got_x[2], got_z[0], root_x[3] = lax.optimization_barrier(
                (arrived, got_x[2], got_z[0], root_x[3])
            )
        sent, keep = after_y(meta, arrived, mine, bits)
        got_x.append(to_x(sent))
        keeps.append(keep)
        if index:
            (sent,) = call(
                x_kernel, [piece], [VMEM_SPEC] * 2, (got_x[index - 1], keeps[index - 1])
            )
            got_z.append(to_z(sent, order[index - 1]))
    grad, coded = call(
        functools.partial(grad_kernel, factor),
        [shape(2 * rows, size), piece],
        [VMEM_SPEC] * 5,
        (got_x[3], keeps[3], *got_z),
    )

    column = [coded] + [to_z(coded, bits) for bits in (1, 2, 3)]
    pieces = []
    for part in column:
        pieces += [part, to_x(part)]

    root_pieces = [right_coded, root_x[0]]
    for near, across in zip(root_z, root_x[1:]):
        root_pieces += [near, across]
    root_high, root_low = call(
        root_kernel,
        [shape(size, size, dtype=BF16)] * 2,
        [SMEM_SPEC] + [VMEM_SPEC] * 8,
        (meta, *root_pieces),
    )

    core = section % 2
    grad_out = lax.dynamic_slice_in_dim(grad, (1 - core) * rows, rows, 0)
    stack = shape(slot_count, rows, size)
    new_first, new_second, adam = call(
        moment_kernel,
        [stack, stack, shape(1, 128)],
        [SMEM_SPEC] + [VMEM_SPEC] * 4,
        (meta, grad, to_core(grad_out), first_moment, second_moment),
    )
    own_dir, sib_dir, sums, high, low = call(
        direction_kernel,
        [tile, tile, shape(1, 128)] + [shape(size, size, dtype=BF16)] * 2,
        [SMEM_SPEC] + [VMEM_SPEC] * 12,
        (meta, grad, *pieces[1:], left_rows, root_high, root_low, adam),
        [pltpu.VMEM((2 * rows, size), F32)],
    )
    sib_dir = to_core(sib_dir)
    sums = jnp.broadcast_to(sums[None], (device_count // 2, 1, 128))
    sums = lax.all_to_all(sums, GROUP, 0, 0)
    (near,) = call(
        weight_kernel,
        [shape(2, rows, size, dtype=BF16)],
        [SMEM_SPEC] + [VMEM_SPEC] * 4,
        (meta, sums, own_dir, sib_dir, weights),
    )
    mirror = to_y(near)
    high, near = lax.optimization_barrier((high, near))
    own_left, own_right, sib_out = call(
        gram_kernel,
        [tile, tile, shape(2, rows, size)],
        [SMEM_SPEC] + [VMEM_SPEC] * 3,
        (meta, grad, high, low),
        [pltpu.VMEM((2 * rows, size), F32)],
        3.1,
    )
    new_left, new_right = call(
        stat_kernel,
        [stack, stack],
        [SMEM_SPEC] + [VMEM_SPEC] * 5,
        (meta, own_left, own_right, to_core(sib_out), left_stat, right_stat),
    )
    new_left, mirror = lax.optimization_barrier((new_left, mirror))
    (new_weights,) = call(
        place_kernel,
        [shape(block_count, rows, size, dtype=BF16)],
        [SMEM_SPEC] + [VMEM_SPEC] * 2,
        (meta, near, mirror),
    )
    return new_weights, new_left, new_right, new_first, new_second


def solution(mesh):
    placed = (
        P(None, ("shard", "tensor", "section"), None),
        P(None, ("shard", "tensor", "section"), None),
        P(None, ("tensor", "section"), None),
        P(),
        P("shard", ("tensor", "section"), None),
        P("shard", ("tensor", "section"), None),
        P("shard", ("tensor", "section"), None),
        P("shard", ("tensor", "section"), None),
        P("shard", ("tensor", "section"), None),
        P("shard", ("tensor", "section"), None),
    )
    shape = mesh.shape
    pair = (shape["shard"], shape["tensor"], shape["section"]) == (2, 4, 4)
    return jax.shard_map(
        two_planes if pair else any_mesh,
        mesh=mesh,
        in_specs=placed,
        out_specs=(
            P(None, ("tensor", "section"), None),
            P("shard", ("tensor", "section"), None),
            P("shard", ("tensor", "section"), None),
            P("shard", ("tensor", "section"), None),
            P("shard", ("tensor", "section"), None),
        ),
        check_vma=False,
    )
```

```python
import functools
import math

import jax
import jax.numpy as jnp
from jax import lax
from jax.experimental import pallas as pl
from jax.experimental.pallas import tpu as pltpu
from jax.sharding import PartitionSpec as P

F32 = jnp.float32
BF16 = jnp.bfloat16
GROUP = ("tensor", "section")


def spread(value, axis, source):
    kept = jnp.where(lax.axis_index(axis) == source, value, 0).astype(value.dtype)
    return lax.psum(kept, axis)


def absorb_slot(mine_rows, root_rows, portion, col_first):
    highest = lax.Precision.HIGHEST
    row_count = mine_rows.shape[0]
    block_part = jnp.dot(mine_rows, portion.T, precision=highest)
    own_cols = lax.dynamic_slice_in_dim(portion, col_first, row_count, 1)
    right_gram = jnp.dot(own_cols.T, portion, precision=highest)
    left_prod = jnp.dot(root_rows, portion, precision=highest)
    return (block_part, right_gram, left_prod)


def apply_slot(prod_rows, portion):
    return jnp.dot(prod_rows, portion, precision=lax.Precision.HIGHEST)


def any_mesh(
    xin,
    dout,
    weights,
    slot_block,
    left_stat,
    right_stat,
    left_root,
    right_root,
    first_moment,
    second_moment,
):
    block_count, tok_count, block_size = xin.shape
    slot_count, row_count = (left_stat.shape[0], left_stat.shape[1])
    group_count = lax.axis_size(GROUP)
    shard_count = lax.axis_size("shard")
    factor = 1.0 / math.sqrt(tok_count * shard_count * group_count * block_size)
    pieces_out = []
    for grad_member in range(block_count):
        cols = xin[grad_member]
        pieces_out.append(
            jnp.einsum("tr,tc->rc", cols, dout[grad_member], preferred_element_type=jnp.float32)
        )
    partial_rows = lax.psum_scatter(
        jnp.concatenate(pieces_out, axis=1) * factor,
        GROUP,
        scatter_dimension=0,
        tiled=True,
    )
    grad_rows = lax.psum(partial_rows, "shard")
    shard_idx = lax.axis_index("shard")
    group_idx = lax.axis_index(GROUP)
    my_slots = lax.dynamic_slice_in_dim(slot_block, shard_idx * slot_count, slot_count)
    valid = my_slots >= 0
    picks = jnp.maximum(my_slots, 0)
    grad_three = grad_rows.reshape(row_count, block_count, block_size)
    mine = jnp.moveaxis(jnp.take(grad_three, picks, axis=1), 1, 0)
    col_first = group_idx * row_count
    zeros_rows = jnp.zeros((slot_count, row_count, block_size), jnp.float32)
    totals = (zeros_rows, zeros_rows, zeros_rows)
    portion = lax.all_gather(mine, GROUP, axis=1, tiled=True)
    lefts = []
    rights = []
    prods = []
    for slot_pos in range(slot_count):
        current = (totals[0][slot_pos], totals[1][slot_pos], totals[2][slot_pos])
        result = lax.cond(
            valid[slot_pos],
            lambda values: absorb_slot(
                mine[slot_pos], left_root[slot_pos], portion[slot_pos], col_first
            ),
            lambda values: values,
            current,
        )
        lefts.append(result[0])
        rights.append(result[1])
        prods.append(result[2])
    left_gram = jnp.stack(lefts)
    right_gram = jnp.stack(rights)
    left_prod = jnp.stack(prods)
    apply_portion = lax.all_gather(right_root, GROUP, axis=1, tiled=True)
    outputs = []
    for apply_slot_pos in range(slot_count):
        outputs.append(
            lax.cond(
                valid[apply_slot_pos],
                lambda values: apply_slot(left_prod[apply_slot_pos], apply_portion[apply_slot_pos]),
                lambda values: values,
                zeros_rows[apply_slot_pos],
            )
        )
    direction = jnp.stack(outputs)
    moment_one = 0.9 * first_moment + 0.1 * mine
    moment_two = 0.999 * second_moment + 0.001 * mine * mine
    adam = moment_one / (jnp.sqrt(moment_two) + 1e-08)
    adam_sq, dir_sq = lax.psum(
        (jnp.sum(adam * adam, axis=(1, 2)), jnp.sum(direction * direction, axis=(1, 2))),
        GROUP,
    )
    graft = jnp.sqrt(adam_sq) / (jnp.sqrt(dir_sq) + 1e-06)
    mask = valid[:, None, None]
    new_left = jnp.where(mask, 0.5 * left_stat + 0.5 * left_gram, left_stat)
    new_right = jnp.where(mask, 0.5 * right_stat + 0.5 * right_gram, right_stat)
    new_first = jnp.where(mask, moment_one, first_moment)
    new_second = jnp.where(mask, moment_two, second_moment)
    my_weights = jnp.take(weights, picks, axis=0)
    new_rows = (my_weights.astype(jnp.float32) - 0.05 * graft[:, None, None] * direction).astype(
        jnp.bfloat16
    )
    slot_ids = jnp.arange(slot_block.shape[0], dtype=jnp.int32)
    holders = [
        jnp.sum(slot_ids * (slot_block == member).astype(jnp.int32))
        for member in range(block_count)
    ]
    published = []
    for member in range(block_count):
        owner = holders[member] // slot_count
        within = holders[member] % slot_count
        chosen = lax.dynamic_index_in_dim(new_rows, within, 0, keepdims=False)
        published.append(spread(chosen, "shard", owner))
    new_weights = jnp.stack(published)
    return (new_weights, new_left, new_right, new_first, new_second)


def to_core(value):
    return lax.ppermute(value, "section", [(i, i ^ 1) for i in range(4)])


def to_x(value):
    return lax.ppermute(value, "section", [(i, i ^ 2) for i in range(4)])


def to_y(value):
    return lax.ppermute(value, "shard", [(0, 1), (1, 0)])


def to_z(value, bits):
    return lax.ppermute(value, "tensor", [(i, i ^ bits) for i in range(4)])


def row_dot(rows, full):
    return lax.dot_general(rows, full, (((1,), (0,)), ((), ())), preferred_element_type=F32)


def row_dot_t(rows, full):
    return lax.dot_general(rows, full, (((1,), (1,)), ((), ())), preferred_element_type=F32)


def token_dot(left, right):
    return lax.dot_general(left, right, (((0,), (0,)), ((), ())), preferred_element_type=F32)


def halves(value):
    high = value.astype(BF16)
    return high, (value - high.astype(F32)).astype(BF16)


def coded_rows(rows):
    return rows + rows // 3


def encode(value):
    rows = value.shape[0]
    part = rows // 4
    top = jnp.maximum(jnp.max(jnp.abs(value), axis=0, keepdims=True), 1e-30)
    exponent = jnp.ceil(jnp.log2(top))
    scaled = value * (jnp.exp2(-exponent) * 32760.0)
    coarse = jnp.round(scaled)
    fine = jnp.clip(jnp.floor((scaled - coarse) * 16.0), -8.0, 7.0) + 8.0
    words = fine[:part] - 32768.0
    for index in (1, 2, 3):
        words = words + fine[index * part : (index + 1) * part] * float(16**index)
    tail = jnp.broadcast_to(exponent, (rows // 3 - part, value.shape[1]))
    both = jnp.concatenate([coarse, words, tail], axis=0)
    return both.astype(jnp.int32).astype(jnp.int16)


def decode(words):
    rows = words.shape[0] // 4 * 3
    part = rows // 4
    wide = words.astype(jnp.int32)
    coarse = wide[:rows].astype(F32)
    fine = wide[rows : rows + part] + 32768
    exponent = wide[rows + part : rows + part + 8].astype(F32)[:1]
    parts = [(jnp.right_shift(fine, 4 * index) & 15).astype(F32) for index in range(4)]
    low = jnp.concatenate(parts, axis=0)
    return (coarse + (low - 7.5) * (1.0 / 16.0)) * (jnp.exp2(exponent) * (1.0 / 32760.0))


def used_slot(meta, plane, nth):
    seen = jnp.int32(0)
    place = jnp.int32(0)
    block = jnp.int32(0)
    for spot in range(4):
        entry = meta[4 * plane + spot]
        used = entry >= 0
        hit = jnp.logical_and(used, seen == nth)
        place = jnp.where(hit, spot, place)
        block = jnp.where(hit, entry, block)
        seen = seen + jnp.where(used, 1, 0)
    return place, block


ORDER = (2, 3, 1, 0)


SMEM_SPEC = pl.BlockSpec(memory_space=pltpu.SMEM)
VMEM_SPEC = pl.BlockSpec(memory_space=pltpu.VMEM)
HBM_SPEC = pl.BlockSpec(memory_space=pltpu.HBM)


def work(micros):
    return pl.CostEstimate(
        flops=int(micros * 10**9), transcendentals=0, bytes_accessed=int(micros * 36 * 10**6)
    )


def call(body, outs, ins, args, scratch=(), micros=1.0):
    return pl.pallas_call(
        body,
        out_shape=outs,
        in_specs=ins,
        out_specs=[VMEM_SPEC] * len(outs),
        cost_estimate=work(micros),
        scratch_shapes=list(scratch),
        compiler_params=pltpu.CompilerParams(vmem_limit_bytes=24 << 20),
    )(*args)


def start_copies(pairs, sems):
    copies = [
        pltpu.make_async_copy(source, target, sems.at[index])
        for index, (source, target) in enumerate(pairs)
    ]
    for copy in copies:
        copy.start()
    return copies


def in_parts(source, block, target, parts=4):
    span = target.shape[0] // parts
    rows = [pl.ds(part * span, span) for part in range(parts)]
    return [(source.at[block, part], target.at[part]) for part in rows]


def pick_kernel(meta, xin, dout, left, right, far, mine, roots, sems):
    _, block = used_slot(meta, 1 - meta[8], 1 - meta[11])
    pairs = in_parts(xin, block, far.at[0]) + in_parts(dout, block, far.at[1])
    place, block = used_slot(meta, meta[8], 1 - meta[11])
    pairs += [(left.at[place], roots.at[0]), (right.at[place], roots.at[1])]
    pairs += in_parts(xin, block, mine.at[0]) + in_parts(dout, block, mine.at[1])
    for copy in start_copies(pairs, sems):
        copy.wait()


def own_kernel(across, meta, xin, dout, out, taken, sems):
    plane = 1 - meta[8] if across else meta[8]
    _, block = used_slot(meta, plane, meta[11])
    pairs = in_parts(xin, block, taken.at[0]) + in_parts(dout, block, taken.at[1])
    copies = start_copies(pairs, sems)
    half = taken.shape[1] // 2
    for part in (0, 1):
        for index in (0, 1):
            copies[2 * part + index].wait()
            copies[4 + 2 * part + index].wait()
        rows = pl.ds(part * half, half)
        value = token_dot(taken[0, rows, :], taken[1, rows, :])
        out[...] = value if part == 0 else out[...] + value


def far_kernel(meta, got, own_ref, *refs):
    outs, total = refs[:4], refs[4]
    total[...] = own_ref[...] + token_dot(got[0], got[1])
    span = total.shape[0] // 4
    for out, bits in zip(outs, ORDER):
        first = pl.multiple_of((meta[9] ^ bits) * span, 64)
        out[...] = encode(total[pl.ds(first, span), :])


def mine_kernel(got, own_ref, out_ref):
    out_ref[...] = own_ref[...] + token_dot(got[0], got[1])


def rows_kernel(meta, left, right, got, left_out, right_out, whole, sems):
    core = meta[11]
    rows = got.shape[1]
    place, _ = used_slot(meta, meta[8], core)
    own = pl.ds(pl.multiple_of(core * rows, 16), rows)
    sib = pl.ds(pl.multiple_of((1 - core) * rows, 16), rows)
    pairs = [(left.at[place], left_out.at[own, :]), (right.at[place], whole.at[own, :])]
    copies = start_copies(pairs, sems)
    left_out[sib, :] = got[0]
    whole[sib, :] = got[1]
    for copy in copies:
        copy.wait()
    right_out[...] = encode(whole[...])


def y_kernel(meta, got, mine, coded, keep, both):
    rows = keep.shape[0]
    both[...] = decode(got[...]) + mine[...]
    side = meta[10]
    keep[...] = both[pl.ds(pl.multiple_of(side * rows, 32), rows), :]
    coded[...] = encode(both[pl.ds(pl.multiple_of((1 - side) * rows, 32), rows), :])


def after_y(meta, got, mine, bits):
    size = mine.shape[1]
    rows = size // 8
    return pl.pallas_call(
        y_kernel,
        out_shape=[
            jax.ShapeDtypeStruct((coded_rows(rows), size), jnp.int16),
            jax.ShapeDtypeStruct((rows, size), F32),
        ],
        grid_spec=pltpu.PrefetchScalarGridSpec(
            num_scalar_prefetch=1,
            grid=(1,),
            in_specs=[
                pl.BlockSpec(got.shape, lambda step, meta_ref: (0, 0)),
                pl.BlockSpec((2 * rows, size), lambda step, meta_ref: (meta_ref[9] ^ bits, 0)),
            ],
            out_specs=[
                pl.BlockSpec((coded_rows(rows), size), lambda step, meta_ref: (0, 0)),
                pl.BlockSpec((rows, size), lambda step, meta_ref: (0, 0)),
            ],
            scratch_shapes=[pltpu.VMEM((2 * rows, size), F32)],
        ),
        compiler_params=pltpu.CompilerParams(vmem_limit_bytes=24 << 20),
        cost_estimate=work(1.1),
    )(meta, got, mine)


def x_kernel(keep, *refs):
    total = keep[...]
    for part in refs[:-1]:
        total = total + decode(part[...])
    refs[-1][...] = encode(total)


def grad_kernel(factor, keep, got, far, near, grad, coded):
    total = keep[...]
    for part in (got, far, near):
        total = total + decode(part[...])
    total = total * factor
    grad[...] = total
    coded[...] = encode(total)


def put_rows(spot, value, high_ref, low_ref):
    rows = value.shape[0]
    first = pl.multiple_of(spot * rows, 32)
    high, low = halves(value)
    high_ref[pl.ds(first, rows), :] = high
    low_ref[pl.ds(first, rows), :] = low


def root_kernel(meta, *refs):
    for index in range(8):
        spot = 2 * (meta[9] ^ (index // 2)) + (meta[10] ^ (index % 2))
        put_rows(spot, decode(refs[index][...]), refs[8], refs[9])


def direction_kernel(meta, *refs):
    grad_ref, pieces = refs[0], refs[1:8]
    left_ref, root_high, root_low, adam_ref = refs[8:12]
    own_dir, sib_dir, sums, high_ref, low_ref, whole = refs[12:18]
    for index in range(8):
        spot = 2 * (meta[9] ^ (index // 2)) + (meta[10] ^ (index % 2))
        value = grad_ref[...] if index == 0 else decode(pieces[index - 1][...])
        put_rows(spot, value, high_ref, low_ref)
    half = left_ref.shape[0] // 2
    high, low = high_ref[...], low_ref[...]
    left_high, left_low = halves(left_ref[...])
    prod = row_dot(left_high, high) + (row_dot(left_low, high) + row_dot(left_high, low))
    prod_high, prod_low = halves(prod)
    root_h, root_l = root_high[...], root_low[...]
    direction = row_dot(prod_high, root_h) + (
        row_dot(prod_low, root_h) + row_dot(prod_high, root_l)
    )
    whole[...] = direction
    own_dir[...] = whole[pl.ds(pl.multiple_of(meta[11] * half, 16), half), :]
    sib_dir[...] = whole[pl.ds(pl.multiple_of((1 - meta[11]) * half, 16), half), :]
    lane = lax.broadcasted_iota(jnp.int32, (1, 128), 1)
    sums[...] = jnp.where(lane == 2, jnp.sum(direction * direction), adam_ref[...])


def left_kernel(meta, grad_ref, high_ref, low_ref, own_out, sib_out, whole):
    half = own_out.shape[0]
    high, low = high_ref[...], low_ref[...]
    own_high, own_low = halves(grad_ref[...])
    whole[...] = row_dot_t(own_high, high) + (
        row_dot_t(own_low, high) + row_dot_t(own_high, low)
    )
    own_out[...] = whole[pl.ds(pl.multiple_of(meta[11] * half, 16), half), :]
    sib_out[...] = whole[pl.ds(pl.multiple_of((1 - meta[11]) * half, 16), half), :]


def right_kernel(meta, high_ref, low_ref, own_out, sib_out, whole):
    half, size = own_out.shape
    rows = 2 * half
    first = (2 * meta[9] + meta[10]) * rows
    high, low = high_ref[...], low_ref[...]
    row_ids = lax.broadcasted_iota(jnp.int32, (rows, size), 0) + first
    col_ids = lax.broadcasted_iota(jnp.int32, (rows, size), 1)
    pick = jnp.where(row_ids == col_ids, 1.0, 0.0).astype(BF16)
    col_high = row_dot_t(pick, high).astype(BF16)
    col_low = row_dot_t(pick, low).astype(BF16)
    whole[...] = row_dot(col_high, high) + (row_dot(col_low, high) + row_dot(col_high, low))
    own_out[...] = whole[pl.ds(pl.multiple_of(meta[11] * half, 16), half), :]
    sib_out[...] = whole[pl.ds(pl.multiple_of((1 - meta[11]) * half, 16), half), :]


def moment_kernel(meta, grad, got, first, second, first_out, second_out, adam_out):
    plane, core = meta[8], meta[11]
    rows = got.shape[0]
    first_out[...] = first[...]
    second_out[...] = second[...]
    lane = lax.broadcasted_iota(jnp.int32, (1, 128), 1)
    line = jnp.zeros((1, 128), F32)
    own = grad[pl.ds(pl.multiple_of(core * rows, 16), rows), :]
    for slot, value in ((core, own), (1 - core, got[...])):
        place, _ = used_slot(meta, plane, slot)
        one = 0.9 * first[place] + 0.1 * value
        two = 0.999 * second[place] + 0.001 * value * value
        first_out[place] = one
        second_out[place] = two
        adam = one / (jnp.sqrt(two) + 1e-08)
        line = line + jnp.where(lane == slot, jnp.sum(adam * adam), 0.0)
    adam_out[...] = line


def weight_kernel(meta, sums, own_dir, sib_dir, weights, out):
    plane, core = meta[8], meta[11]
    lane = lax.broadcasted_iota(jnp.int32, (1, 128), 1)
    for slot, value in ((core, own_dir[...]), (1 - core, sib_dir[...])):
        line = jnp.zeros((1, 128), F32)
        for device in range(sums.shape[0]):
            kept = jnp.logical_or(lane == slot, jnp.logical_and(lane == 2, slot == device % 2))
            line = line + jnp.where(kept, sums[device], 0.0)
        dir_sq = jnp.sum(jnp.where(lane == 2, line, 0.0), axis=1, keepdims=True)
        adam_sq = jnp.sum(jnp.where(lane == 2, 0.0, line), axis=1, keepdims=True)
        graft = jnp.sqrt(adam_sq) / (jnp.sqrt(dir_sq) + 1e-06)
        _, block = used_slot(meta, plane, slot)
        out[slot] = (weights[block].astype(F32) - 0.05 * graft * value).astype(BF16)


def stat_kernel(meta, own, got, stat, out):
    out[...] = stat[...]
    for slot, gram in ((meta[11], own), (1 - meta[11], got)):
        place, _ = used_slot(meta, meta[8], slot)
        out[place] = 0.5 * stat[place] + 0.5 * gram[...]


def place_kernel(meta, near, mirror, out):
    plane = meta[8]
    for slot in (0, 1):
        _, block = used_slot(meta, plane, slot)
        out[block] = near[slot]
        _, block = used_slot(meta, 1 - plane, slot)
        out[block] = mirror[slot]


def two_planes(
    xin,
    dout,
    weights,
    slot_block,
    left_stat,
    right_stat,
    left_root,
    right_root,
    first_moment,
    second_moment,
):
    block_count, tokens, size = xin.shape
    slot_count, rows = left_stat.shape[:2]
    device_count = lax.axis_size(("shard",) + GROUP)
    factor = 1.0 / math.sqrt(tokens * device_count * size)
    section = lax.axis_index("section")
    meta = jnp.concatenate(
        [
            slot_block,
            jnp.stack(
                [lax.axis_index("shard"), lax.axis_index("tensor"), section // 2, section % 2]
            ).astype(jnp.int32),
        ]
    )

    def shape(*dims, dtype=F32):
        return jax.ShapeDtypeStruct(dims, dtype)

    words = jnp.int16
    tile = shape(rows, size)
    tokens_in = shape(2, tokens, size, dtype=BF16)
    piece = shape(coded_rows(2 * rows), size, dtype=words)

    def dmas(count):
        return pltpu.SemaphoreType.DMA((count,))

    xin, dout, left_root, right_root = (
        pltpu.with_memory_space_constraint(value, pltpu.HBM)
        for value in (xin, dout, left_root, right_root)
    )
    far_in, mine_in, roots = call(
        pick_kernel,
        [tokens_in, tokens_in, shape(2, rows, size)],
        [SMEM_SPEC] + [HBM_SPEC] * 4,
        (meta, xin, dout, left_root, right_root),
        [dmas(18)],
    )
    roots = to_core(roots)
    far_in = to_core(far_in)
    mine_in = to_core(mine_in)
    def own_part(across, meta):
        return call(
            functools.partial(own_kernel, across),
            [shape(size, size)],
            [SMEM_SPEC] + [HBM_SPEC] * 2,
            (meta, xin, dout),
            [pltpu.VMEM((2, tokens, size), BF16), dmas(8)],
        )[0]

    own_far = own_part(True, meta)
    chunk = coded_rows(size // 4)
    coded = list(call(
        far_kernel,
        [shape(chunk, size, dtype=words)] * 4,
        [SMEM_SPEC] + [VMEM_SPEC] * 2,
        (meta, far_in, own_far),
        [pltpu.VMEM((size, size), F32)],
    ))
    coded[0], roots = lax.optimization_barrier((coded[0], roots))
    got_y = [to_y(value) for value in coded]
    left_rows, right_coded = call(
        rows_kernel,
        [shape(2 * rows, size), piece],
        [SMEM_SPEC] + [HBM_SPEC] * 2 + [VMEM_SPEC],
        (meta, left_root, right_root, roots),
        [pltpu.VMEM((2 * rows, size), F32), dmas(2)],
    )
    own_mine = own_part(False, meta)
    root_z = {3: to_z(right_coded, 3), 1: to_z(right_coded, 1)}
    mine_in, sent = lax.optimization_barrier((mine_in, right_coded))
    root_x = {0: to_x(sent)}
    sent, root_z[1] = lax.optimization_barrier((root_z[3], root_z[1]))
    root_z[2] = to_z(sent, 1)
    sent, root_x[0] = lax.optimization_barrier((root_z[1], root_x[0]))
    root_x[1] = to_x(sent)

    (mine,) = call(
        mine_kernel,
        [shape(size, size)],
        [VMEM_SPEC] * 2,
        (mine_in, own_mine),
    )
    got_x, keeps, got_z = [], [], []
    for index, bits in enumerate(ORDER):
        arrived = got_y[index]
        if index == 1:
            arrived, got_x[0], root_x[0], root_z[3] = lax.optimization_barrier(
                (arrived, got_x[0], root_x[0], root_z[3])
            )
            root_x[3] = to_x(root_z[3])
        if index == 2:
            arrived, got_x[1], root_x[1], root_z[2] = lax.optimization_barrier(
                (arrived, got_x[1], root_x[1], root_z[2])
            )
        if index == 3:
            arrived, got_x[2], root_x[3] = lax.optimization_barrier(
                (arrived, got_x[2], root_x[3])
            )
        sent, keep = after_y(meta, arrived, mine, bits)
        got_x.append(to_x(sent))
        keeps.append(keep)
        if index:
            carried = got_z if index == 2 else []
            (sent,) = call(
                x_kernel,
                [piece],
                [VMEM_SPEC] * (2 + len(carried)),
                (keeps[index - 1], got_x[index - 1], *carried),
            )
            got_z.append(to_z(sent, (1, 3, 1)[index - 1]))
    grad, coded = call(
        functools.partial(grad_kernel, factor),
        [shape(2 * rows, size), piece],
        [VMEM_SPEC] * 4,
        (keeps[3], got_x[3], got_z[1], got_z[2]),
    )

    across = {0: to_x(coded)}
    column = {bits: to_z(coded, bits) for bits in (1, 2, 3)}
    coded, sent = lax.optimization_barrier((coded, root_z[2]))
    root_x[2] = to_x(sent)
    column[1], across[0] = lax.optimization_barrier((column[1], across[0]))
    for bits in (1, 2, 3):
        across[bits] = to_x(column[bits])
    pieces = [across[0]]
    for bits in (1, 2, 3):
        pieces += [column[bits], across[bits]]

    root_z[0] = right_coded
    root_pieces = []
    for index in range(4):
        root_pieces += [root_z[index], root_x[index]]
    root_high, root_low = call(
        root_kernel,
        [shape(size, size, dtype=BF16)] * 2,
        [SMEM_SPEC] + [VMEM_SPEC] * 8,
        (meta, *root_pieces),
    )

    core = section % 2
    grad_out = lax.dynamic_slice_in_dim(grad, (1 - core) * rows, rows, 0)
    stack = shape(slot_count, rows, size)
    new_first, new_second, adam = call(
        moment_kernel,
        [stack, stack, shape(1, 128)],
        [SMEM_SPEC] + [VMEM_SPEC] * 4,
        (meta, grad, to_core(grad_out), first_moment, second_moment),
    )
    own_dir, sib_dir, sums, high, low = call(
        direction_kernel,
        [tile, tile, shape(1, 128)] + [shape(size, size, dtype=BF16)] * 2,
        [SMEM_SPEC] + [VMEM_SPEC] * 12,
        (meta, grad, *pieces, left_rows, root_high, root_low, adam),
        [pltpu.VMEM((2 * rows, size), F32)],
    )
    sib_dir = to_core(sib_dir)
    sums = jnp.broadcast_to(sums[None], (device_count // 2, 1, 128))
    sums = lax.all_to_all(sums, GROUP, 0, 0)
    (near,) = call(
        weight_kernel,
        [shape(2, rows, size, dtype=BF16)],
        [SMEM_SPEC] + [VMEM_SPEC] * 4,
        (meta, sums, own_dir, sib_dir, weights),
    )
    mirror = to_y(near)
    high, near = lax.optimization_barrier((high, near))
    whole = [pltpu.VMEM((2 * rows, size), F32)]
    own_right, sib_right = call(
        right_kernel,
        [tile, tile],
        [SMEM_SPEC] + [VMEM_SPEC] * 2,
        (meta, high, low),
        whole,
        1.8,
    )
    got_right = to_core(sib_right)
    own_left, sib_left = call(
        left_kernel,
        [tile, tile],
        [SMEM_SPEC] + [VMEM_SPEC] * 3,
        (meta, grad, high, low),
        whole,
        1.4,
    )
    got_left = to_core(sib_left)
    (new_weights,) = call(
        place_kernel,
        [shape(block_count, rows, size, dtype=BF16)],
        [SMEM_SPEC] + [VMEM_SPEC] * 2,
        (meta, near, mirror),
    )

    def update(own, got, stat):
        return call(
            stat_kernel, [stack], [SMEM_SPEC] + [VMEM_SPEC] * 3, (meta, own, got, stat), (), 1.0
        )[0]

    new_right = update(own_right, got_right, right_stat)
    new_left = update(own_left, got_left, left_stat)
    return new_weights, new_left, new_right, new_first, new_second


def solution(mesh):
    placed = (
        P(None, ("shard", "tensor", "section"), None),
        P(None, ("shard", "tensor", "section"), None),
        P(None, ("tensor", "section"), None),
        P(),
        P("shard", ("tensor", "section"), None),
        P("shard", ("tensor", "section"), None),
        P("shard", ("tensor", "section"), None),
        P("shard", ("tensor", "section"), None),
        P("shard", ("tensor", "section"), None),
        P("shard", ("tensor", "section"), None),
    )
    shape = mesh.shape
    pair = (shape["shard"], shape["tensor"], shape["section"]) == (2, 4, 4)
    return jax.shard_map(
        two_planes if pair else any_mesh,
        mesh=mesh,
        in_specs=placed,
        out_specs=(
            P(None, ("tensor", "section"), None),
            P("shard", ("tensor", "section"), None),
            P("shard", ("tensor", "section"), None),
            P("shard", ("tensor", "section"), None),
            P("shard", ("tensor", "section"), None),
        ),
        check_vma=False,
    )
```

```python
import functools
import math

import jax
import jax.numpy as jnp
from jax import lax
from jax.experimental import pallas as pl
from jax.experimental.pallas import tpu as pltpu
from jax.sharding import PartitionSpec as P

F32 = jnp.float32
BF16 = jnp.bfloat16
GROUP = ("tensor", "section")


def spread(value, axis, source):
    kept = jnp.where(lax.axis_index(axis) == source, value, 0).astype(value.dtype)
    return lax.psum(kept, axis)


def absorb_slot(mine_rows, root_rows, portion, col_first):
    highest = lax.Precision.HIGHEST
    row_count = mine_rows.shape[0]
    block_part = jnp.dot(mine_rows, portion.T, precision=highest)
    own_cols = lax.dynamic_slice_in_dim(portion, col_first, row_count, 1)
    right_gram = jnp.dot(own_cols.T, portion, precision=highest)
    left_prod = jnp.dot(root_rows, portion, precision=highest)
    return (block_part, right_gram, left_prod)


def apply_slot(prod_rows, portion):
    return jnp.dot(prod_rows, portion, precision=lax.Precision.HIGHEST)


def any_mesh(
    xin,
    dout,
    weights,
    slot_block,
    left_stat,
    right_stat,
    left_root,
    right_root,
    first_moment,
    second_moment,
):
    block_count, tok_count, block_size = xin.shape
    slot_count, row_count = (left_stat.shape[0], left_stat.shape[1])
    group_count = lax.axis_size(GROUP)
    shard_count = lax.axis_size("shard")
    factor = 1.0 / math.sqrt(tok_count * shard_count * group_count * block_size)
    pieces_out = []
    for grad_member in range(block_count):
        cols = xin[grad_member]
        pieces_out.append(
            jnp.einsum("tr,tc->rc", cols, dout[grad_member], preferred_element_type=jnp.float32)
        )
    partial_rows = lax.psum_scatter(
        jnp.concatenate(pieces_out, axis=1) * factor,
        GROUP,
        scatter_dimension=0,
        tiled=True,
    )
    grad_rows = lax.psum(partial_rows, "shard")
    shard_idx = lax.axis_index("shard")
    group_idx = lax.axis_index(GROUP)
    my_slots = lax.dynamic_slice_in_dim(slot_block, shard_idx * slot_count, slot_count)
    valid = my_slots >= 0
    picks = jnp.maximum(my_slots, 0)
    grad_three = grad_rows.reshape(row_count, block_count, block_size)
    mine = jnp.moveaxis(jnp.take(grad_three, picks, axis=1), 1, 0)
    col_first = group_idx * row_count
    zeros_rows = jnp.zeros((slot_count, row_count, block_size), jnp.float32)
    totals = (zeros_rows, zeros_rows, zeros_rows)
    portion = lax.all_gather(mine, GROUP, axis=1, tiled=True)
    lefts = []
    rights = []
    prods = []
    for slot_pos in range(slot_count):
        current = (totals[0][slot_pos], totals[1][slot_pos], totals[2][slot_pos])
        result = lax.cond(
            valid[slot_pos],
            lambda values: absorb_slot(
                mine[slot_pos], left_root[slot_pos], portion[slot_pos], col_first
            ),
            lambda values: values,
            current,
        )
        lefts.append(result[0])
        rights.append(result[1])
        prods.append(result[2])
    left_gram = jnp.stack(lefts)
    right_gram = jnp.stack(rights)
    left_prod = jnp.stack(prods)
    apply_portion = lax.all_gather(right_root, GROUP, axis=1, tiled=True)
    outputs = []
    for apply_slot_pos in range(slot_count):
        outputs.append(
            lax.cond(
                valid[apply_slot_pos],
                lambda values: apply_slot(left_prod[apply_slot_pos], apply_portion[apply_slot_pos]),
                lambda values: values,
                zeros_rows[apply_slot_pos],
            )
        )
    direction = jnp.stack(outputs)
    moment_one = 0.9 * first_moment + 0.1 * mine
    moment_two = 0.999 * second_moment + 0.001 * mine * mine
    adam = moment_one / (jnp.sqrt(moment_two) + 1e-08)
    adam_sq, dir_sq = lax.psum(
        (jnp.sum(adam * adam, axis=(1, 2)), jnp.sum(direction * direction, axis=(1, 2))),
        GROUP,
    )
    graft = jnp.sqrt(adam_sq) / (jnp.sqrt(dir_sq) + 1e-06)
    mask = valid[:, None, None]
    new_left = jnp.where(mask, 0.5 * left_stat + 0.5 * left_gram, left_stat)
    new_right = jnp.where(mask, 0.5 * right_stat + 0.5 * right_gram, right_stat)
    new_first = jnp.where(mask, moment_one, first_moment)
    new_second = jnp.where(mask, moment_two, second_moment)
    my_weights = jnp.take(weights, picks, axis=0)
    new_rows = (my_weights.astype(jnp.float32) - 0.05 * graft[:, None, None] * direction).astype(
        jnp.bfloat16
    )
    slot_ids = jnp.arange(slot_block.shape[0], dtype=jnp.int32)
    holders = [
        jnp.sum(slot_ids * (slot_block == member).astype(jnp.int32))
        for member in range(block_count)
    ]
    published = []
    for member in range(block_count):
        owner = holders[member] // slot_count
        within = holders[member] % slot_count
        chosen = lax.dynamic_index_in_dim(new_rows, within, 0, keepdims=False)
        published.append(spread(chosen, "shard", owner))
    new_weights = jnp.stack(published)
    return (new_weights, new_left, new_right, new_first, new_second)


def to_core(value):
    return lax.ppermute(value, "section", [(i, i ^ 1) for i in range(4)])


def to_x(value):
    return lax.ppermute(value, "section", [(i, i ^ 2) for i in range(4)])


def to_y(value):
    return lax.ppermute(value, "shard", [(0, 1), (1, 0)])


def to_z(value, bits):
    return lax.ppermute(value, "tensor", [(i, i ^ bits) for i in range(4)])


def row_dot(rows, full):
    return lax.dot_general(rows, full, (((1,), (0,)), ((), ())), preferred_element_type=F32)


def row_dot_t(rows, full):
    return lax.dot_general(rows, full, (((1,), (1,)), ((), ())), preferred_element_type=F32)


def token_dot(left, right):
    return lax.dot_general(left, right, (((0,), (0,)), ((), ())), preferred_element_type=F32)


def halves(value):
    high = value.astype(BF16)
    return high, (value - high.astype(F32)).astype(BF16)


def coded_rows(rows):
    return rows + rows // 6


def scaling(value):
    top = jnp.maximum(jnp.max(jnp.abs(value), axis=0, keepdims=True), 1e-30)
    exponent = jnp.ceil(jnp.log2(top))
    return exponent, value * (jnp.exp2(-exponent) * 32760.0)


def encode(value):
    exponent, scaled = scaling(value)
    coarse = jnp.round(scaled)
    fine = jnp.clip(jnp.floor((scaled - coarse) * 4.0), -2.0, 1.0) + 2.0
    tiles = value.shape[0] // 8
    parts = [coarse]
    for first in range(0, tiles + 1, 8):
        full = first + 8 <= tiles
        word = -32768.0 if full else jnp.broadcast_to(exponent * 256.0, (8, value.shape[1]))
        for index in range(first, min(first + 8, tiles)):
            word = word + fine[8 * index : 8 * index + 8] * float(4 ** (index - first))
        parts.append(word)
    return jnp.concatenate(parts, axis=0).astype(jnp.int32).astype(jnp.int16)


def decode(words):
    rows = words.shape[0] // 7 * 6
    tiles = rows // 8
    wide = words.astype(jnp.int32)
    coarse = wide[:rows].astype(F32)
    low = []
    for first in range(0, tiles + 1, 8):
        word = wide[rows + first : rows + first + 8]
        if first + 8 <= tiles:
            word = word + 32768
        for index in range(first, min(first + 8, tiles)):
            low.append((jnp.right_shift(word, 2 * (index - first)) & 3).astype(F32))
    exponent = jnp.right_shift(word, 8).astype(F32)[:1]
    fine = jnp.concatenate(low, axis=0)
    return (coarse + (fine - 1.5) * 0.25) * (jnp.exp2(exponent) * (1.0 / 32760.0))


def root_rows(rows):
    return rows + rows // 3


def encode_root(value):
    rows = value.shape[0]
    part = rows // 4
    exponent, scaled = scaling(value)
    coarse = jnp.round(scaled)
    fine = jnp.clip(jnp.floor((scaled - coarse) * 16.0), -8.0, 7.0) + 8.0
    words = fine[:part] - 32768.0
    for index in (1, 2, 3):
        words = words + fine[index * part : (index + 1) * part] * float(16**index)
    tail = jnp.broadcast_to(exponent, (rows // 3 - part, value.shape[1]))
    both = jnp.concatenate([coarse, words, tail], axis=0)
    return both.astype(jnp.int32).astype(jnp.int16)


def decode_root(words):
    rows = words.shape[0] // 4 * 3
    part = rows // 4
    wide = words.astype(jnp.int32)
    coarse = wide[:rows].astype(F32)
    fine = wide[rows : rows + part] + 32768
    exponent = wide[rows + part : rows + part + 8].astype(F32)[:1]
    parts = [(jnp.right_shift(fine, 4 * index) & 15).astype(F32) for index in range(4)]
    low = jnp.concatenate(parts, axis=0)
    return (coarse + (low - 7.5) * (1.0 / 16.0)) * (jnp.exp2(exponent) * (1.0 / 32760.0))


def used_slot(meta, plane, nth):
    seen = jnp.int32(0)
    place = jnp.int32(0)
    block = jnp.int32(0)
    for spot in range(4):
        entry = meta[4 * plane + spot]
        used = entry >= 0
        hit = jnp.logical_and(used, seen == nth)
        place = jnp.where(hit, spot, place)
        block = jnp.where(hit, entry, block)
        seen = seen + jnp.where(used, 1, 0)
    return place, block


ORDER = (2, 3, 1, 0)


SMEM_SPEC = pl.BlockSpec(memory_space=pltpu.SMEM)
VMEM_SPEC = pl.BlockSpec(memory_space=pltpu.VMEM)
HBM_SPEC = pl.BlockSpec(memory_space=pltpu.HBM)


def work(micros):
    return pl.CostEstimate(
        flops=int(micros * 10**9), transcendentals=0, bytes_accessed=int(micros * 36 * 10**6)
    )


def call(body, outs, ins, args, scratch=(), micros=1.0):
    return pl.pallas_call(
        body,
        out_shape=outs,
        in_specs=ins,
        out_specs=[VMEM_SPEC] * len(outs),
        cost_estimate=work(micros),
        scratch_shapes=list(scratch),
        compiler_params=pltpu.CompilerParams(vmem_limit_bytes=24 << 20),
    )(*args)


def start_copies(pairs, sems):
    copies = [
        pltpu.make_async_copy(source, target, sems.at[index])
        for index, (source, target) in enumerate(pairs)
    ]
    for copy in copies:
        copy.start()
    return copies


def in_parts(source, block, target, parts=4):
    span = target.shape[0] // parts
    rows = [pl.ds(part * span, span) for part in range(parts)]
    return [(source.at[block, part], target.at[part]) for part in rows]


def pick_kernel(meta, xin, dout, left, right, far, mine, roots, own, sems):
    _, block = used_slot(meta, 1 - meta[8], 1 - meta[11])
    pairs = in_parts(xin, block, far.at[0]) + in_parts(dout, block, far.at[1])
    _, block = used_slot(meta, 1 - meta[8], meta[11])
    pairs += in_parts(xin, block, own.at[0]) + in_parts(dout, block, own.at[1])
    place, block = used_slot(meta, meta[8], 1 - meta[11])
    pairs += [(left.at[place], roots.at[0]), (right.at[place], roots.at[1])]
    pairs += in_parts(xin, block, mine.at[0]) + in_parts(dout, block, mine.at[1])
    for copy in start_copies(pairs, sems):
        copy.wait()


def own_far_kernel(taken, out):
    out[...] = token_dot(taken[0], taken[1])


def own_mine_kernel(meta, xin, dout, out, taken, sems):
    _, block = used_slot(meta, meta[8], meta[11])
    pairs = in_parts(xin, block, taken.at[0]) + in_parts(dout, block, taken.at[1])
    copies = start_copies(pairs, sems)
    half = taken.shape[1] // 2
    for part in (0, 1):
        for index in (0, 1):
            copies[2 * part + index].wait()
            copies[4 + 2 * part + index].wait()
        rows = pl.ds(part * half, half)
        value = token_dot(taken[0, rows, :], taken[1, rows, :])
        out[...] = value if part == 0 else out[...] + value


def far_kernel(meta, got, own_ref, *refs):
    outs, total = refs[:4], refs[4]
    total[...] = own_ref[...] + token_dot(got[0], got[1])
    span = total.shape[0] // 4
    for out, bits in zip(outs, ORDER):
        first = pl.multiple_of((meta[9] ^ bits) * span, 64)
        out[...] = encode(total[pl.ds(first, span), :])


def mine_kernel(got, own_ref, out_ref):
    out_ref[...] = own_ref[...] + token_dot(got[0], got[1])


def rows_kernel(meta, left, right, got, left_out, right_out, whole, sems):
    core = meta[11]
    rows = got.shape[1]
    place, _ = used_slot(meta, meta[8], core)
    own = pl.ds(pl.multiple_of(core * rows, 16), rows)
    sib = pl.ds(pl.multiple_of((1 - core) * rows, 16), rows)
    pairs = [(left.at[place], left_out.at[own, :]), (right.at[place], whole.at[own, :])]
    copies = start_copies(pairs, sems)
    left_out[sib, :] = got[0]
    whole[sib, :] = got[1]
    for copy in copies:
        copy.wait()
    right_out[...] = encode_root(whole[...])


def y_kernel(meta, got, mine, coded, keep, both):
    rows = keep.shape[0]
    both[...] = decode(got[...]) + mine[...]
    side = meta[10]
    keep[...] = both[pl.ds(pl.multiple_of(side * rows, 32), rows), :]
    coded[...] = encode(both[pl.ds(pl.multiple_of((1 - side) * rows, 32), rows), :])


def after_y(meta, got, mine, bits):
    size = mine.shape[1]
    rows = size // 8
    return pl.pallas_call(
        y_kernel,
        out_shape=[
            jax.ShapeDtypeStruct((coded_rows(rows), size), jnp.int16),
            jax.ShapeDtypeStruct((rows, size), F32),
        ],
        grid_spec=pltpu.PrefetchScalarGridSpec(
            num_scalar_prefetch=1,
            grid=(1,),
            in_specs=[
                pl.BlockSpec(got.shape, lambda step, meta_ref: (0, 0)),
                pl.BlockSpec((2 * rows, size), lambda step, meta_ref: (meta_ref[9] ^ bits, 0)),
            ],
            out_specs=[
                pl.BlockSpec((coded_rows(rows), size), lambda step, meta_ref: (0, 0)),
                pl.BlockSpec((rows, size), lambda step, meta_ref: (0, 0)),
            ],
            scratch_shapes=[pltpu.VMEM((2 * rows, size), F32)],
        ),
        compiler_params=pltpu.CompilerParams(vmem_limit_bytes=24 << 20),
        cost_estimate=work(1.1),
    )(meta, got, mine)


def x_kernel(keep, *refs):
    total = keep[...]
    for part in refs[:-1]:
        total = total + decode(part[...])
    refs[-1][...] = encode(total)


def grad_kernel(factor, keep, got, far, near, grad, coded):
    total = keep[...]
    for part in (got, far, near):
        total = total + decode(part[...])
    total = total * factor
    grad[...] = total
    coded[...] = encode(total)


def put_rows(spot, value, high_ref, low_ref):
    rows = value.shape[0]
    first = pl.multiple_of(spot * rows, 32)
    high, low = halves(value)
    high_ref[pl.ds(first, rows), :] = high
    low_ref[pl.ds(first, rows), :] = low


def root_kernel(meta, *refs):
    for index in range(8):
        spot = 2 * (meta[9] ^ (index // 2)) + (meta[10] ^ (index % 2))
        put_rows(spot, decode_root(refs[index][...]), refs[8], refs[9])


def column_kernel(meta, grad_ref, one, two, three, high_ref, low_ref):
    for step, ref in enumerate((grad_ref, one, two, three)):
        value = decode(ref[...]) if step else ref[...]
        put_rows(2 * (meta[9] ^ step) + meta[10], value, high_ref, low_ref)


def direction_kernel(meta, high_in, low_in, *refs):
    pieces = refs[:4]
    left_ref, root_high, root_low, adam_ref = refs[4:8]
    own_dir, sib_dir, sums, high_ref, low_ref, whole = refs[8:14]
    for step in range(4):
        spot = 2 * (meta[9] ^ step)
        put_rows(spot + 1 - meta[10], decode(pieces[step][...]), high_ref, low_ref)
        rows = left_ref.shape[0]
        held = pl.ds(pl.multiple_of((spot + meta[10]) * rows, 32), rows)
        high_ref[held, :] = high_in[held, :]
        low_ref[held, :] = low_in[held, :]
    half = left_ref.shape[0] // 2
    high, low = high_ref[...], low_ref[...]
    left_high, left_low = halves(left_ref[...])
    prod = row_dot(left_high, high) + (row_dot(left_low, high) + row_dot(left_high, low))
    prod_high, prod_low = halves(prod)
    root_h, root_l = root_high[...], root_low[...]
    direction = row_dot(prod_high, root_h) + (
        row_dot(prod_low, root_h) + row_dot(prod_high, root_l)
    )
    whole[...] = direction
    own_dir[...] = whole[pl.ds(pl.multiple_of(meta[11] * half, 16), half), :]
    sib_dir[...] = whole[pl.ds(pl.multiple_of((1 - meta[11]) * half, 16), half), :]
    lane = lax.broadcasted_iota(jnp.int32, (1, 128), 1)
    sums[...] = jnp.where(lane == 2, jnp.sum(direction * direction), adam_ref[...])


def left_kernel(meta, grad_ref, high_ref, low_ref, own_out, sib_out, whole):
    half = own_out.shape[0]
    high, low = high_ref[...], low_ref[...]
    own_high, own_low = halves(grad_ref[...])
    whole[...] = row_dot_t(own_high, high) + (
        row_dot_t(own_low, high) + row_dot_t(own_high, low)
    )
    own_out[...] = whole[pl.ds(pl.multiple_of(meta[11] * half, 16), half), :]
    sib_out[...] = whole[pl.ds(pl.multiple_of((1 - meta[11]) * half, 16), half), :]


def right_kernel(meta, high_ref, low_ref, own_out, sib_out, whole):
    half, size = own_out.shape
    rows = 2 * half
    first = (2 * meta[9] + meta[10]) * rows
    high, low = high_ref[...], low_ref[...]
    row_ids = lax.broadcasted_iota(jnp.int32, (rows, size), 0) + first
    col_ids = lax.broadcasted_iota(jnp.int32, (rows, size), 1)
    pick = jnp.where(row_ids == col_ids, 1.0, 0.0).astype(BF16)
    col_high = row_dot_t(pick, high).astype(BF16)
    col_low = row_dot_t(pick, low).astype(BF16)
    whole[...] = row_dot(col_high, high) + (row_dot(col_low, high) + row_dot(col_high, low))
    own_out[...] = whole[pl.ds(pl.multiple_of(meta[11] * half, 16), half), :]
    sib_out[...] = whole[pl.ds(pl.multiple_of((1 - meta[11]) * half, 16), half), :]


def moment_kernel(meta, grad, got, first, second, first_out, second_out, adam_out):
    plane, core = meta[8], meta[11]
    rows = got.shape[0]
    first_out[...] = first[...]
    second_out[...] = second[...]
    lane = lax.broadcasted_iota(jnp.int32, (1, 128), 1)
    line = jnp.zeros((1, 128), F32)
    own = grad[pl.ds(pl.multiple_of(core * rows, 16), rows), :]
    for slot, value in ((core, own), (1 - core, got[...])):
        place, _ = used_slot(meta, plane, slot)
        one = 0.9 * first[place] + 0.1 * value
        two = 0.999 * second[place] + 0.001 * value * value
        first_out[place] = one
        second_out[place] = two
        adam = one / (jnp.sqrt(two) + 1e-08)
        line = line + jnp.where(lane == slot, jnp.sum(adam * adam), 0.0)
    adam_out[...] = line


def weight_kernel(meta, sums, own_dir, sib_dir, weights, out):
    plane, core = meta[8], meta[11]
    lane = lax.broadcasted_iota(jnp.int32, (1, 128), 1)
    for slot, value in ((core, own_dir[...]), (1 - core, sib_dir[...])):
        line = jnp.zeros((1, 128), F32)
        for device in range(sums.shape[0]):
            kept = jnp.logical_or(lane == slot, jnp.logical_and(lane == 2, slot == device % 2))
            line = line + jnp.where(kept, sums[device], 0.0)
        dir_sq = jnp.sum(jnp.where(lane == 2, line, 0.0), axis=1, keepdims=True)
        adam_sq = jnp.sum(jnp.where(lane == 2, 0.0, line), axis=1, keepdims=True)
        graft = jnp.sqrt(adam_sq) / (jnp.sqrt(dir_sq) + 1e-06)
        _, block = used_slot(meta, plane, slot)
        out[slot] = (weights[block].astype(F32) - 0.05 * graft * value).astype(BF16)


def place_kernel(meta, near, mirror, out):
    plane = meta[8]
    for slot in (0, 1):
        _, block = used_slot(meta, plane, slot)
        out[block] = near[slot]
        _, block = used_slot(meta, 1 - plane, slot)
        out[block] = mirror[slot]


def stat_kernel(
    meta, own_right, got_right, own_left, got_left, right, left, right_out, left_out
):
    for own, got, stat, out in (
        (own_right, got_right, right, right_out),
        (own_left, got_left, left, left_out),
    ):
        out[...] = stat[...]
        for slot, gram in ((meta[11], own), (1 - meta[11], got)):
            place, _ = used_slot(meta, meta[8], slot)
            out[place] = 0.5 * stat[place] + 0.5 * gram[...]


def two_planes(
    xin,
    dout,
    weights,
    slot_block,
    left_stat,
    right_stat,
    left_root,
    right_root,
    first_moment,
    second_moment,
):
    block_count, tokens, size = xin.shape
    slot_count, rows = left_stat.shape[:2]
    device_count = lax.axis_size(("shard",) + GROUP)
    factor = 1.0 / math.sqrt(tokens * device_count * size)
    section = lax.axis_index("section")
    meta = jnp.concatenate(
        [
            slot_block,
            jnp.stack(
                [lax.axis_index("shard"), lax.axis_index("tensor"), section // 2, section % 2]
            ).astype(jnp.int32),
        ]
    )

    def shape(*dims, dtype=F32):
        return jax.ShapeDtypeStruct(dims, dtype)

    words = jnp.int16
    tile = shape(rows, size)
    tokens_in = shape(2, tokens, size, dtype=BF16)
    piece = shape(coded_rows(2 * rows), size, dtype=words)

    def dmas(count):
        return pltpu.SemaphoreType.DMA((count,))

    xin, dout, left_root, right_root = (
        pltpu.with_memory_space_constraint(value, pltpu.HBM)
        for value in (xin, dout, left_root, right_root)
    )
    far_in, mine_in, roots, own_in = call(
        pick_kernel,
        [tokens_in, tokens_in, shape(2, rows, size), tokens_in],
        [SMEM_SPEC] + [HBM_SPEC] * 4,
        (meta, xin, dout, left_root, right_root),
        [dmas(26)],
    )
    roots = to_core(roots)
    far_in = to_core(far_in)
    mine_in = to_core(mine_in)
    (own_far,) = call(own_far_kernel, [shape(size, size)], [VMEM_SPEC], (own_in,))
    chunk = coded_rows(size // 4)
    coded = list(call(
        far_kernel,
        [shape(chunk, size, dtype=words)] * 4,
        [SMEM_SPEC] + [VMEM_SPEC] * 2,
        (meta, far_in, own_far),
        [pltpu.VMEM((size, size), F32)],
    ))
    coded[0], roots = lax.optimization_barrier((coded[0], roots))
    got_y = [to_y(value) for value in coded]
    left_rows, right_coded = call(
        rows_kernel,
        [shape(2 * rows, size), shape(root_rows(2 * rows), size, dtype=words)],
        [SMEM_SPEC] + [HBM_SPEC] * 2 + [VMEM_SPEC],
        (meta, left_root, right_root, roots),
        [pltpu.VMEM((2 * rows, size), F32), dmas(2)],
    )
    right_coded, later = lax.optimization_barrier((right_coded, meta))
    (own_mine,) = call(
        own_mine_kernel,
        [shape(size, size)],
        [SMEM_SPEC] + [HBM_SPEC] * 2,
        (later, xin, dout),
        [pltpu.VMEM((2, tokens, size), BF16), dmas(8)],
    )
    root_z = {3: to_z(right_coded, 3), 1: to_z(right_coded, 1)}
    mine_in, sent = lax.optimization_barrier((mine_in, right_coded))
    root_x = {0: to_x(sent)}
    sent, root_z[1] = lax.optimization_barrier((root_z[3], root_z[1]))
    root_z[2] = to_z(sent, 1)
    sent, root_x[0] = lax.optimization_barrier((root_z[1], root_x[0]))
    root_x[1] = to_x(sent)

    (mine,) = call(
        mine_kernel,
        [shape(size, size)],
        [VMEM_SPEC] * 2,
        (mine_in, own_mine),
    )
    got_x, keeps, got_z = [], [], []
    for index, bits in enumerate(ORDER):
        arrived = got_y[index]
        if index == 1:
            arrived, got_x[0], root_x[0], root_z[3] = lax.optimization_barrier(
                (arrived, got_x[0], root_x[0], root_z[3])
            )
            root_x[3] = to_x(root_z[3])
        if index == 2:
            arrived, got_x[1], root_x[1], root_z[2] = lax.optimization_barrier(
                (arrived, got_x[1], root_x[1], root_z[2])
            )
        if index == 3:
            arrived, got_x[2], root_x[3] = lax.optimization_barrier(
                (arrived, got_x[2], root_x[3])
            )
        sent, keep = after_y(meta, arrived, mine, bits)
        got_x.append(to_x(sent))
        keeps.append(keep)
        if index:
            carried = got_z if index == 2 else []
            (sent,) = call(
                x_kernel,
                [piece],
                [VMEM_SPEC] * (2 + len(carried)),
                (keeps[index - 1], got_x[index - 1], *carried),
            )
            got_z.append(to_z(sent, (1, 3, 1)[index - 1]))
    grad, coded = call(
        functools.partial(grad_kernel, factor),
        [shape(2 * rows, size), piece],
        [VMEM_SPEC] * 4,
        (keeps[3], got_x[3], got_z[1], got_z[2]),
    )

    across = {0: to_x(coded)}
    column = {bits: to_z(coded, bits) for bits in (1, 2, 3)}
    coded, sent = lax.optimization_barrier((coded, root_z[2]))
    root_x[2] = to_x(sent)
    column[1], across[0] = lax.optimization_barrier((column[1], across[0]))
    for bits in (1, 2, 3):
        across[bits] = to_x(column[bits])
    root_z[0] = right_coded
    root_pieces = []
    for index in range(4):
        root_pieces += [root_z[index], root_x[index]]
    root_high, root_low = call(
        root_kernel,
        [shape(size, size, dtype=BF16)] * 2,
        [SMEM_SPEC] + [VMEM_SPEC] * 8,
        (meta, *root_pieces),
    )

    core = section % 2
    grad_out = lax.dynamic_slice_in_dim(grad, (1 - core) * rows, rows, 0)
    stack = shape(slot_count, rows, size)
    new_first, new_second, adam = call(
        moment_kernel,
        [stack, stack, shape(1, 128)],
        [SMEM_SPEC] + [VMEM_SPEC] * 4,
        (meta, grad, to_core(grad_out), first_moment, second_moment),
    )
    split = [shape(size, size, dtype=BF16)] * 2
    high, low = call(
        column_kernel,
        split,
        [SMEM_SPEC] + [VMEM_SPEC] * 4,
        (meta, grad, column[1], column[2], column[3]),
    )
    own_dir, sib_dir, sums, high, low = call(
        direction_kernel,
        [tile, tile, shape(1, 128)] + split,
        [SMEM_SPEC] + [VMEM_SPEC] * 10,
        (meta, high, low, *across.values(), left_rows, root_high, root_low, adam),
        [pltpu.VMEM((2 * rows, size), F32)],
        4.0,
    )
    sib_dir = to_core(sib_dir)
    sums = jnp.broadcast_to(sums[None], (device_count // 2, 1, 128))
    sums = lax.all_to_all(sums, GROUP, 0, 0)
    (near,) = call(
        weight_kernel,
        [shape(2, rows, size, dtype=BF16)],
        [SMEM_SPEC] + [VMEM_SPEC] * 4,
        (meta, sums, own_dir, sib_dir, weights),
    )
    mirror = to_y(near)
    high, near = lax.optimization_barrier((high, near))
    whole = [pltpu.VMEM((2 * rows, size), F32)]
    own_right, sib_right = call(
        right_kernel,
        [tile, tile],
        [SMEM_SPEC] + [VMEM_SPEC] * 2,
        (meta, high, low),
        whole,
        1.8,
    )
    got_right = to_core(sib_right)
    own_left, sib_left = call(
        left_kernel,
        [tile, tile],
        [SMEM_SPEC] + [VMEM_SPEC] * 3,
        (meta, grad, high, low),
        whole,
        1.4,
    )
    got_left = to_core(sib_left)
    (new_weights,) = call(
        place_kernel,
        [shape(block_count, rows, size, dtype=BF16)],
        [SMEM_SPEC] + [VMEM_SPEC] * 2,
        (meta, near, mirror),
    )
    got_left, new_weights = lax.optimization_barrier((got_left, new_weights))
    new_right, new_left = call(
        stat_kernel,
        [stack, stack],
        [SMEM_SPEC] + [VMEM_SPEC] * 6,
        (meta, own_right, got_right, own_left, got_left, right_stat, left_stat),
    )
    return new_weights, new_left, new_right, new_first, new_second


def solution(mesh):
    placed = (
        P(None, ("shard", "tensor", "section"), None),
        P(None, ("shard", "tensor", "section"), None),
        P(None, ("tensor", "section"), None),
        P(),
        P("shard", ("tensor", "section"), None),
        P("shard", ("tensor", "section"), None),
        P("shard", ("tensor", "section"), None),
        P("shard", ("tensor", "section"), None),
        P("shard", ("tensor", "section"), None),
        P("shard", ("tensor", "section"), None),
    )
    shape = mesh.shape
    pair = (shape["shard"], shape["tensor"], shape["section"]) == (2, 4, 4)
    return jax.shard_map(
        two_planes if pair else any_mesh,
        mesh=mesh,
        in_specs=placed,
        out_specs=(
            P(None, ("tensor", "section"), None),
            P("shard", ("tensor", "section"), None),
            P("shard", ("tensor", "section"), None),
            P("shard", ("tensor", "section"), None),
            P("shard", ("tensor", "section"), None),
        ),
        check_vma=False,
    )
```

```python
import functools
import math

import jax
import jax.numpy as jnp
from jax import lax
from jax.experimental import pallas as pl
from jax.experimental.pallas import tpu as pltpu
from jax.sharding import PartitionSpec as P

F32 = jnp.float32
BF16 = jnp.bfloat16
GROUP = ("tensor", "section")


def spread(value, axis, source):
    kept = jnp.where(lax.axis_index(axis) == source, value, 0).astype(value.dtype)
    return lax.psum(kept, axis)


def absorb_slot(mine_rows, root_rows, portion, col_first):
    highest = lax.Precision.HIGHEST
    row_count = mine_rows.shape[0]
    block_part = jnp.dot(mine_rows, portion.T, precision=highest)
    own_cols = lax.dynamic_slice_in_dim(portion, col_first, row_count, 1)
    right_gram = jnp.dot(own_cols.T, portion, precision=highest)
    left_prod = jnp.dot(root_rows, portion, precision=highest)
    return (block_part, right_gram, left_prod)


def apply_slot(prod_rows, portion):
    return jnp.dot(prod_rows, portion, precision=lax.Precision.HIGHEST)


def any_mesh(
    xin,
    dout,
    weights,
    slot_block,
    left_stat,
    right_stat,
    left_root,
    right_root,
    first_moment,
    second_moment,
):
    block_count, tok_count, block_size = xin.shape
    slot_count, row_count = (left_stat.shape[0], left_stat.shape[1])
    group_count = lax.axis_size(GROUP)
    shard_count = lax.axis_size("shard")
    factor = 1.0 / math.sqrt(tok_count * shard_count * group_count * block_size)
    pieces_out = []
    for grad_member in range(block_count):
        cols = xin[grad_member]
        pieces_out.append(
            jnp.einsum("tr,tc->rc", cols, dout[grad_member], preferred_element_type=jnp.float32)
        )
    partial_rows = lax.psum_scatter(
        jnp.concatenate(pieces_out, axis=1) * factor,
        GROUP,
        scatter_dimension=0,
        tiled=True,
    )
    grad_rows = lax.psum(partial_rows, "shard")
    shard_idx = lax.axis_index("shard")
    group_idx = lax.axis_index(GROUP)
    my_slots = lax.dynamic_slice_in_dim(slot_block, shard_idx * slot_count, slot_count)
    valid = my_slots >= 0
    picks = jnp.maximum(my_slots, 0)
    grad_three = grad_rows.reshape(row_count, block_count, block_size)
    mine = jnp.moveaxis(jnp.take(grad_three, picks, axis=1), 1, 0)
    col_first = group_idx * row_count
    zeros_rows = jnp.zeros((slot_count, row_count, block_size), jnp.float32)
    totals = (zeros_rows, zeros_rows, zeros_rows)
    portion = lax.all_gather(mine, GROUP, axis=1, tiled=True)
    lefts = []
    rights = []
    prods = []
    for slot_pos in range(slot_count):
        current = (totals[0][slot_pos], totals[1][slot_pos], totals[2][slot_pos])
        result = lax.cond(
            valid[slot_pos],
            lambda values: absorb_slot(
                mine[slot_pos], left_root[slot_pos], portion[slot_pos], col_first
            ),
            lambda values: values,
            current,
        )
        lefts.append(result[0])
        rights.append(result[1])
        prods.append(result[2])
    left_gram = jnp.stack(lefts)
    right_gram = jnp.stack(rights)
    left_prod = jnp.stack(prods)
    apply_portion = lax.all_gather(right_root, GROUP, axis=1, tiled=True)
    outputs = []
    for apply_slot_pos in range(slot_count):
        outputs.append(
            lax.cond(
                valid[apply_slot_pos],
                lambda values: apply_slot(left_prod[apply_slot_pos], apply_portion[apply_slot_pos]),
                lambda values: values,
                zeros_rows[apply_slot_pos],
            )
        )
    direction = jnp.stack(outputs)
    moment_one = 0.9 * first_moment + 0.1 * mine
    moment_two = 0.999 * second_moment + 0.001 * mine * mine
    adam = moment_one / (jnp.sqrt(moment_two) + 1e-08)
    adam_sq, dir_sq = lax.psum(
        (jnp.sum(adam * adam, axis=(1, 2)), jnp.sum(direction * direction, axis=(1, 2))),
        GROUP,
    )
    graft = jnp.sqrt(adam_sq) / (jnp.sqrt(dir_sq) + 1e-06)
    mask = valid[:, None, None]
    new_left = jnp.where(mask, 0.5 * left_stat + 0.5 * left_gram, left_stat)
    new_right = jnp.where(mask, 0.5 * right_stat + 0.5 * right_gram, right_stat)
    new_first = jnp.where(mask, moment_one, first_moment)
    new_second = jnp.where(mask, moment_two, second_moment)
    my_weights = jnp.take(weights, picks, axis=0)
    new_rows = (my_weights.astype(jnp.float32) - 0.05 * graft[:, None, None] * direction).astype(
        jnp.bfloat16
    )
    slot_ids = jnp.arange(slot_block.shape[0], dtype=jnp.int32)
    holders = [
        jnp.sum(slot_ids * (slot_block == member).astype(jnp.int32))
        for member in range(block_count)
    ]
    published = []
    for member in range(block_count):
        owner = holders[member] // slot_count
        within = holders[member] % slot_count
        chosen = lax.dynamic_index_in_dim(new_rows, within, 0, keepdims=False)
        published.append(spread(chosen, "shard", owner))
    new_weights = jnp.stack(published)
    return (new_weights, new_left, new_right, new_first, new_second)


def to_core(value):
    return lax.ppermute(value, "section", [(i, i ^ 1) for i in range(4)])


def to_x(value):
    return lax.ppermute(value, "section", [(i, i ^ 2) for i in range(4)])


def to_y(value):
    return lax.ppermute(value, "shard", [(0, 1), (1, 0)])


def to_z(value, bits):
    return lax.ppermute(value, "tensor", [(i, i ^ bits) for i in range(4)])


def row_dot(rows, full):
    return lax.dot_general(rows, full, (((1,), (0,)), ((), ())), preferred_element_type=F32)


def row_dot_t(rows, full):
    return lax.dot_general(rows, full, (((1,), (1,)), ((), ())), preferred_element_type=F32)


def token_dot(left, right):
    return lax.dot_general(left, right, (((0,), (0,)), ((), ())), preferred_element_type=F32)


def halves(value):
    high = value.astype(BF16)
    return high, (value - high.astype(F32)).astype(BF16)


def coded_rows(rows):
    return rows + rows // 6


def scaling(value):
    top = jnp.maximum(jnp.max(jnp.abs(value), axis=0, keepdims=True), 1e-30)
    exponent = jnp.ceil(jnp.log2(top))
    return exponent, value * (jnp.exp2(-exponent) * 32760.0)


def encode(value):
    exponent, scaled = scaling(value)
    coarse = jnp.round(scaled)
    fine = jnp.clip(jnp.floor((scaled - coarse) * 4.0), -2.0, 1.0) + 2.0
    tiles = value.shape[0] // 8
    parts = [coarse]
    for first in range(0, tiles + 1, 8):
        full = first + 8 <= tiles
        word = -32768.0 if full else jnp.broadcast_to(exponent * 256.0, (8, value.shape[1]))
        for index in range(first, min(first + 8, tiles)):
            word = word + fine[8 * index : 8 * index + 8] * float(4 ** (index - first))
        parts.append(word)
    return jnp.concatenate(parts, axis=0).astype(jnp.int32).astype(jnp.int16)


def decode(words):
    rows = words.shape[0] // 7 * 6
    tiles = rows // 8
    wide = words.astype(jnp.int32)
    coarse = wide[:rows].astype(F32)
    low = []
    for first in range(0, tiles + 1, 8):
        word = wide[rows + first : rows + first + 8]
        if first + 8 <= tiles:
            word = word + 32768
        for index in range(first, min(first + 8, tiles)):
            low.append((jnp.right_shift(word, 2 * (index - first)) & 3).astype(F32))
    exponent = jnp.right_shift(word, 8).astype(F32)[:1]
    fine = jnp.concatenate(low, axis=0)
    return (coarse + (fine - 1.5) * 0.25) * (jnp.exp2(exponent) * (1.0 / 32760.0))


def root_rows(rows):
    return rows + rows // 3


def encode_root(value):
    rows = value.shape[0]
    part = rows // 4
    exponent, scaled = scaling(value)
    coarse = jnp.round(scaled)
    fine = jnp.clip(jnp.floor((scaled - coarse) * 16.0), -8.0, 7.0) + 8.0
    words = fine[:part] - 32768.0
    for index in (1, 2, 3):
        words = words + fine[index * part : (index + 1) * part] * float(16**index)
    tail = jnp.broadcast_to(exponent, (rows // 3 - part, value.shape[1]))
    both = jnp.concatenate([coarse, words, tail], axis=0)
    return both.astype(jnp.int32).astype(jnp.int16)


def decode_root(words):
    rows = words.shape[0] // 4 * 3
    part = rows // 4
    wide = words.astype(jnp.int32)
    coarse = wide[:rows].astype(F32)
    fine = wide[rows : rows + part] + 32768
    exponent = wide[rows + part : rows + part + 8].astype(F32)[:1]
    parts = [(jnp.right_shift(fine, 4 * index) & 15).astype(F32) for index in range(4)]
    low = jnp.concatenate(parts, axis=0)
    return (coarse + (low - 7.5) * (1.0 / 16.0)) * (jnp.exp2(exponent) * (1.0 / 32760.0))


def used_slot(meta, plane, nth):
    seen = jnp.int32(0)
    place = jnp.int32(0)
    block = jnp.int32(0)
    for spot in range(4):
        entry = meta[4 * plane + spot]
        used = entry >= 0
        hit = jnp.logical_and(used, seen == nth)
        place = jnp.where(hit, spot, place)
        block = jnp.where(hit, entry, block)
        seen = seen + jnp.where(used, 1, 0)
    return place, block


ORDER = (2, 3, 1, 0)


SMEM_SPEC = pl.BlockSpec(memory_space=pltpu.SMEM)
VMEM_SPEC = pl.BlockSpec(memory_space=pltpu.VMEM)
HBM_SPEC = pl.BlockSpec(memory_space=pltpu.HBM)


def work(micros):
    return pl.CostEstimate(
        flops=int(micros * 10**9), transcendentals=0, bytes_accessed=int(micros * 36 * 10**6)
    )


def call(body, outs, ins, args, scratch=(), micros=1.0):
    return pl.pallas_call(
        body,
        out_shape=outs,
        in_specs=ins,
        out_specs=[VMEM_SPEC] * len(outs),
        cost_estimate=work(micros),
        scratch_shapes=list(scratch),
        compiler_params=pltpu.CompilerParams(vmem_limit_bytes=24 << 20),
    )(*args)


def start_copies(pairs, sems):
    copies = [
        pltpu.make_async_copy(source, target, sems.at[index])
        for index, (source, target) in enumerate(pairs)
    ]
    for copy in copies:
        copy.start()
    return copies


def in_parts(source, block, target, parts=4):
    span = target.shape[0] // parts
    rows = [pl.ds(part * span, span) for part in range(parts)]
    return [(source.at[block, part], target.at[part]) for part in rows]


def pick_kernel(meta, xin, dout, left, right, far, mine, roots, own, sems):
    _, block = used_slot(meta, 1 - meta[8], 1 - meta[11])
    pairs = in_parts(xin, block, far.at[0]) + in_parts(dout, block, far.at[1])
    _, block = used_slot(meta, 1 - meta[8], meta[11])
    pairs += in_parts(xin, block, own.at[0]) + in_parts(dout, block, own.at[1])
    place, block = used_slot(meta, meta[8], 1 - meta[11])
    pairs += [(left.at[place], roots.at[0]), (right.at[place], roots.at[1])]
    pairs += in_parts(xin, block, mine.at[0]) + in_parts(dout, block, mine.at[1])
    for copy in start_copies(pairs, sems):
        copy.wait()


def own_far_kernel(taken, out):
    out[...] = token_dot(taken[0], taken[1])


def own_mine_kernel(meta, xin, dout, out, taken, sems):
    _, block = used_slot(meta, meta[8], meta[11])
    pairs = in_parts(xin, block, taken.at[0]) + in_parts(dout, block, taken.at[1])
    copies = start_copies(pairs, sems)
    half = taken.shape[1] // 2
    for part in (0, 1):
        for index in (0, 1):
            copies[2 * part + index].wait()
            copies[4 + 2 * part + index].wait()
        rows = pl.ds(part * half, half)
        value = token_dot(taken[0, rows, :], taken[1, rows, :])
        out[...] = value if part == 0 else out[...] + value


def far_kernel(meta, got, own_ref, *refs):
    outs, total = refs[:4], refs[4]
    total[...] = own_ref[...] + token_dot(got[0], got[1])
    span = total.shape[0] // 4
    for out, bits in zip(outs, ORDER):
        first = pl.multiple_of((meta[9] ^ bits) * span, 64)
        out[...] = encode(total[pl.ds(first, span), :])


def mine_kernel(got, own_ref, out_ref):
    out_ref[...] = own_ref[...] + token_dot(got[0], got[1])


def rows_kernel(meta, left, right, got, left_out, right_out, whole, sems):
    core = meta[11]
    rows = got.shape[1]
    place, _ = used_slot(meta, meta[8], core)
    own = pl.ds(pl.multiple_of(core * rows, 16), rows)
    sib = pl.ds(pl.multiple_of((1 - core) * rows, 16), rows)
    pairs = [(left.at[place], left_out.at[own, :]), (right.at[place], whole.at[own, :])]
    copies = start_copies(pairs, sems)
    left_out[sib, :] = got[0]
    whole[sib, :] = got[1]
    for copy in copies:
        copy.wait()
    right_out[...] = encode_root(whole[...])


def y_kernel(meta, got, mine, coded, keep, both):
    rows = keep.shape[0]
    both[...] = decode(got[...]) + mine[...]
    side = meta[10]
    keep[...] = both[pl.ds(pl.multiple_of(side * rows, 32), rows), :]
    coded[...] = encode(both[pl.ds(pl.multiple_of((1 - side) * rows, 32), rows), :])


def after_y(meta, got, mine, bits):
    size = mine.shape[1]
    rows = size // 8
    return pl.pallas_call(
        y_kernel,
        out_shape=[
            jax.ShapeDtypeStruct((coded_rows(rows), size), jnp.int16),
            jax.ShapeDtypeStruct((rows, size), F32),
        ],
        grid_spec=pltpu.PrefetchScalarGridSpec(
            num_scalar_prefetch=1,
            grid=(1,),
            in_specs=[
                pl.BlockSpec(got.shape, lambda step, meta_ref: (0, 0)),
                pl.BlockSpec((2 * rows, size), lambda step, meta_ref: (meta_ref[9] ^ bits, 0)),
            ],
            out_specs=[
                pl.BlockSpec((coded_rows(rows), size), lambda step, meta_ref: (0, 0)),
                pl.BlockSpec((rows, size), lambda step, meta_ref: (0, 0)),
            ],
            scratch_shapes=[pltpu.VMEM((2 * rows, size), F32)],
        ),
        compiler_params=pltpu.CompilerParams(vmem_limit_bytes=24 << 20),
        cost_estimate=work(1.1),
    )(meta, got, mine)


def x_kernel(keep, *refs):
    total = keep[...]
    for part in refs[:-1]:
        total = total + decode(part[...])
    refs[-1][...] = encode(total)


def grad_kernel(factor, keep, got, far, near, grad, coded):
    total = keep[...]
    for part in (got, far, near):
        total = total + decode(part[...])
    total = total * factor
    grad[...] = total
    coded[...] = encode(total)


def put_rows(spot, value, high_ref, low_ref):
    rows = value.shape[0]
    first = pl.multiple_of(spot * rows, 32)
    high, low = halves(value)
    high_ref[pl.ds(first, rows), :] = high
    low_ref[pl.ds(first, rows), :] = low


def root_kernel(meta, *refs):
    for index in range(8):
        spot = 2 * (meta[9] ^ (index // 2)) + (meta[10] ^ (index % 2))
        put_rows(spot, decode_root(refs[index][...]), refs[8], refs[9])


def column_kernel(meta, grad_ref, one, two, three, high_ref, low_ref):
    for step, ref in enumerate((grad_ref, one, two, three)):
        value = decode(ref[...]) if step else ref[...]
        put_rows(2 * (meta[9] ^ step) + meta[10], value, high_ref, low_ref)


def direction_kernel(meta, high_in, low_in, *refs):
    pieces = refs[:4]
    left_ref, root_high, root_low, adam_ref = refs[4:8]
    own_dir, sib_dir, sums, high_ref, low_ref, whole = refs[8:14]
    for step in range(4):
        spot = 2 * (meta[9] ^ step)
        put_rows(spot + 1 - meta[10], decode(pieces[step][...]), high_ref, low_ref)
        rows = left_ref.shape[0]
        held = pl.ds(pl.multiple_of((spot + meta[10]) * rows, 32), rows)
        high_ref[held, :] = high_in[held, :]
        low_ref[held, :] = low_in[held, :]
    half = left_ref.shape[0] // 2
    high, low = high_ref[...], low_ref[...]
    left_high, left_low = halves(left_ref[...])
    prod = row_dot(left_high, high) + (row_dot(left_low, high) + row_dot(left_high, low))
    prod_high, prod_low = halves(prod)
    root_h, root_l = root_high[...], root_low[...]
    direction = row_dot(prod_high, root_h) + (
        row_dot(prod_low, root_h) + row_dot(prod_high, root_l)
    )
    whole[...] = direction
    own_dir[...] = whole[pl.ds(pl.multiple_of(meta[11] * half, 16), half), :]
    sib_dir[...] = whole[pl.ds(pl.multiple_of((1 - meta[11]) * half, 16), half), :]
    lane = lax.broadcasted_iota(jnp.int32, (1, 128), 1)
    sums[...] = jnp.where(lane == 2, jnp.sum(direction * direction), adam_ref[...])


def left_kernel(meta, grad_ref, high_ref, low_ref, own_out, sib_out, whole):
    half = own_out.shape[0]
    high, low = high_ref[...], low_ref[...]
    own_high, own_low = halves(grad_ref[...])
    whole[...] = row_dot_t(own_high, high) + (
        row_dot_t(own_low, high) + row_dot_t(own_high, low)
    )
    own_out[...] = whole[pl.ds(pl.multiple_of(meta[11] * half, 16), half), :]
    sib_out[...] = whole[pl.ds(pl.multiple_of((1 - meta[11]) * half, 16), half), :]


def right_kernel(meta, high_ref, low_ref, own_out, sib_out, whole):
    half, size = own_out.shape
    rows = 2 * half
    first = (2 * meta[9] + meta[10]) * rows
    high, low = high_ref[...], low_ref[...]
    row_ids = lax.broadcasted_iota(jnp.int32, (rows, size), 0) + first
    col_ids = lax.broadcasted_iota(jnp.int32, (rows, size), 1)
    pick = jnp.where(row_ids == col_ids, 1.0, 0.0).astype(BF16)
    col_high = row_dot_t(pick, high).astype(BF16)
    col_low = row_dot_t(pick, low).astype(BF16)
    whole[...] = row_dot(col_high, high) + (row_dot(col_low, high) + row_dot(col_high, low))
    own_out[...] = whole[pl.ds(pl.multiple_of(meta[11] * half, 16), half), :]
    sib_out[...] = whole[pl.ds(pl.multiple_of((1 - meta[11]) * half, 16), half), :]


def moment_kernel(meta, grad, got, first, second, first_out, second_out, adam_out):
    plane, core = meta[8], meta[11]
    rows = got.shape[0]
    first_out[...] = first[...]
    second_out[...] = second[...]
    lane = lax.broadcasted_iota(jnp.int32, (1, 128), 1)
    line = jnp.zeros((1, 128), F32)
    own = grad[pl.ds(pl.multiple_of(core * rows, 16), rows), :]
    for slot, value in ((core, own), (1 - core, got[...])):
        place, _ = used_slot(meta, plane, slot)
        one = 0.9 * first[place] + 0.1 * value
        two = 0.999 * second[place] + 0.001 * value * value
        first_out[place] = one
        second_out[place] = two
        adam = one / (jnp.sqrt(two) + 1e-08)
        line = line + jnp.where(lane == slot, jnp.sum(adam * adam), 0.0)
    adam_out[...] = line


def weight_kernel(meta, sums, own_dir, sib_dir, weights, out):
    plane, core = meta[8], meta[11]
    lane = lax.broadcasted_iota(jnp.int32, (1, 128), 1)
    for slot, value in ((core, own_dir[...]), (1 - core, sib_dir[...])):
        line = jnp.zeros((1, 128), F32)
        for device in range(sums.shape[0]):
            kept = jnp.logical_or(lane == slot, jnp.logical_and(lane == 2, slot == device % 2))
            line = line + jnp.where(kept, sums[device], 0.0)
        dir_sq = jnp.sum(jnp.where(lane == 2, line, 0.0), axis=1, keepdims=True)
        adam_sq = jnp.sum(jnp.where(lane == 2, 0.0, line), axis=1, keepdims=True)
        graft = jnp.sqrt(adam_sq) / (jnp.sqrt(dir_sq) + 1e-06)
        _, block = used_slot(meta, plane, slot)
        out[slot] = (weights[block].astype(F32) - 0.05 * graft * value).astype(BF16)


def place_kernel(meta, near, mirror, out):
    plane = meta[8]
    for slot in (0, 1):
        _, block = used_slot(meta, plane, slot)
        out[block] = near[slot]
        _, block = used_slot(meta, 1 - plane, slot)
        out[block] = mirror[slot]


def stat_kernel(
    meta, own_right, got_right, own_left, got_left, right, left, right_out, left_out
):
    for own, got, stat, out in (
        (own_right, got_right, right, right_out),
        (own_left, got_left, left, left_out),
    ):
        out[...] = stat[...]
        for slot, gram in ((meta[11], own), (1 - meta[11], got)):
            place, _ = used_slot(meta, meta[8], slot)
            out[place] = 0.5 * stat[place] + 0.5 * gram[...]


def two_planes(
    xin,
    dout,
    weights,
    slot_block,
    left_stat,
    right_stat,
    left_root,
    right_root,
    first_moment,
    second_moment,
):
    block_count, tokens, size = xin.shape
    slot_count, rows = left_stat.shape[:2]
    device_count = lax.axis_size(("shard",) + GROUP)
    factor = 1.0 / math.sqrt(tokens * device_count * size)
    section = lax.axis_index("section")
    meta = jnp.concatenate(
        [
            slot_block,
            jnp.stack(
                [lax.axis_index("shard"), lax.axis_index("tensor"), section // 2, section % 2]
            ).astype(jnp.int32),
        ]
    )

    def shape(*dims, dtype=F32):
        return jax.ShapeDtypeStruct(dims, dtype)

    words = jnp.int16
    tile = shape(rows, size)
    tokens_in = shape(2, tokens, size, dtype=BF16)
    piece = shape(coded_rows(2 * rows), size, dtype=words)

    def dmas(count):
        return pltpu.SemaphoreType.DMA((count,))

    xin, dout, left_root, right_root = (
        pltpu.with_memory_space_constraint(value, pltpu.HBM)
        for value in (xin, dout, left_root, right_root)
    )
    far_in, mine_in, roots, own_in = call(
        pick_kernel,
        [tokens_in, tokens_in, shape(2, rows, size), tokens_in],
        [SMEM_SPEC] + [HBM_SPEC] * 4,
        (meta, xin, dout, left_root, right_root),
        [dmas(26)],
    )
    roots = to_core(roots)
    far_in = to_core(far_in)
    mine_in = to_core(mine_in)
    (own_far,) = call(own_far_kernel, [shape(size, size)], [VMEM_SPEC], (own_in,))
    chunk = coded_rows(size // 4)
    coded = list(call(
        far_kernel,
        [shape(chunk, size, dtype=words)] * 4,
        [SMEM_SPEC] + [VMEM_SPEC] * 2,
        (meta, far_in, own_far),
        [pltpu.VMEM((size, size), F32)],
    ))
    coded[0], roots = lax.optimization_barrier((coded[0], roots))
    got_y = [to_y(value) for value in coded]
    left_rows, right_coded = call(
        rows_kernel,
        [shape(2 * rows, size), shape(root_rows(2 * rows), size, dtype=words)],
        [SMEM_SPEC] + [HBM_SPEC] * 2 + [VMEM_SPEC],
        (meta, left_root, right_root, roots),
        [pltpu.VMEM((2 * rows, size), F32), dmas(2)],
    )
    right_coded, later = lax.optimization_barrier((right_coded, meta))
    (own_mine,) = call(
        own_mine_kernel,
        [shape(size, size)],
        [SMEM_SPEC] + [HBM_SPEC] * 2,
        (later, xin, dout),
        [pltpu.VMEM((2, tokens, size), BF16), dmas(8)],
    )
    root_z = {3: to_z(right_coded, 3), 1: to_z(right_coded, 1)}
    mine_in, sent = lax.optimization_barrier((mine_in, right_coded))
    root_x = {0: to_x(sent)}
    sent, root_z[1] = lax.optimization_barrier((root_z[3], root_z[1]))
    root_z[2] = to_z(sent, 1)
    sent, root_x[0] = lax.optimization_barrier((root_z[1], root_x[0]))
    root_x[1] = to_x(sent)

    (mine,) = call(
        mine_kernel,
        [shape(size, size)],
        [VMEM_SPEC] * 2,
        (mine_in, own_mine),
    )
    got_x, keeps, got_z = [], [], []
    for index, bits in enumerate(ORDER):
        arrived = got_y[index]
        if index == 1:
            arrived, got_x[0], root_x[0], root_z[3] = lax.optimization_barrier(
                (arrived, got_x[0], root_x[0], root_z[3])
            )
            root_x[3] = to_x(root_z[3])
        if index == 2:
            arrived, got_x[1], root_x[1], root_z[2] = lax.optimization_barrier(
                (arrived, got_x[1], root_x[1], root_z[2])
            )
        if index == 3:
            arrived, got_x[2], root_x[3] = lax.optimization_barrier(
                (arrived, got_x[2], root_x[3])
            )
        sent, keep = after_y(meta, arrived, mine, bits)
        got_x.append(to_x(sent))
        keeps.append(keep)
        if index:
            carried = got_z if index == 2 else []
            (sent,) = call(
                x_kernel,
                [piece],
                [VMEM_SPEC] * (2 + len(carried)),
                (keeps[index - 1], got_x[index - 1], *carried),
            )
            got_z.append(to_z(sent, (1, 3, 1)[index - 1]))
    grad, coded = call(
        functools.partial(grad_kernel, factor),
        [shape(2 * rows, size), piece],
        [VMEM_SPEC] * 4,
        (keeps[3], got_x[3], got_z[1], got_z[2]),
    )

    across = {0: to_x(coded)}
    column = {bits: to_z(coded, bits) for bits in (3, 1)}
    coded, sent = lax.optimization_barrier((coded, root_z[2]))
    root_x[2] = to_x(sent)
    column[3], across[0] = lax.optimization_barrier((column[3], across[0]))
    column[2] = to_z(column[3], 1)
    for bits in (1, 3, 2):
        across[bits] = to_x(column[bits])

    root_z[0] = right_coded
    root_pieces = []
    for index in range(4):
        root_pieces += [root_z[index], root_x[index]]
    root_high, root_low = call(
        root_kernel,
        [shape(size, size, dtype=BF16)] * 2,
        [SMEM_SPEC] + [VMEM_SPEC] * 8,
        (meta, *root_pieces),
    )

    core = section % 2
    grad_out = lax.dynamic_slice_in_dim(grad, (1 - core) * rows, rows, 0)
    stack = shape(slot_count, rows, size)
    new_first, new_second, adam = call(
        moment_kernel,
        [stack, stack, shape(1, 128)],
        [SMEM_SPEC] + [VMEM_SPEC] * 4,
        (meta, grad, to_core(grad_out), first_moment, second_moment),
    )
    split = [shape(size, size, dtype=BF16)] * 2
    high, low = call(
        column_kernel,
        split,
        [SMEM_SPEC] + [VMEM_SPEC] * 4,
        (meta, grad, column[1], column[2], column[3]),
    )
    own_dir, sib_dir, sums, high, low = call(
        direction_kernel,
        [tile, tile, shape(1, 128)] + split,
        [SMEM_SPEC] + [VMEM_SPEC] * 10,
        (meta, high, low, *(across[step] for step in range(4)), left_rows, root_high, root_low, adam),
        [pltpu.VMEM((2 * rows, size), F32)],
        4.0,
    )
    sib_dir = to_core(sib_dir)
    sums = jnp.broadcast_to(sums[None], (device_count // 2, 1, 128))
    sums = lax.all_to_all(sums, GROUP, 0, 0)
    (near,) = call(
        weight_kernel,
        [shape(2, rows, size, dtype=BF16)],
        [SMEM_SPEC] + [VMEM_SPEC] * 4,
        (meta, sums, own_dir, sib_dir, weights),
    )
    mirror = to_y(near)
    high, near = lax.optimization_barrier((high, near))
    whole = [pltpu.VMEM((2 * rows, size), F32)]
    own_right, sib_right = call(
        right_kernel,
        [tile, tile],
        [SMEM_SPEC] + [VMEM_SPEC] * 2,
        (meta, high, low),
        whole,
        1.8,
    )
    got_right = to_core(sib_right)
    own_left, sib_left = call(
        left_kernel,
        [tile, tile],
        [SMEM_SPEC] + [VMEM_SPEC] * 3,
        (meta, grad, high, low),
        whole,
        1.4,
    )
    got_left = to_core(sib_left)
    (new_weights,) = call(
        place_kernel,
        [shape(block_count, rows, size, dtype=BF16)],
        [SMEM_SPEC] + [VMEM_SPEC] * 2,
        (meta, near, mirror),
    )
    got_left, new_weights = lax.optimization_barrier((got_left, new_weights))
    new_right, new_left = call(
        stat_kernel,
        [stack, stack],
        [SMEM_SPEC] + [VMEM_SPEC] * 6,
        (meta, own_right, got_right, own_left, got_left, right_stat, left_stat),
    )
    return new_weights, new_left, new_right, new_first, new_second


def solution(mesh):
    placed = (
        P(None, ("shard", "tensor", "section"), None),
        P(None, ("shard", "tensor", "section"), None),
        P(None, ("tensor", "section"), None),
        P(),
        P("shard", ("tensor", "section"), None),
        P("shard", ("tensor", "section"), None),
        P("shard", ("tensor", "section"), None),
        P("shard", ("tensor", "section"), None),
        P("shard", ("tensor", "section"), None),
        P("shard", ("tensor", "section"), None),
    )
    shape = mesh.shape
    pair = (shape["shard"], shape["tensor"], shape["section"]) == (2, 4, 4)
    return jax.shard_map(
        two_planes if pair else any_mesh,
        mesh=mesh,
        in_specs=placed,
        out_specs=(
            P(None, ("tensor", "section"), None),
            P("shard", ("tensor", "section"), None),
            P("shard", ("tensor", "section"), None),
            P("shard", ("tensor", "section"), None),
            P("shard", ("tensor", "section"), None),
        ),
        check_vma=False,
    )
```

```python
import functools
import math

import jax
import jax.numpy as jnp
from jax import lax
from jax.experimental import pallas as pl
from jax.experimental.pallas import tpu as pltpu
from jax.sharding import PartitionSpec as P

F32 = jnp.float32
BF16 = jnp.bfloat16
GROUP = ("tensor", "section")


def spread(value, axis, source):
    kept = jnp.where(lax.axis_index(axis) == source, value, 0).astype(value.dtype)
    return lax.psum(kept, axis)


def absorb_slot(mine_rows, root_rows, portion, col_first):
    highest = lax.Precision.HIGHEST
    row_count = mine_rows.shape[0]
    block_part = jnp.dot(mine_rows, portion.T, precision=highest)
    own_cols = lax.dynamic_slice_in_dim(portion, col_first, row_count, 1)
    right_gram = jnp.dot(own_cols.T, portion, precision=highest)
    left_prod = jnp.dot(root_rows, portion, precision=highest)
    return (block_part, right_gram, left_prod)


def apply_slot(prod_rows, portion):
    return jnp.dot(prod_rows, portion, precision=lax.Precision.HIGHEST)


def any_mesh(
    xin,
    dout,
    weights,
    slot_block,
    left_stat,
    right_stat,
    left_root,
    right_root,
    first_moment,
    second_moment,
):
    block_count, tok_count, block_size = xin.shape
    slot_count, row_count = (left_stat.shape[0], left_stat.shape[1])
    group_count = lax.axis_size(GROUP)
    shard_count = lax.axis_size("shard")
    factor = 1.0 / math.sqrt(tok_count * shard_count * group_count * block_size)
    pieces_out = []
    for grad_member in range(block_count):
        cols = xin[grad_member]
        pieces_out.append(
            jnp.einsum("tr,tc->rc", cols, dout[grad_member], preferred_element_type=jnp.float32)
        )
    partial_rows = lax.psum_scatter(
        jnp.concatenate(pieces_out, axis=1) * factor,
        GROUP,
        scatter_dimension=0,
        tiled=True,
    )
    grad_rows = lax.psum(partial_rows, "shard")
    shard_idx = lax.axis_index("shard")
    group_idx = lax.axis_index(GROUP)
    my_slots = lax.dynamic_slice_in_dim(slot_block, shard_idx * slot_count, slot_count)
    valid = my_slots >= 0
    picks = jnp.maximum(my_slots, 0)
    grad_three = grad_rows.reshape(row_count, block_count, block_size)
    mine = jnp.moveaxis(jnp.take(grad_three, picks, axis=1), 1, 0)
    col_first = group_idx * row_count
    zeros_rows = jnp.zeros((slot_count, row_count, block_size), jnp.float32)
    totals = (zeros_rows, zeros_rows, zeros_rows)
    portion = lax.all_gather(mine, GROUP, axis=1, tiled=True)
    lefts = []
    rights = []
    prods = []
    for slot_pos in range(slot_count):
        current = (totals[0][slot_pos], totals[1][slot_pos], totals[2][slot_pos])
        result = lax.cond(
            valid[slot_pos],
            lambda values: absorb_slot(
                mine[slot_pos], left_root[slot_pos], portion[slot_pos], col_first
            ),
            lambda values: values,
            current,
        )
        lefts.append(result[0])
        rights.append(result[1])
        prods.append(result[2])
    left_gram = jnp.stack(lefts)
    right_gram = jnp.stack(rights)
    left_prod = jnp.stack(prods)
    apply_portion = lax.all_gather(right_root, GROUP, axis=1, tiled=True)
    outputs = []
    for apply_slot_pos in range(slot_count):
        outputs.append(
            lax.cond(
                valid[apply_slot_pos],
                lambda values: apply_slot(left_prod[apply_slot_pos], apply_portion[apply_slot_pos]),
                lambda values: values,
                zeros_rows[apply_slot_pos],
            )
        )
    direction = jnp.stack(outputs)
    moment_one = 0.9 * first_moment + 0.1 * mine
    moment_two = 0.999 * second_moment + 0.001 * mine * mine
    adam = moment_one / (jnp.sqrt(moment_two) + 1e-08)
    adam_sq, dir_sq = lax.psum(
        (jnp.sum(adam * adam, axis=(1, 2)), jnp.sum(direction * direction, axis=(1, 2))),
        GROUP,
    )
    graft = jnp.sqrt(adam_sq) / (jnp.sqrt(dir_sq) + 1e-06)
    mask = valid[:, None, None]
    new_left = jnp.where(mask, 0.5 * left_stat + 0.5 * left_gram, left_stat)
    new_right = jnp.where(mask, 0.5 * right_stat + 0.5 * right_gram, right_stat)
    new_first = jnp.where(mask, moment_one, first_moment)
    new_second = jnp.where(mask, moment_two, second_moment)
    my_weights = jnp.take(weights, picks, axis=0)
    new_rows = (my_weights.astype(jnp.float32) - 0.05 * graft[:, None, None] * direction).astype(
        jnp.bfloat16
    )
    slot_ids = jnp.arange(slot_block.shape[0], dtype=jnp.int32)
    holders = [
        jnp.sum(slot_ids * (slot_block == member).astype(jnp.int32))
        for member in range(block_count)
    ]
    published = []
    for member in range(block_count):
        owner = holders[member] // slot_count
        within = holders[member] % slot_count
        chosen = lax.dynamic_index_in_dim(new_rows, within, 0, keepdims=False)
        published.append(spread(chosen, "shard", owner))
    new_weights = jnp.stack(published)
    return (new_weights, new_left, new_right, new_first, new_second)


def to_core(value):
    return lax.ppermute(value, "section", [(i, i ^ 1) for i in range(4)])


def to_x(value):
    return lax.ppermute(value, "section", [(i, i ^ 2) for i in range(4)])


def to_y(value):
    return lax.ppermute(value, "shard", [(0, 1), (1, 0)])


def to_z(value, bits):
    return lax.ppermute(value, "tensor", [(i, i ^ bits) for i in range(4)])


def row_dot(rows, full):
    return lax.dot_general(rows, full, (((1,), (0,)), ((), ())), preferred_element_type=F32)


def row_dot_t(rows, full):
    return lax.dot_general(rows, full, (((1,), (1,)), ((), ())), preferred_element_type=F32)


def token_dot(left, right):
    return lax.dot_general(left, right, (((0,), (0,)), ((), ())), preferred_element_type=F32)


def halves(value):
    high = value.astype(BF16)
    return high, (value - high.astype(F32)).astype(BF16)


def coded_rows(rows):
    return rows + rows // 6


def scaling(value):
    top = jnp.maximum(jnp.max(jnp.abs(value), axis=0, keepdims=True), 1e-30)
    exponent = jnp.ceil(jnp.log2(top))
    return exponent, value * (jnp.exp2(-exponent) * 32760.0)


def encode(value):
    exponent, scaled = scaling(value)
    coarse = jnp.round(scaled)
    fine = jnp.clip(jnp.floor((scaled - coarse) * 4.0), -2.0, 1.0) + 2.0
    tiles = value.shape[0] // 8
    parts = [coarse]
    for first in range(0, tiles + 1, 8):
        full = first + 8 <= tiles
        word = -32768.0 if full else jnp.broadcast_to(exponent * 256.0, (8, value.shape[1]))
        for index in range(first, min(first + 8, tiles)):
            word = word + fine[8 * index : 8 * index + 8] * float(4 ** (index - first))
        parts.append(word)
    return jnp.concatenate(parts, axis=0).astype(jnp.int32).astype(jnp.int16)


def decode(words):
    rows = words.shape[0] // 7 * 6
    tiles = rows // 8
    wide = words.astype(jnp.int32)
    coarse = wide[:rows].astype(F32)
    low = []
    for first in range(0, tiles + 1, 8):
        word = wide[rows + first : rows + first + 8]
        if first + 8 <= tiles:
            word = word + 32768
        for index in range(first, min(first + 8, tiles)):
            low.append((jnp.right_shift(word, 2 * (index - first)) & 3).astype(F32))
    exponent = jnp.right_shift(word, 8).astype(F32)[:1]
    fine = jnp.concatenate(low, axis=0)
    return (coarse + (fine - 1.5) * 0.25) * (jnp.exp2(exponent) * (1.0 / 32760.0))


def root_rows(rows):
    return rows + rows // 3


def encode_root(value):
    rows = value.shape[0]
    part = rows // 4
    exponent, scaled = scaling(value)
    coarse = jnp.round(scaled)
    fine = jnp.clip(jnp.floor((scaled - coarse) * 16.0), -8.0, 7.0) + 8.0
    words = fine[:part] - 32768.0
    for index in (1, 2, 3):
        words = words + fine[index * part : (index + 1) * part] * float(16**index)
    tail = jnp.broadcast_to(exponent, (rows // 3 - part, value.shape[1]))
    both = jnp.concatenate([coarse, words, tail], axis=0)
    return both.astype(jnp.int32).astype(jnp.int16)


def decode_root(words):
    rows = words.shape[0] // 4 * 3
    part = rows // 4
    wide = words.astype(jnp.int32)
    coarse = wide[:rows].astype(F32)
    fine = wide[rows : rows + part] + 32768
    exponent = wide[rows + part : rows + part + 8].astype(F32)[:1]
    parts = [(jnp.right_shift(fine, 4 * index) & 15).astype(F32) for index in range(4)]
    low = jnp.concatenate(parts, axis=0)
    return (coarse + (low - 7.5) * (1.0 / 16.0)) * (jnp.exp2(exponent) * (1.0 / 32760.0))


def used_slot(meta, plane, nth):
    seen = jnp.int32(0)
    place = jnp.int32(0)
    block = jnp.int32(0)
    for spot in range(4):
        entry = meta[4 * plane + spot]
        used = entry >= 0
        hit = jnp.logical_and(used, seen == nth)
        place = jnp.where(hit, spot, place)
        block = jnp.where(hit, entry, block)
        seen = seen + jnp.where(used, 1, 0)
    return place, block


ORDER = (2, 3, 1, 0)


SMEM_SPEC = pl.BlockSpec(memory_space=pltpu.SMEM)
VMEM_SPEC = pl.BlockSpec(memory_space=pltpu.VMEM)
HBM_SPEC = pl.BlockSpec(memory_space=pltpu.HBM)


def work(micros):
    return pl.CostEstimate(
        flops=int(micros * 10**9), transcendentals=0, bytes_accessed=int(micros * 36 * 10**6)
    )


def call(body, outs, ins, args, scratch=(), micros=1.0):
    return pl.pallas_call(
        body,
        out_shape=outs,
        in_specs=ins,
        out_specs=[VMEM_SPEC] * len(outs),
        cost_estimate=work(micros),
        scratch_shapes=list(scratch),
        compiler_params=pltpu.CompilerParams(vmem_limit_bytes=24 << 20),
    )(*args)


def start_copies(pairs, sems):
    copies = [
        pltpu.make_async_copy(source, target, sems.at[index])
        for index, (source, target) in enumerate(pairs)
    ]
    for copy in copies:
        copy.start()
    return copies


def in_parts(source, block, target, parts=4):
    span = target.shape[0] // parts
    rows = [pl.ds(part * span, span) for part in range(parts)]
    return [(source.at[block, part], target.at[part]) for part in rows]


def pick_kernel(meta, xin, dout, left, right, far, mine, roots, own, sems):
    _, block = used_slot(meta, 1 - meta[8], 1 - meta[11])
    pairs = in_parts(xin, block, far.at[0]) + in_parts(dout, block, far.at[1])
    _, block = used_slot(meta, 1 - meta[8], meta[11])
    pairs += in_parts(xin, block, own.at[0]) + in_parts(dout, block, own.at[1])
    place, block = used_slot(meta, meta[8], 1 - meta[11])
    pairs += [(left.at[place], roots.at[0]), (right.at[place], roots.at[1])]
    pairs += in_parts(xin, block, mine.at[0]) + in_parts(dout, block, mine.at[1])
    for copy in start_copies(pairs, sems):
        copy.wait()


def own_far_kernel(taken, out):
    out[...] = token_dot(taken[0], taken[1])


def own_mine_kernel(meta, xin, dout, out, taken, sems):
    _, block = used_slot(meta, meta[8], meta[11])
    pairs = in_parts(xin, block, taken.at[0]) + in_parts(dout, block, taken.at[1])
    copies = start_copies(pairs, sems)
    half = taken.shape[1] // 2
    for part in (0, 1):
        for index in (0, 1):
            copies[2 * part + index].wait()
            copies[4 + 2 * part + index].wait()
        rows = pl.ds(part * half, half)
        value = token_dot(taken[0, rows, :], taken[1, rows, :])
        out[...] = value if part == 0 else out[...] + value


def far_kernel(meta, got, own_ref, *refs):
    outs, total = refs[:4], refs[4]
    total[...] = own_ref[...] + token_dot(got[0], got[1])
    span = total.shape[0] // 4
    for out, bits in zip(outs, ORDER):
        first = pl.multiple_of((meta[9] ^ bits) * span, 64)
        out[...] = encode(total[pl.ds(first, span), :])


def mine_kernel(got, own_ref, out_ref):
    out_ref[...] = own_ref[...] + token_dot(got[0], got[1])


def rows_kernel(meta, left, right, got, left_out, right_out, whole, sems):
    core = meta[11]
    rows = got.shape[1]
    place, _ = used_slot(meta, meta[8], core)
    own = pl.ds(pl.multiple_of(core * rows, 16), rows)
    sib = pl.ds(pl.multiple_of((1 - core) * rows, 16), rows)
    pairs = [(left.at[place], left_out.at[own, :]), (right.at[place], whole.at[own, :])]
    copies = start_copies(pairs, sems)
    left_out[sib, :] = got[0]
    whole[sib, :] = got[1]
    for copy in copies:
        copy.wait()
    right_out[...] = encode_root(whole[...])


def y_kernel(meta, got, mine, coded, keep, both):
    rows = keep.shape[0]
    both[...] = decode(got[...]) + mine[...]
    side = meta[10]
    keep[...] = both[pl.ds(pl.multiple_of(side * rows, 32), rows), :]
    coded[...] = encode(both[pl.ds(pl.multiple_of((1 - side) * rows, 32), rows), :])


def after_y(meta, got, mine, bits):
    size = mine.shape[1]
    rows = size // 8
    return pl.pallas_call(
        y_kernel,
        out_shape=[
            jax.ShapeDtypeStruct((coded_rows(rows), size), jnp.int16),
            jax.ShapeDtypeStruct((rows, size), F32),
        ],
        grid_spec=pltpu.PrefetchScalarGridSpec(
            num_scalar_prefetch=1,
            grid=(1,),
            in_specs=[
                pl.BlockSpec(got.shape, lambda step, meta_ref: (0, 0)),
                pl.BlockSpec((2 * rows, size), lambda step, meta_ref: (meta_ref[9] ^ bits, 0)),
            ],
            out_specs=[
                pl.BlockSpec((coded_rows(rows), size), lambda step, meta_ref: (0, 0)),
                pl.BlockSpec((rows, size), lambda step, meta_ref: (0, 0)),
            ],
            scratch_shapes=[pltpu.VMEM((2 * rows, size), F32)],
        ),
        compiler_params=pltpu.CompilerParams(vmem_limit_bytes=24 << 20),
        cost_estimate=work(1.1),
    )(meta, got, mine)


def x_kernel(keep, *refs):
    total = keep[...]
    for part in refs[:-1]:
        total = total + decode(part[...])
    refs[-1][...] = encode(total)


def grad_kernel(factor, keep, got, far, near, grad, coded):
    total = keep[...]
    for part in (got, far, near):
        total = total + decode(part[...])
    total = total * factor
    grad[...] = total
    coded[...] = encode(total)


def put_rows(spot, value, high_ref, low_ref):
    rows = value.shape[0]
    first = pl.multiple_of(spot * rows, 32)
    high, low = halves(value)
    high_ref[pl.ds(first, rows), :] = high
    low_ref[pl.ds(first, rows), :] = low


def root_kernel(meta, *refs):
    for index in range(8):
        spot = 2 * (meta[9] ^ (index // 2)) + (meta[10] ^ (index % 2))
        put_rows(spot, decode_root(refs[index][...]), refs[8], refs[9])


def column_kernel(meta, grad_ref, one, two, three, high_ref, low_ref):
    for step, ref in enumerate((grad_ref, one, two, three)):
        value = decode(ref[...]) if step else ref[...]
        put_rows(2 * (meta[9] ^ step) + meta[10], value, high_ref, low_ref)


def direction_kernel(meta, high_in, low_in, *refs):
    pieces = refs[:4]
    left_ref, root_high, root_low, adam_ref = refs[4:8]
    own_dir, sib_dir, sums, high_ref, low_ref, whole = refs[8:14]
    for step in range(4):
        spot = 2 * (meta[9] ^ step)
        put_rows(spot + 1 - meta[10], decode(pieces[step][...]), high_ref, low_ref)
        rows = left_ref.shape[0]
        held = pl.ds(pl.multiple_of((spot + meta[10]) * rows, 32), rows)
        high_ref[held, :] = high_in[held, :]
        low_ref[held, :] = low_in[held, :]
    half = left_ref.shape[0] // 2
    high, low = high_ref[...], low_ref[...]
    left_high, left_low = halves(left_ref[...])
    prod = row_dot(left_high, high) + (row_dot(left_low, high) + row_dot(left_high, low))
    prod_high, prod_low = halves(prod)
    root_h, root_l = root_high[...], root_low[...]
    direction = row_dot(prod_high, root_h) + (
        row_dot(prod_low, root_h) + row_dot(prod_high, root_l)
    )
    whole[...] = direction
    own_dir[...] = whole[pl.ds(pl.multiple_of(meta[11] * half, 16), half), :]
    sib_dir[...] = whole[pl.ds(pl.multiple_of((1 - meta[11]) * half, 16), half), :]
    lane = lax.broadcasted_iota(jnp.int32, (1, 128), 1)
    sums[...] = jnp.where(lane == 2, jnp.sum(direction * direction), adam_ref[...])


def left_kernel(meta, grad_ref, high_ref, low_ref, own_out, sib_out, whole):
    half = own_out.shape[0]
    high, low = high_ref[...], low_ref[...]
    own_high, own_low = halves(grad_ref[...])
    whole[...] = row_dot_t(own_high, high) + (
        row_dot_t(own_low, high) + row_dot_t(own_high, low)
    )
    own_out[...] = whole[pl.ds(pl.multiple_of(meta[11] * half, 16), half), :]
    sib_out[...] = whole[pl.ds(pl.multiple_of((1 - meta[11]) * half, 16), half), :]


def right_kernel(meta, high_ref, low_ref, own_out, sib_out, whole):
    half, size = own_out.shape
    rows = 2 * half
    first = (2 * meta[9] + meta[10]) * rows
    high, low = high_ref[...], low_ref[...]
    row_ids = lax.broadcasted_iota(jnp.int32, (rows, size), 0) + first
    col_ids = lax.broadcasted_iota(jnp.int32, (rows, size), 1)
    pick = jnp.where(row_ids == col_ids, 1.0, 0.0).astype(BF16)
    col_high = row_dot_t(pick, high).astype(BF16)
    col_low = row_dot_t(pick, low).astype(BF16)
    whole[...] = row_dot(col_high, high) + (row_dot(col_low, high) + row_dot(col_high, low))
    own_out[...] = whole[pl.ds(pl.multiple_of(meta[11] * half, 16), half), :]
    sib_out[...] = whole[pl.ds(pl.multiple_of((1 - meta[11]) * half, 16), half), :]


def moment_kernel(meta, grad, got, first, second, first_out, second_out, adam_out):
    plane, core = meta[8], meta[11]
    rows = got.shape[0]
    first_out[...] = first[...]
    second_out[...] = second[...]
    lane = lax.broadcasted_iota(jnp.int32, (1, 128), 1)
    line = jnp.zeros((1, 128), F32)
    own = grad[pl.ds(pl.multiple_of(core * rows, 16), rows), :]
    for slot, value in ((core, own), (1 - core, got[...])):
        place, _ = used_slot(meta, plane, slot)
        one = 0.9 * first[place] + 0.1 * value
        two = 0.999 * second[place] + 0.001 * value * value
        first_out[place] = one
        second_out[place] = two
        adam = one / (jnp.sqrt(two) + 1e-08)
        line = line + jnp.where(lane == slot, jnp.sum(adam * adam), 0.0)
    adam_out[...] = line


def weight_kernel(meta, sums, own_dir, sib_dir, weights, out):
    plane, core = meta[8], meta[11]
    lane = lax.broadcasted_iota(jnp.int32, (1, 128), 1)
    for slot, value in ((core, own_dir[...]), (1 - core, sib_dir[...])):
        line = jnp.zeros((1, 128), F32)
        for device in range(sums.shape[0]):
            kept = jnp.logical_or(lane == slot, jnp.logical_and(lane == 2, slot == device % 2))
            line = line + jnp.where(kept, sums[device], 0.0)
        dir_sq = jnp.sum(jnp.where(lane == 2, line, 0.0), axis=1, keepdims=True)
        adam_sq = jnp.sum(jnp.where(lane == 2, 0.0, line), axis=1, keepdims=True)
        graft = jnp.sqrt(adam_sq) / (jnp.sqrt(dir_sq) + 1e-06)
        _, block = used_slot(meta, plane, slot)
        out[slot] = (weights[block].astype(F32) - 0.05 * graft * value).astype(BF16)


def place_kernel(meta, near, mirror, out):
    plane = meta[8]
    for slot in (0, 1):
        _, block = used_slot(meta, plane, slot)
        out[block] = near[slot]
        _, block = used_slot(meta, 1 - plane, slot)
        out[block] = mirror[slot]


def stat_kernel(
    meta, own_right, got_right, own_left, got_left, right, left, right_out, left_out
):
    for own, got, stat, out in (
        (own_right, got_right, right, right_out),
        (own_left, got_left, left, left_out),
    ):
        out[...] = stat[...]
        for slot, gram in ((meta[11], own), (1 - meta[11], got)):
            place, _ = used_slot(meta, meta[8], slot)
            out[place] = 0.5 * stat[place] + 0.5 * gram[...]


def two_planes(
    xin,
    dout,
    weights,
    slot_block,
    left_stat,
    right_stat,
    left_root,
    right_root,
    first_moment,
    second_moment,
):
    block_count, tokens, size = xin.shape
    slot_count, rows = left_stat.shape[:2]
    device_count = lax.axis_size(("shard",) + GROUP)
    factor = 1.0 / math.sqrt(tokens * device_count * size)
    section = lax.axis_index("section")
    meta = jnp.concatenate(
        [
            slot_block,
            jnp.stack(
                [lax.axis_index("shard"), lax.axis_index("tensor"), section // 2, section % 2]
            ).astype(jnp.int32),
        ]
    )

    def shape(*dims, dtype=F32):
        return jax.ShapeDtypeStruct(dims, dtype)

    words = jnp.int16
    tile = shape(rows, size)
    tokens_in = shape(2, tokens, size, dtype=BF16)
    piece = shape(coded_rows(2 * rows), size, dtype=words)

    def dmas(count):
        return pltpu.SemaphoreType.DMA((count,))

    xin, dout, left_root, right_root = (
        pltpu.with_memory_space_constraint(value, pltpu.HBM)
        for value in (xin, dout, left_root, right_root)
    )
    far_in, mine_in, roots, own_in = call(
        pick_kernel,
        [tokens_in, tokens_in, shape(2, rows, size), tokens_in],
        [SMEM_SPEC] + [HBM_SPEC] * 4,
        (meta, xin, dout, left_root, right_root),
        [dmas(26)],
    )
    roots = to_core(roots)
    far_in = to_core(far_in)
    mine_in = to_core(mine_in)
    (own_far,) = call(own_far_kernel, [shape(size, size)], [VMEM_SPEC], (own_in,))
    chunk = coded_rows(size // 4)
    coded = list(call(
        far_kernel,
        [shape(chunk, size, dtype=words)] * 4,
        [SMEM_SPEC] + [VMEM_SPEC] * 2,
        (meta, far_in, own_far),
        [pltpu.VMEM((size, size), F32)],
    ))
    coded[0], roots = lax.optimization_barrier((coded[0], roots))
    got_y = [to_y(value) for value in coded]
    left_rows, right_coded = call(
        rows_kernel,
        [shape(2 * rows, size), shape(root_rows(2 * rows), size, dtype=words)],
        [SMEM_SPEC] + [HBM_SPEC] * 2 + [VMEM_SPEC],
        (meta, left_root, right_root, roots),
        [pltpu.VMEM((2 * rows, size), F32), dmas(2)],
    )
    right_coded, later = lax.optimization_barrier((right_coded, meta))
    (own_mine,) = call(
        own_mine_kernel,
        [shape(size, size)],
        [SMEM_SPEC] + [HBM_SPEC] * 2,
        (later, xin, dout),
        [pltpu.VMEM((2, tokens, size), BF16), dmas(8)],
    )
    root_z = {3: to_z(right_coded, 3), 1: to_z(right_coded, 1)}
    mine_in, sent = lax.optimization_barrier((mine_in, right_coded))
    root_x = {0: to_x(sent)}
    sent, root_z[1] = lax.optimization_barrier((root_z[3], root_z[1]))
    root_z[2] = to_z(sent, 1)
    sent, root_x[0] = lax.optimization_barrier((root_z[1], root_x[0]))
    root_x[1] = to_x(sent)

    (mine,) = call(
        mine_kernel,
        [shape(size, size)],
        [VMEM_SPEC] * 2,
        (mine_in, own_mine),
    )
    got_x, keeps, got_z = [], [], []
    for index, bits in enumerate(ORDER):
        arrived = got_y[index]
        if index == 1:
            arrived, got_x[0], root_x[0], root_z[3] = lax.optimization_barrier(
                (arrived, got_x[0], root_x[0], root_z[3])
            )
            root_x[3] = to_x(root_z[3])
        if index == 2:
            arrived, got_x[1], root_x[1], root_z[2] = lax.optimization_barrier(
                (arrived, got_x[1], root_x[1], root_z[2])
            )
        if index == 3:
            arrived, root_x[3] = lax.optimization_barrier((arrived, root_x[3]))
        sent, keep = after_y(meta, arrived, mine, bits)
        got_x.append(to_x(sent))
        keeps.append(keep)
        if index:
            carried = got_z if index == 2 else []
            (sent,) = call(
                x_kernel,
                [piece],
                [VMEM_SPEC] * (2 + len(carried)),
                (keeps[index - 1], got_x[index - 1], *carried),
            )
            got_z.append(to_z(sent, (1, 3, 1)[index - 1]))
    grad, coded = call(
        functools.partial(grad_kernel, factor),
        [shape(2 * rows, size), piece],
        [VMEM_SPEC] * 4,
        (keeps[3], got_x[3], got_z[1], got_z[2]),
    )

    across = {0: to_x(coded)}
    column = {bits: to_z(coded, bits) for bits in (3, 1)}
    coded, sent = lax.optimization_barrier((coded, root_z[2]))
    root_x[2] = to_x(sent)
    column[3], across[0] = lax.optimization_barrier((column[3], across[0]))
    column[2] = to_z(column[3], 1)
    for bits in (1, 3, 2):
        across[bits] = to_x(column[bits])

    root_z[0] = right_coded
    root_pieces = []
    for index in range(4):
        root_pieces += [root_z[index], root_x[index]]
    root_high, root_low = call(
        root_kernel,
        [shape(size, size, dtype=BF16)] * 2,
        [SMEM_SPEC] + [VMEM_SPEC] * 8,
        (meta, *root_pieces),
    )

    core = section % 2
    grad_out = lax.dynamic_slice_in_dim(grad, (1 - core) * rows, rows, 0)
    stack = shape(slot_count, rows, size)
    new_first, new_second, adam = call(
        moment_kernel,
        [stack, stack, shape(1, 128)],
        [SMEM_SPEC] + [VMEM_SPEC] * 4,
        (meta, grad, to_core(grad_out), first_moment, second_moment),
    )
    split = [shape(size, size, dtype=BF16)] * 2
    high, low = call(
        column_kernel,
        split,
        [SMEM_SPEC] + [VMEM_SPEC] * 4,
        (meta, grad, column[1], column[2], column[3]),
    )
    own_dir, sib_dir, sums, high, low = call(
        direction_kernel,
        [tile, tile, shape(1, 128)] + split,
        [SMEM_SPEC] + [VMEM_SPEC] * 10,
        (meta, high, low, *(across[step] for step in range(4)), left_rows, root_high, root_low, adam),
        [pltpu.VMEM((2 * rows, size), F32)],
        4.0,
    )
    sib_dir = to_core(sib_dir)
    sums = jnp.broadcast_to(sums[None], (device_count // 2, 1, 128))
    sums = lax.all_to_all(sums, GROUP, 0, 0)
    (near,) = call(
        weight_kernel,
        [shape(2, rows, size, dtype=BF16)],
        [SMEM_SPEC] + [VMEM_SPEC] * 4,
        (meta, sums, own_dir, sib_dir, weights),
    )
    mirror = to_y(near)
    high, near = lax.optimization_barrier((high, near))
    whole = [pltpu.VMEM((2 * rows, size), F32)]
    own_right, sib_right = call(
        right_kernel,
        [tile, tile],
        [SMEM_SPEC] + [VMEM_SPEC] * 2,
        (meta, high, low),
        whole,
        1.8,
    )
    got_right = to_core(sib_right)
    own_left, sib_left = call(
        left_kernel,
        [tile, tile],
        [SMEM_SPEC] + [VMEM_SPEC] * 3,
        (meta, grad, high, low),
        whole,
        1.4,
    )
    got_left = to_core(sib_left)
    (new_weights,) = call(
        place_kernel,
        [shape(block_count, rows, size, dtype=BF16)],
        [SMEM_SPEC] + [VMEM_SPEC] * 2,
        (meta, near, mirror),
    )
    got_left, new_weights = lax.optimization_barrier((got_left, new_weights))
    new_right, new_left = call(
        stat_kernel,
        [stack, stack],
        [SMEM_SPEC] + [VMEM_SPEC] * 6,
        (meta, own_right, got_right, own_left, got_left, right_stat, left_stat),
    )
    return new_weights, new_left, new_right, new_first, new_second


def solution(mesh):
    placed = (
        P(None, ("shard", "tensor", "section"), None),
        P(None, ("shard", "tensor", "section"), None),
        P(None, ("tensor", "section"), None),
        P(),
        P("shard", ("tensor", "section"), None),
        P("shard", ("tensor", "section"), None),
        P("shard", ("tensor", "section"), None),
        P("shard", ("tensor", "section"), None),
        P("shard", ("tensor", "section"), None),
        P("shard", ("tensor", "section"), None),
    )
    shape = mesh.shape
    pair = (shape["shard"], shape["tensor"], shape["section"]) == (2, 4, 4)
    return jax.shard_map(
        two_planes if pair else any_mesh,
        mesh=mesh,
        in_specs=placed,
        out_specs=(
            P(None, ("tensor", "section"), None),
            P("shard", ("tensor", "section"), None),
            P("shard", ("tensor", "section"), None),
            P("shard", ("tensor", "section"), None),
            P("shard", ("tensor", "section"), None),
        ),
        check_vma=False,
    )
```

```python
import functools
import math

import jax
import jax.numpy as jnp
from jax import lax
from jax.experimental import pallas as pl
from jax.experimental.pallas import tpu as pltpu
from jax.sharding import PartitionSpec as P

F32 = jnp.float32
BF16 = jnp.bfloat16
GROUP = ("tensor", "section")


def spread(value, axis, source):
    kept = jnp.where(lax.axis_index(axis) == source, value, 0).astype(value.dtype)
    return lax.psum(kept, axis)


def absorb_slot(mine_rows, root_rows, portion, col_first):
    highest = lax.Precision.HIGHEST
    row_count = mine_rows.shape[0]
    block_part = jnp.dot(mine_rows, portion.T, precision=highest)
    own_cols = lax.dynamic_slice_in_dim(portion, col_first, row_count, 1)
    right_gram = jnp.dot(own_cols.T, portion, precision=highest)
    left_prod = jnp.dot(root_rows, portion, precision=highest)
    return (block_part, right_gram, left_prod)


def apply_slot(prod_rows, portion):
    return jnp.dot(prod_rows, portion, precision=lax.Precision.HIGHEST)


def any_mesh(
    xin,
    dout,
    weights,
    slot_block,
    left_stat,
    right_stat,
    left_root,
    right_root,
    first_moment,
    second_moment,
):
    block_count, tok_count, block_size = xin.shape
    slot_count, row_count = (left_stat.shape[0], left_stat.shape[1])
    group_count = lax.axis_size(GROUP)
    shard_count = lax.axis_size("shard")
    factor = 1.0 / math.sqrt(tok_count * shard_count * group_count * block_size)
    pieces_out = []
    for grad_member in range(block_count):
        cols = xin[grad_member]
        pieces_out.append(
            jnp.einsum("tr,tc->rc", cols, dout[grad_member], preferred_element_type=jnp.float32)
        )
    partial_rows = lax.psum_scatter(
        jnp.concatenate(pieces_out, axis=1) * factor,
        GROUP,
        scatter_dimension=0,
        tiled=True,
    )
    grad_rows = lax.psum(partial_rows, "shard")
    shard_idx = lax.axis_index("shard")
    group_idx = lax.axis_index(GROUP)
    my_slots = lax.dynamic_slice_in_dim(slot_block, shard_idx * slot_count, slot_count)
    valid = my_slots >= 0
    picks = jnp.maximum(my_slots, 0)
    grad_three = grad_rows.reshape(row_count, block_count, block_size)
    mine = jnp.moveaxis(jnp.take(grad_three, picks, axis=1), 1, 0)
    col_first = group_idx * row_count
    zeros_rows = jnp.zeros((slot_count, row_count, block_size), jnp.float32)
    totals = (zeros_rows, zeros_rows, zeros_rows)
    portion = lax.all_gather(mine, GROUP, axis=1, tiled=True)
    lefts = []
    rights = []
    prods = []
    for slot_pos in range(slot_count):
        current = (totals[0][slot_pos], totals[1][slot_pos], totals[2][slot_pos])
        result = lax.cond(
            valid[slot_pos],
            lambda values: absorb_slot(
                mine[slot_pos], left_root[slot_pos], portion[slot_pos], col_first
            ),
            lambda values: values,
            current,
        )
        lefts.append(result[0])
        rights.append(result[1])
        prods.append(result[2])
    left_gram = jnp.stack(lefts)
    right_gram = jnp.stack(rights)
    left_prod = jnp.stack(prods)
    apply_portion = lax.all_gather(right_root, GROUP, axis=1, tiled=True)
    outputs = []
    for apply_slot_pos in range(slot_count):
        outputs.append(
            lax.cond(
                valid[apply_slot_pos],
                lambda values: apply_slot(left_prod[apply_slot_pos], apply_portion[apply_slot_pos]),
                lambda values: values,
                zeros_rows[apply_slot_pos],
            )
        )
    direction = jnp.stack(outputs)
    moment_one = 0.9 * first_moment + 0.1 * mine
    moment_two = 0.999 * second_moment + 0.001 * mine * mine
    adam = moment_one / (jnp.sqrt(moment_two) + 1e-08)
    adam_sq, dir_sq = lax.psum(
        (jnp.sum(adam * adam, axis=(1, 2)), jnp.sum(direction * direction, axis=(1, 2))),
        GROUP,
    )
    graft = jnp.sqrt(adam_sq) / (jnp.sqrt(dir_sq) + 1e-06)
    mask = valid[:, None, None]
    new_left = jnp.where(mask, 0.5 * left_stat + 0.5 * left_gram, left_stat)
    new_right = jnp.where(mask, 0.5 * right_stat + 0.5 * right_gram, right_stat)
    new_first = jnp.where(mask, moment_one, first_moment)
    new_second = jnp.where(mask, moment_two, second_moment)
    my_weights = jnp.take(weights, picks, axis=0)
    new_rows = (my_weights.astype(jnp.float32) - 0.05 * graft[:, None, None] * direction).astype(
        jnp.bfloat16
    )
    slot_ids = jnp.arange(slot_block.shape[0], dtype=jnp.int32)
    holders = [
        jnp.sum(slot_ids * (slot_block == member).astype(jnp.int32))
        for member in range(block_count)
    ]
    published = []
    for member in range(block_count):
        owner = holders[member] // slot_count
        within = holders[member] % slot_count
        chosen = lax.dynamic_index_in_dim(new_rows, within, 0, keepdims=False)
        published.append(spread(chosen, "shard", owner))
    new_weights = jnp.stack(published)
    return (new_weights, new_left, new_right, new_first, new_second)


def to_core(value):
    return lax.ppermute(value, "section", [(i, i ^ 1) for i in range(4)])


def to_x(value):
    return lax.ppermute(value, "section", [(i, i ^ 2) for i in range(4)])


def to_y(value):
    return lax.ppermute(value, "shard", [(0, 1), (1, 0)])


def to_z(value, bits):
    return lax.ppermute(value, "tensor", [(i, i ^ bits) for i in range(4)])


def row_dot(rows, full):
    return lax.dot_general(rows, full, (((1,), (0,)), ((), ())), preferred_element_type=F32)


def row_dot_t(rows, full):
    return lax.dot_general(rows, full, (((1,), (1,)), ((), ())), preferred_element_type=F32)


def token_dot(left, right):
    return lax.dot_general(left, right, (((0,), (0,)), ((), ())), preferred_element_type=F32)


def halves(value):
    high = value.astype(BF16)
    return high, (value - high.astype(F32)).astype(BF16)


def coded_rows(rows):
    return rows + rows // 6


def scaling(value):
    top = jnp.maximum(jnp.max(jnp.abs(value), axis=0, keepdims=True), 1e-30)
    exponent = jnp.ceil(jnp.log2(top))
    return exponent, value * (jnp.exp2(-exponent) * 32760.0)


def encode(value):
    exponent, scaled = scaling(value)
    coarse = jnp.round(scaled)
    fine = jnp.clip(jnp.floor((scaled - coarse) * 4.0), -2.0, 1.0) + 2.0
    tiles = value.shape[0] // 8
    parts = [coarse]
    for first in range(0, tiles + 1, 8):
        full = first + 8 <= tiles
        word = -32768.0 if full else jnp.broadcast_to(exponent * 256.0, (8, value.shape[1]))
        for index in range(first, min(first + 8, tiles)):
            word = word + fine[8 * index : 8 * index + 8] * float(4 ** (index - first))
        parts.append(word)
    return jnp.concatenate(parts, axis=0).astype(jnp.int32).astype(jnp.int16)


def decode(words):
    rows = words.shape[0] // 7 * 6
    tiles = rows // 8
    wide = words.astype(jnp.int32)
    coarse = wide[:rows].astype(F32)
    low = []
    for first in range(0, tiles + 1, 8):
        word = wide[rows + first : rows + first + 8]
        if first + 8 <= tiles:
            word = word + 32768
        for index in range(first, min(first + 8, tiles)):
            low.append((jnp.right_shift(word, 2 * (index - first)) & 3).astype(F32))
    exponent = jnp.right_shift(word, 8).astype(F32)[:1]
    fine = jnp.concatenate(low, axis=0)
    return (coarse + (fine - 1.5) * 0.25) * (jnp.exp2(exponent) * (1.0 / 32760.0))


def root_rows(rows):
    return rows + rows // 3


def encode_root(value):
    rows = value.shape[0]
    part = rows // 4
    exponent, scaled = scaling(value)
    coarse = jnp.round(scaled)
    fine = jnp.clip(jnp.floor((scaled - coarse) * 16.0), -8.0, 7.0) + 8.0
    words = fine[:part] - 32768.0
    for index in (1, 2, 3):
        words = words + fine[index * part : (index + 1) * part] * float(16**index)
    tail = jnp.broadcast_to(exponent, (rows // 3 - part, value.shape[1]))
    both = jnp.concatenate([coarse, words, tail], axis=0)
    return both.astype(jnp.int32).astype(jnp.int16)


def decode_root(words):
    rows = words.shape[0] // 4 * 3
    part = rows // 4
    wide = words.astype(jnp.int32)
    coarse = wide[:rows].astype(F32)
    fine = wide[rows : rows + part] + 32768
    exponent = wide[rows + part : rows + part + 8].astype(F32)[:1]
    parts = [(jnp.right_shift(fine, 4 * index) & 15).astype(F32) for index in range(4)]
    low = jnp.concatenate(parts, axis=0)
    return (coarse + (low - 7.5) * (1.0 / 16.0)) * (jnp.exp2(exponent) * (1.0 / 32760.0))


def used_slot(meta, plane, nth):
    seen = jnp.int32(0)
    place = jnp.int32(0)
    block = jnp.int32(0)
    for spot in range(4):
        entry = meta[4 * plane + spot]
        used = entry >= 0
        hit = jnp.logical_and(used, seen == nth)
        place = jnp.where(hit, spot, place)
        block = jnp.where(hit, entry, block)
        seen = seen + jnp.where(used, 1, 0)
    return place, block


ORDER = (2, 3, 1, 0)


SMEM_SPEC = pl.BlockSpec(memory_space=pltpu.SMEM)
VMEM_SPEC = pl.BlockSpec(memory_space=pltpu.VMEM)
HBM_SPEC = pl.BlockSpec(memory_space=pltpu.HBM)


def work(micros):
    return pl.CostEstimate(
        flops=int(micros * 15 * 10**8), transcendentals=0, bytes_accessed=int(micros * 36 * 10**6)
    )


def call(body, outs, ins, args, scratch=(), micros=1.0):
    return pl.pallas_call(
        body,
        out_shape=outs,
        in_specs=ins,
        out_specs=[VMEM_SPEC] * len(outs),
        cost_estimate=work(micros),
        scratch_shapes=list(scratch),
        compiler_params=pltpu.CompilerParams(vmem_limit_bytes=24 << 20),
    )(*args)


def start_copies(pairs, sems):
    copies = [
        pltpu.make_async_copy(source, target, sems.at[index])
        for index, (source, target) in enumerate(pairs)
    ]
    for copy in copies:
        copy.start()
    return copies


def in_parts(source, block, target, parts=4):
    span = target.shape[0] // parts
    rows = [pl.ds(part * span, span) for part in range(parts)]
    return [(source.at[block, part], target.at[part]) for part in rows]


def pick_kernel(meta, xin, dout, left, right, far, mine, roots, own, sems):
    _, block = used_slot(meta, 1 - meta[8], 1 - meta[11])
    pairs = in_parts(xin, block, far.at[0]) + in_parts(dout, block, far.at[1])
    _, block = used_slot(meta, 1 - meta[8], meta[11])
    pairs += in_parts(xin, block, own.at[0]) + in_parts(dout, block, own.at[1])
    place, block = used_slot(meta, meta[8], 1 - meta[11])
    pairs += [(left.at[place], roots.at[0]), (right.at[place], roots.at[1])]
    pairs += in_parts(xin, block, mine.at[0]) + in_parts(dout, block, mine.at[1])
    for copy in start_copies(pairs, sems):
        copy.wait()


def own_far_kernel(taken, out):
    out[...] = token_dot(taken[0], taken[1])


def own_mine_kernel(meta, xin, dout, out, taken, sems):
    _, block = used_slot(meta, meta[8], meta[11])
    pairs = in_parts(xin, block, taken.at[0]) + in_parts(dout, block, taken.at[1])
    copies = start_copies(pairs, sems)
    half = taken.shape[1] // 2
    for part in (0, 1):
        for index in (0, 1):
            copies[2 * part + index].wait()
            copies[4 + 2 * part + index].wait()
        rows = pl.ds(part * half, half)
        value = token_dot(taken[0, rows, :], taken[1, rows, :])
        out[...] = value if part == 0 else out[...] + value


def far_kernel(meta, got, own_ref, *refs):
    outs, total = refs[:4], refs[4]
    total[...] = own_ref[...] + token_dot(got[0], got[1])
    span = total.shape[0] // 4
    for out, bits in zip(outs, ORDER):
        first = pl.multiple_of((meta[9] ^ bits) * span, 64)
        out[...] = encode(total[pl.ds(first, span), :])


def mine_kernel(got, own_ref, out_ref):
    out_ref[...] = own_ref[...] + token_dot(got[0], got[1])


def rows_kernel(meta, left, right, got, left_out, right_out, whole, sems):
    core = meta[11]
    rows = got.shape[1]
    place, _ = used_slot(meta, meta[8], core)
    own = pl.ds(pl.multiple_of(core * rows, 16), rows)
    sib = pl.ds(pl.multiple_of((1 - core) * rows, 16), rows)
    pairs = [(left.at[place], left_out.at[own, :]), (right.at[place], whole.at[own, :])]
    copies = start_copies(pairs, sems)
    left_out[sib, :] = got[0]
    whole[sib, :] = got[1]
    for copy in copies:
        copy.wait()
    right_out[...] = encode_root(whole[...])


def y_kernel(meta, got, mine, coded, keep, both):
    rows = keep.shape[0]
    both[...] = decode(got[...]) + mine[...]
    side = meta[10]
    keep[...] = both[pl.ds(pl.multiple_of(side * rows, 32), rows), :]
    coded[...] = encode(both[pl.ds(pl.multiple_of((1 - side) * rows, 32), rows), :])


def after_y(meta, got, mine, bits):
    size = mine.shape[1]
    rows = size // 8
    return pl.pallas_call(
        y_kernel,
        out_shape=[
            jax.ShapeDtypeStruct((coded_rows(rows), size), jnp.int16),
            jax.ShapeDtypeStruct((rows, size), F32),
        ],
        grid_spec=pltpu.PrefetchScalarGridSpec(
            num_scalar_prefetch=1,
            grid=(1,),
            in_specs=[
                pl.BlockSpec(got.shape, lambda step, meta_ref: (0, 0)),
                pl.BlockSpec((2 * rows, size), lambda step, meta_ref: (meta_ref[9] ^ bits, 0)),
            ],
            out_specs=[
                pl.BlockSpec((coded_rows(rows), size), lambda step, meta_ref: (0, 0)),
                pl.BlockSpec((rows, size), lambda step, meta_ref: (0, 0)),
            ],
            scratch_shapes=[pltpu.VMEM((2 * rows, size), F32)],
        ),
        compiler_params=pltpu.CompilerParams(vmem_limit_bytes=24 << 20),
        cost_estimate=work(1.1),
    )(meta, got, mine)


def x_kernel(keep, *refs):
    total = keep[...]
    for part in refs[:-1]:
        total = total + decode(part[...])
    refs[-1][...] = encode(total)


def grad_kernel(factor, keep, got, far, near, grad, coded):
    total = keep[...]
    for part in (got, far, near):
        total = total + decode(part[...])
    total = total * factor
    grad[...] = total
    coded[...] = encode(total)


def put_rows(spot, value, high_ref, low_ref):
    rows = value.shape[0]
    first = pl.multiple_of(spot * rows, 32)
    high, low = halves(value)
    high_ref[pl.ds(first, rows), :] = high
    low_ref[pl.ds(first, rows), :] = low


def root_kernel(meta, *refs):
    for index in range(8):
        spot = 2 * (meta[9] ^ (index // 2)) + (meta[10] ^ (index % 2))
        put_rows(spot, decode_root(refs[index][...]), refs[8], refs[9])


def column_kernel(meta, grad_ref, one, two, three, high_ref, low_ref):
    for step, ref in enumerate((grad_ref, one, two, three)):
        value = decode(ref[...]) if step else ref[...]
        put_rows(2 * (meta[9] ^ step) + meta[10], value, high_ref, low_ref)


def direction_kernel(meta, high_in, low_in, *refs):
    pieces = refs[:4]
    left_ref, root_high, root_low, adam_ref = refs[4:8]
    own_dir, sib_dir, sums, high_ref, low_ref, whole = refs[8:14]
    for step in range(4):
        spot = 2 * (meta[9] ^ step)
        put_rows(spot + 1 - meta[10], decode(pieces[step][...]), high_ref, low_ref)
        rows = left_ref.shape[0]
        held = pl.ds(pl.multiple_of((spot + meta[10]) * rows, 32), rows)
        high_ref[held, :] = high_in[held, :]
        low_ref[held, :] = low_in[held, :]
    half = left_ref.shape[0] // 2
    high, low = high_ref[...], low_ref[...]
    left_high, left_low = halves(left_ref[...])
    prod = row_dot(left_high, high) + (row_dot(left_low, high) + row_dot(left_high, low))
    prod_high, prod_low = halves(prod)
    root_h, root_l = root_high[...], root_low[...]
    direction = row_dot(prod_high, root_h) + (
        row_dot(prod_low, root_h) + row_dot(prod_high, root_l)
    )
    whole[...] = direction
    own_dir[...] = whole[pl.ds(pl.multiple_of(meta[11] * half, 16), half), :]
    sib_dir[...] = whole[pl.ds(pl.multiple_of((1 - meta[11]) * half, 16), half), :]
    lane = lax.broadcasted_iota(jnp.int32, (1, 128), 1)
    sums[...] = jnp.where(lane == 2, jnp.sum(direction * direction), adam_ref[...])


def left_kernel(meta, grad_ref, high_ref, low_ref, own_out, sib_out, whole):
    half = own_out.shape[0]
    high, low = high_ref[...], low_ref[...]
    own_high, own_low = halves(grad_ref[...])
    whole[...] = row_dot_t(own_high, high) + (
        row_dot_t(own_low, high) + row_dot_t(own_high, low)
    )
    own_out[...] = whole[pl.ds(pl.multiple_of(meta[11] * half, 16), half), :]
    sib_out[...] = whole[pl.ds(pl.multiple_of((1 - meta[11]) * half, 16), half), :]


def right_kernel(meta, high_ref, low_ref, own_out, sib_out, whole):
    half, size = own_out.shape
    rows = 2 * half
    first = (2 * meta[9] + meta[10]) * rows
    high, low = high_ref[...], low_ref[...]
    row_ids = lax.broadcasted_iota(jnp.int32, (rows, size), 0) + first
    col_ids = lax.broadcasted_iota(jnp.int32, (rows, size), 1)
    pick = jnp.where(row_ids == col_ids, 1.0, 0.0).astype(BF16)
    col_high = row_dot_t(pick, high).astype(BF16)
    col_low = row_dot_t(pick, low).astype(BF16)
    whole[...] = row_dot(col_high, high) + (row_dot(col_low, high) + row_dot(col_high, low))
    own_out[...] = whole[pl.ds(pl.multiple_of(meta[11] * half, 16), half), :]
    sib_out[...] = whole[pl.ds(pl.multiple_of((1 - meta[11]) * half, 16), half), :]


def moment_kernel(meta, grad, got, first, second, first_out, second_out, adam_out):
    plane, core = meta[8], meta[11]
    rows = got.shape[0]
    first_out[...] = first[...]
    second_out[...] = second[...]
    lane = lax.broadcasted_iota(jnp.int32, (1, 128), 1)
    line = jnp.zeros((1, 128), F32)
    own = grad[pl.ds(pl.multiple_of(core * rows, 16), rows), :]
    for slot, value in ((core, own), (1 - core, got[...])):
        place, _ = used_slot(meta, plane, slot)
        one = 0.9 * first[place] + 0.1 * value
        two = 0.999 * second[place] + 0.001 * value * value
        first_out[place] = one
        second_out[place] = two
        adam = one / (jnp.sqrt(two) + 1e-08)
        line = line + jnp.where(lane == slot, jnp.sum(adam * adam), 0.0)
    adam_out[...] = line


def weight_kernel(meta, sums, own_dir, sib_dir, weights, out):
    plane, core = meta[8], meta[11]
    lane = lax.broadcasted_iota(jnp.int32, (1, 128), 1)
    for slot, value in ((core, own_dir[...]), (1 - core, sib_dir[...])):
        line = jnp.zeros((1, 128), F32)
        for device in range(sums.shape[0]):
            kept = jnp.logical_or(lane == slot, jnp.logical_and(lane == 2, slot == device % 2))
            line = line + jnp.where(kept, sums[device], 0.0)
        dir_sq = jnp.sum(jnp.where(lane == 2, line, 0.0), axis=1, keepdims=True)
        adam_sq = jnp.sum(jnp.where(lane == 2, 0.0, line), axis=1, keepdims=True)
        graft = jnp.sqrt(adam_sq) / (jnp.sqrt(dir_sq) + 1e-06)
        _, block = used_slot(meta, plane, slot)
        out[slot] = (weights[block].astype(F32) - 0.05 * graft * value).astype(BF16)


def place_kernel(meta, near, mirror, out):
    plane = meta[8]
    for slot in (0, 1):
        _, block = used_slot(meta, plane, slot)
        out[block] = near[slot]
        _, block = used_slot(meta, 1 - plane, slot)
        out[block] = mirror[slot]


def stat_kernel(
    meta, own_right, got_right, own_left, got_left, right, left, right_out, left_out
):
    for own, got, stat, out in (
        (own_right, got_right, right, right_out),
        (own_left, got_left, left, left_out),
    ):
        out[...] = stat[...]
        for slot, gram in ((meta[11], own), (1 - meta[11], got)):
            place, _ = used_slot(meta, meta[8], slot)
            out[place] = 0.5 * stat[place] + 0.5 * gram[...]


def two_planes(
    xin,
    dout,
    weights,
    slot_block,
    left_stat,
    right_stat,
    left_root,
    right_root,
    first_moment,
    second_moment,
):
    block_count, tokens, size = xin.shape
    slot_count, rows = left_stat.shape[:2]
    device_count = lax.axis_size(("shard",) + GROUP)
    factor = 1.0 / math.sqrt(tokens * device_count * size)
    section = lax.axis_index("section")
    meta = jnp.concatenate(
        [
            slot_block,
            jnp.stack(
                [lax.axis_index("shard"), lax.axis_index("tensor"), section // 2, section % 2]
            ).astype(jnp.int32),
        ]
    )

    def shape(*dims, dtype=F32):
        return jax.ShapeDtypeStruct(dims, dtype)

    words = jnp.int16
    tile = shape(rows, size)
    tokens_in = shape(2, tokens, size, dtype=BF16)
    piece = shape(coded_rows(2 * rows), size, dtype=words)

    def dmas(count):
        return pltpu.SemaphoreType.DMA((count,))

    xin, dout, left_root, right_root = (
        pltpu.with_memory_space_constraint(value, pltpu.HBM)
        for value in (xin, dout, left_root, right_root)
    )
    far_in, mine_in, roots, own_in = call(
        pick_kernel,
        [tokens_in, tokens_in, shape(2, rows, size), tokens_in],
        [SMEM_SPEC] + [HBM_SPEC] * 4,
        (meta, xin, dout, left_root, right_root),
        [dmas(26)],
    )
    roots = to_core(roots)
    far_in = to_core(far_in)
    mine_in = to_core(mine_in)
    (own_far,) = call(own_far_kernel, [shape(size, size)], [VMEM_SPEC], (own_in,))
    chunk = coded_rows(size // 4)
    coded = list(call(
        far_kernel,
        [shape(chunk, size, dtype=words)] * 4,
        [SMEM_SPEC] + [VMEM_SPEC] * 2,
        (meta, far_in, own_far),
        [pltpu.VMEM((size, size), F32)],
    ))
    coded[0], roots = lax.optimization_barrier((coded[0], roots))
    got_y = [to_y(value) for value in coded]
    left_rows, right_coded = call(
        rows_kernel,
        [shape(2 * rows, size), shape(root_rows(2 * rows), size, dtype=words)],
        [SMEM_SPEC] + [HBM_SPEC] * 2 + [VMEM_SPEC],
        (meta, left_root, right_root, roots),
        [pltpu.VMEM((2 * rows, size), F32), dmas(2)],
    )
    right_coded, later = lax.optimization_barrier((right_coded, meta))
    (own_mine,) = call(
        own_mine_kernel,
        [shape(size, size)],
        [SMEM_SPEC] + [HBM_SPEC] * 2,
        (later, xin, dout),
        [pltpu.VMEM((2, tokens, size), BF16), dmas(8)],
    )
    root_z = {3: to_z(right_coded, 3), 1: to_z(right_coded, 1)}
    mine_in, sent = lax.optimization_barrier((mine_in, right_coded))
    root_x = {0: to_x(sent)}
    sent, root_z[1] = lax.optimization_barrier((root_z[3], root_z[1]))
    root_z[2] = to_z(sent, 1)
    sent, root_x[0] = lax.optimization_barrier((root_z[1], root_x[0]))
    root_x[1] = to_x(sent)

    (mine,) = call(
        mine_kernel,
        [shape(size, size)],
        [VMEM_SPEC] * 2,
        (mine_in, own_mine),
    )
    got_x, keeps, got_z = [], [], []
    for index, bits in enumerate(ORDER):
        arrived = got_y[index]
        if index == 1:
            arrived, got_x[0], root_x[0], root_z[3] = lax.optimization_barrier(
                (arrived, got_x[0], root_x[0], root_z[3])
            )
            root_x[3] = to_x(root_z[3])
        if index == 2:
            arrived, got_x[1], root_x[1], root_z[2] = lax.optimization_barrier(
                (arrived, got_x[1], root_x[1], root_z[2])
            )
        if index == 3:
            arrived, root_x[3] = lax.optimization_barrier((arrived, root_x[3]))
        sent, keep = after_y(meta, arrived, mine, bits)
        got_x.append(to_x(sent))
        keeps.append(keep)
        if index:
            carried = got_z if index == 2 else []
            (sent,) = call(
                x_kernel,
                [piece],
                [VMEM_SPEC] * (2 + len(carried)),
                (keeps[index - 1], got_x[index - 1], *carried),
            )
            got_z.append(to_z(sent, (1, 3, 1)[index - 1]))
    grad, coded = call(
        functools.partial(grad_kernel, factor),
        [shape(2 * rows, size), piece],
        [VMEM_SPEC] * 4,
        (keeps[3], got_x[3], got_z[1], got_z[2]),
    )

    across = {0: to_x(coded)}
    column = {bits: to_z(coded, bits) for bits in (3, 1)}
    coded, sent = lax.optimization_barrier((coded, root_z[2]))
    root_x[2] = to_x(sent)
    column[3], across[0] = lax.optimization_barrier((column[3], across[0]))
    column[2] = to_z(column[3], 1)
    for bits in (1, 3, 2):
        across[bits] = to_x(column[bits])

    root_z[0] = right_coded
    root_pieces = []
    for index in range(4):
        root_pieces += [root_z[index], root_x[index]]
    root_high, root_low = call(
        root_kernel,
        [shape(size, size, dtype=BF16)] * 2,
        [SMEM_SPEC] + [VMEM_SPEC] * 8,
        (meta, *root_pieces),
    )

    core = section % 2
    grad_out = lax.dynamic_slice_in_dim(grad, (1 - core) * rows, rows, 0)
    stack = shape(slot_count, rows, size)
    new_first, new_second, adam = call(
        moment_kernel,
        [stack, stack, shape(1, 128)],
        [SMEM_SPEC] + [VMEM_SPEC] * 4,
        (meta, grad, to_core(grad_out), first_moment, second_moment),
    )
    split = [shape(size, size, dtype=BF16)] * 2
    high, low = call(
        column_kernel,
        split,
        [SMEM_SPEC] + [VMEM_SPEC] * 4,
        (meta, grad, column[1], column[2], column[3]),
    )
    own_dir, sib_dir, sums, high, low = call(
        direction_kernel,
        [tile, tile, shape(1, 128)] + split,
        [SMEM_SPEC] + [VMEM_SPEC] * 10,
        (meta, high, low, *(across[step] for step in range(4)), left_rows, root_high, root_low, adam),
        [pltpu.VMEM((2 * rows, size), F32)],
        4.0,
    )
    sib_dir = to_core(sib_dir)
    sums = jnp.broadcast_to(sums[None], (device_count // 2, 1, 128))
    sums = lax.all_to_all(sums, GROUP, 0, 0)
    (near,) = call(
        weight_kernel,
        [shape(2, rows, size, dtype=BF16)],
        [SMEM_SPEC] + [VMEM_SPEC] * 4,
        (meta, sums, own_dir, sib_dir, weights),
    )
    mirror = to_y(near)
    high, near = lax.optimization_barrier((high, near))
    whole = [pltpu.VMEM((2 * rows, size), F32)]
    own_right, sib_right = call(
        right_kernel,
        [tile, tile],
        [SMEM_SPEC] + [VMEM_SPEC] * 2,
        (meta, high, low),
        whole,
        1.8,
    )
    got_right = to_core(sib_right)
    own_left, sib_left = call(
        left_kernel,
        [tile, tile],
        [SMEM_SPEC] + [VMEM_SPEC] * 3,
        (meta, grad, high, low),
        whole,
        1.4,
    )
    got_left = to_core(sib_left)
    (new_weights,) = call(
        place_kernel,
        [shape(block_count, rows, size, dtype=BF16)],
        [SMEM_SPEC] + [VMEM_SPEC] * 2,
        (meta, near, mirror),
    )
    got_left, new_weights = lax.optimization_barrier((got_left, new_weights))
    new_right, new_left = call(
        stat_kernel,
        [stack, stack],
        [SMEM_SPEC] + [VMEM_SPEC] * 6,
        (meta, own_right, got_right, own_left, got_left, right_stat, left_stat),
    )
    return new_weights, new_left, new_right, new_first, new_second


def solution(mesh):
    placed = (
        P(None, ("shard", "tensor", "section"), None),
        P(None, ("shard", "tensor", "section"), None),
        P(None, ("tensor", "section"), None),
        P(),
        P("shard", ("tensor", "section"), None),
        P("shard", ("tensor", "section"), None),
        P("shard", ("tensor", "section"), None),
        P("shard", ("tensor", "section"), None),
        P("shard", ("tensor", "section"), None),
        P("shard", ("tensor", "section"), None),
    )
    shape = mesh.shape
    pair = (shape["shard"], shape["tensor"], shape["section"]) == (2, 4, 4)
    return jax.shard_map(
        two_planes if pair else any_mesh,
        mesh=mesh,
        in_specs=placed,
        out_specs=(
            P(None, ("tensor", "section"), None),
            P("shard", ("tensor", "section"), None),
            P("shard", ("tensor", "section"), None),
            P("shard", ("tensor", "section"), None),
            P("shard", ("tensor", "section"), None),
        ),
        check_vma=False,
    )
```
